32 devices in a mesh: dp: 16 (over z, y, core), head: 2 (over x).
Axes of the slice: x: 2, y: 2, z: 4, core: 2. Of those that a mesh axis runs over, the one named last changes fastest.
Arguments:
- tokens: bfloat16 [16, 1024, 1536], P('dp', 'head'), may hold values from -6 to 6
- context: bfloat16 [16, 128, 768], P('dp'), may hold values from -6 to 6
- lengths: int32 [16], P('dp'), may hold values from 4 to 128, as said below
- norm_gains: float32 [3, 1536], replicated, may hold values from 0.5 to 1.5
- w_qkv: bfloat16 [1536, 4608], P('dp'), may hold values from -0.15625 to 0.15625
- w_out: bfloat16 [1536, 1536], P('dp'), may hold values from -0.875 to 0.875
- w_q2: bfloat16 [1536, 1536], P('dp'), may hold values from -0.15625 to 0.15625
- w_kv2: bfloat16 [768, 3072], P('dp'), may hold values from -0.21875 to 0.21875
- w_out2: bfloat16 [1536, 1536], P('dp'), may hold values from -0.4375 to 0.4375
- w_in: bfloat16 [1536, 12288], P('dp'), may hold values from -0.15625 to 0.15625
- w_down: bfloat16 [6144, 1536], P('dp'), may hold values from -0.078125 to 0.078125
- cotangent: bfloat16 [16, 1024, 1536], P('dp', 'head'), may hold values from -6 to 6
Outputs:
- block_out: bfloat16 [16, 1024, 1536], P('dp', 'head')
- tokens_grad: float32 [16, 1024, 1536], P('dp', 'head')
- gains_grad: float32 [3, 1536], replicated
- qkv_grad: float32 [1536, 4608], P('dp')
- out_grad: float32 [1536, 1536], P('dp')
- q2_grad: float32 [1536, 1536], P('dp')
- kv2_grad: float32 [768, 3072], P('dp')
- out2_grad: float32 [1536, 1536], P('dp')
- in_grad: float32 [1536, 12288], P('dp')
- down_grad: float32 [6144, 1536], P('dp')
The draws below stay inside these ranges and needn't reach their ends.
Inputs may be any that keep to these rules, and one draw needn't show every extreme that they name: lengths[s] is the number of real prompt tokens of sequence s; context rows at or past it are padding; some sequence has 128.
All inputs are finite; a program needn't handle non-finite values.
Results may differ from the reference program's by a relative error of at most 0.023.
Values may be sent and summed in bfloat16 or wider, within the bound.
A program may use at most 448 MiB of HBM per device.

```python
import jax
import jax.numpy as jnp
from jax import lax

D = 1536
HEADS = 24
HEAD_DIM = 64
FF = 6144
CTX = 768
PLEN = 128
LEN = 1024
SEQS = 16


def draw_lengths(key, part):
    uniform_base = jax.random.randint(jax.random.fold_in(key, 11), (SEQS,), 0, PLEN - 3)
    spread_out = 4 + uniform_base * uniform_base * uniform_base // ((PLEN - 4) * (PLEN - 4))
    longest_at = jax.random.randint(jax.random.fold_in(key, 12), (), 0, SEQS)
    return jnp.where(jnp.arange(SEQS) == longest_at, PLEN, spread_out).astype(jnp.int32)


def with_spikes(drawn, stream_key, source, target, shards_of, factor):
    owner, partner = [(jnp.arange(drawn.shape[axis_at]) // (drawn.shape[axis_at] // shards_of)).reshape([-1 if axis == axis_at else 1 for axis in range(drawn.ndim)]) for axis_at in (source, target)]
    chosen = jax.random.permutation(stream_key, shards_of)[partner]
    strong = (owner == chosen) | (owner == (partner + shards_of // 2) % shards_of)
    return jnp.where(strong, factor * drawn, drawn)


def level_of(own_key, shape, shards, low, high):
    def one(dim, shards_of):
        heights = jax.random.uniform(jax.random.fold_in(jax.random.fold_in(own_key, 6), dim), (shards_of,), jnp.float32, low / len(shards), high / len(shards))
        return jnp.repeat(jnp.exp(heights), shape[dim] // shards_of).reshape((-1,) + (1,) * (len(shape) - dim - 1))

    level = one(*shards[0])
    for cut in shards[1:]:
        level = level * one(*cut)
    return level


def gaussian(stream_key, shape, width, reach, pieces=(), kind=jnp.bfloat16):
    loudness = level_of(stream_key, shape, pieces, -0.22, 0.18) if pieces else 1.0
    entries = jax.random.normal(stream_key, shape, jnp.float32) * width * loudness
    return jnp.minimum(jnp.maximum(entries, -reach), reach).astype(kind)


def noise_with(stream_key, extent, spread, reach, shards, heavy, held_as=jnp.bfloat16):
    array = spread * jax.random.normal(stream_key, extent, jnp.float32)
    if shards:
        array = array * level_of(stream_key, extent, shards, -0.22, 0.18)
    return jnp.clip(with_spikes(array, jax.random.fold_in(stream_key, 3), *heavy), -reach, reach).astype(held_as)


def setup_inputs(seed: int = 0) -> dict:
    streams_of = jax.random.split(jax.random.key(seed), 13)
    tokens = noise_with(streams_of[0], (SEQS, LEN, D), 1.0, 6.0, ((0, 16), (1, 2)), (0, 2, 16, 2.0))
    context = gaussian(streams_of[1], (SEQS, PLEN, CTX), 1.0, 6.0, ((0, 16),))
    lengths = draw_lengths(jax.random.fold_in(streams_of[12], 71), 0)
    norm_gains = jnp.clip(1.0 + 0.1 * jax.random.normal(streams_of[3], (3, D), jnp.float32), 0.5, 1.5)
    w_qkv = gaussian(streams_of[4], (D, 3 * D), D ** -0.5, 0.15625, ((0, 16),))
    w_out = gaussian(streams_of[5], (D, D), (D // 32) ** -0.5, 0.875, ((0, 16),))
    w_q2 = gaussian(streams_of[6], (D, D), D ** -0.5, 0.15625, ((0, 16),))
    w_kv2 = gaussian(streams_of[7], (CTX, 2 * D), CTX ** -0.5, 0.21875, ((0, 16),))
    w_out2 = gaussian(streams_of[8], (D, D), (D // 8) ** -0.5, 0.4375, ((0, 16),))
    w_in = gaussian(streams_of[9], (D, 2 * FF), D ** -0.5, 0.15625, ((0, 16),))
    w_down = gaussian(streams_of[10], (FF, D), FF ** -0.5, 0.078125, ((0, 16),))
    cotangent = gaussian(streams_of[11], (SEQS, LEN, D), 1.0, 6.0, ((0, 16), (1, 2)))
    return dict(tokens=tokens, context=context, lengths=lengths, norm_gains=norm_gains, w_qkv=w_qkv, w_out=w_out, w_q2=w_q2, w_kv2=w_kv2, w_out2=w_out2, w_in=w_in, w_down=w_down, cotangent=cotangent)


EPSILON = 1e-05
MASKED = -1000000000.0
HIGHEST = lax.Precision.HIGHEST

@jax.custom_vjp
def low(v):
    return lax.optimization_barrier(v.astype(jnp.bfloat16)).astype(jnp.float32)

@jax.custom_vjp
def low_back(v):
    return v

def low_keep(v):
    return (low(v), None)

def low_pass(kept, grad):
    return (grad,)

def back_keep(v):
    return (v, None)

def back_low(kept, grad):
    return (low(grad),)
low.defvjp(low_keep, low_pass)
low_back.defvjp(back_keep, back_low)

def layer_norm(values, gain_row):
    centred = values - lax.optimization_barrier(jnp.mean(values, axis=-1, keepdims=True))
    variance = lax.optimization_barrier(jnp.mean(centred * centred, axis=-1, keepdims=True))
    return centred * lax.rsqrt(variance + EPSILON) * gain_row

def rotate(rotated_in, cosine_table, sine_table):
    half_dim = rotated_in.shape[-1] // 2
    first_half = rotated_in[..., :half_dim]
    second_half = rotated_in[..., half_dim:]
    return jnp.concatenate([first_half * cosine_table - second_half * sine_table, second_half * cosine_table + first_half * sine_table], axis=-1)

def attend(queries, key_heads, values, key_valid):
    length_q = queries.shape[0]
    block_rows = min(512, length_q)
    scale = HEAD_DIM ** (-0.5)

    def one_block(query_block):
        scores = low_back(jnp.einsum('qhd,khd->hqk', query_block, key_heads, precision=HIGHEST) * scale)
        scores = jnp.where(key_valid[None, None, :], scores, MASKED)
        weights = low(jax.nn.softmax(scores, axis=-1))
        return low_back(low(jnp.einsum('hqk,khd->qhd', weights, values, precision=HIGHEST)))
    blocks = queries.reshape(length_q // block_rows, block_rows, HEADS, HEAD_DIM)
    return lax.map(jax.checkpoint(one_block), blocks).reshape(length_q, HEADS * HEAD_DIM)

def layer_forward(frames_in, context_row, length_one, gains, weights):
    w_qkv, w_out, w_q2, w_kv2, w_out2, w_in, w_down = weights
    length = frames_in.shape[0]
    half_dim = HEAD_DIM // 2
    frequencies = 10000.0 ** (-2.0 * jnp.arange(half_dim, dtype=jnp.float32) / HEAD_DIM)
    positions = jnp.arange(length, dtype=jnp.float32)
    angles = positions[:, None] * frequencies[None, :]
    cosine_table = jnp.cos(angles)[:, None, :]
    sine_table = jnp.sin(angles)[:, None, :]
    normed1 = low(layer_norm(frames_in, gains[0]))
    projected = low_back(jnp.dot(normed1, w_qkv, precision=HIGHEST)).reshape(length, 3, HEADS, HEAD_DIM)
    queries = low(low_back(rotate(projected[:, 0], cosine_table, sine_table)))
    key_heads = low(low_back(rotate(projected[:, 1], cosine_table, sine_table)))
    values = low(low_back(projected[:, 2]))
    everywhere = jnp.ones((length,), dtype=jnp.bool_)
    attended = attend(queries, key_heads, values, everywhere)
    first = frames_in + low_back(jnp.dot(attended, w_out, precision=HIGHEST))
    normed2 = low(layer_norm(first, gains[1]))
    query2 = low(low_back(jnp.dot(normed2, w_q2, precision=HIGHEST))).reshape(length, HEADS, HEAD_DIM)
    prompt_rows = context_row.shape[0]
    key_value = low(low_back(jnp.dot(context_row, w_kv2, precision=HIGHEST))).reshape(prompt_rows, 2, HEADS, HEAD_DIM)
    key_valid = jnp.arange(prompt_rows, dtype=jnp.int32) < length_one
    crossed = attend(query2, key_value[:, 0], key_value[:, 1], key_valid)
    second = first + low_back(jnp.dot(crossed, w_out2, precision=HIGHEST))
    normed3 = low(layer_norm(second, gains[2]))
    gate_up = low_back(jnp.dot(normed3, w_in, precision=HIGHEST))
    hidden = low(jax.nn.silu(gate_up[:, :FF]) * gate_up[:, FF:])
    return second + low_back(jnp.dot(hidden, w_down, precision=HIGHEST))

def reference(tokens, context, lengths, norm_gains, w_qkv, w_out, w_q2, w_kv2, w_out2, w_in, w_down, cotangent):
    weights = tuple((matrix.astype(jnp.float32) for matrix in (w_qkv, w_out, w_q2, w_kv2, w_out2, w_in, w_down)))
    gains = norm_gains.astype(jnp.float32)

    def one_sequence(carried, inputs):
        frames_in, context_row, length_one, cot_row = inputs

        def apply(frames_arg, gain_arg, weight_args):
            return layer_forward(frames_arg, context_row.astype(jnp.float32), length_one, gain_arg, weight_args)
        result, pullback = jax.vjp(apply, frames_in.astype(jnp.float32), gains, weights)
        frames_grad, gain_grad, weight_grads = pullback(cot_row.astype(jnp.float32))
        carried = jax.tree.map(jnp.add, carried, (gain_grad, weight_grads))
        return (carried, (result.astype(jnp.bfloat16), frames_grad))
    initial = jax.tree.map(jnp.zeros_like, (gains, weights))
    totals, outputs = lax.scan(one_sequence, initial, (tokens, context, lengths, cotangent))
    block_out, tokens_grad = outputs
    matrix_grads = totals[1]
    return (block_out, tokens_grad, totals[0], matrix_grads[0], matrix_grads[1], matrix_grads[2], matrix_grads[3], matrix_grads[4], matrix_grads[5], matrix_grads[6])
```

```python
import functools

import jax
import jax.numpy as jnp
from jax import lax
from jax.experimental import pallas as pl
from jax.experimental.pallas import tpu as pltpu
from jax.sharding import PartitionSpec as P

D = 1536
HEADS = 24
HEAD_DIM = 64
FF = 6144
CTX = 768


EPSILON = 1e-05
MASKED = -1000000000.0


def normalize(values, gain_row):
    centred = values - jnp.mean(values, axis=-1, keepdims=True)
    inverse = lax.rsqrt(jnp.mean(centred * centred, axis=-1, keepdims=True) + EPSILON)
    scaled = centred * inverse
    return (scaled * gain_row, (scaled, inverse))


def normalize_back(grad_out, gain_row, saved):
    scaled, inverse = saved
    gain_term = jnp.sum(grad_out * scaled, axis=0)
    inner = grad_out * gain_row
    result = inverse * (
        inner
        - jnp.mean(inner, axis=-1, keepdims=True)
        - scaled * jnp.mean(inner * scaled, axis=-1, keepdims=True)
    )
    return (result, gain_term)


def rotary_tables(first_frame, frame_rows):
    half_dim = HEAD_DIM // 2
    frequencies = 10000.0 ** (-2.0 * jnp.arange(half_dim, dtype=jnp.float32) / HEAD_DIM)
    positions = (first_frame + jnp.arange(frame_rows, dtype=jnp.int32)).astype(jnp.float32)
    angles = positions[:, None] * frequencies[None, :]
    return (jnp.cos(angles)[:, None, None, :], jnp.sin(angles)[:, None, None, :])


def rotate(rotated_in, cosine_table, sine_table):
    half_dim = rotated_in.shape[-1] // 2
    first_half = rotated_in[..., :half_dim]
    second_half = rotated_in[..., half_dim:]
    return jnp.concatenate(
        [
            first_half * cosine_table - second_half * sine_table,
            second_half * cosine_table + first_half * sine_table,
        ],
        axis=-1,
    )


def times_transposed(left, weight):
    return lax.dot_general(
        left, weight, (((1,), (1,)), ((), ())), preferred_element_type=jnp.float32
    )


def weight_term(left, right, spread_columns=None):

    def term_rows():
        product = lax.dot_general(
            left, right, (((0,), (0,)), ((), ())), preferred_element_type=jnp.float32
        )
        if spread_columns is None:
            return product
        return spread_columns(product)

    return lax.psum_scatter(
        term_rows().astype(jnp.bfloat16), "dp", scatter_dimension=0, tiled=True
    ).astype(jnp.float32)


def attend_forward(queries, key_heads, values, key_valid):
    length_q, local_heads, head_dim = queries.shape
    block_rows = min(512, length_q)
    scale = head_dim ** (-0.5)

    def one_block(query_block):
        scores = (
            jnp.einsum("qhd,khd->hqk", query_block, key_heads, preferred_element_type=jnp.float32)
            * scale
        )
        scores = jnp.where(key_valid[None, None, :], scores, MASKED)
        row_max = jnp.max(scores, axis=-1, keepdims=True)
        exponent = jnp.exp(scores - row_max)
        row_total = jnp.sum(exponent, axis=-1, keepdims=True)
        weights = (exponent / row_total).astype(jnp.bfloat16)
        output = jnp.einsum("hqk,khd->qhd", weights, values, preferred_element_type=jnp.float32)
        return (output.astype(jnp.bfloat16), (row_max + jnp.log(row_total))[..., 0])

    blocks = queries.reshape(length_q // block_rows, block_rows, local_heads, head_dim)
    outputs, logsum = lax.map(one_block, blocks)
    return (outputs.reshape(length_q, local_heads, head_dim), logsum)


def attend_backward(queries, key_heads, values, key_valid, logsum, out_grad):
    length_q, local_heads, head_dim = queries.shape
    block_rows = logsum.shape[2]
    scale = head_dim ** (-0.5)
    query_blocks = queries.reshape(length_q // block_rows, block_rows, local_heads, head_dim)
    grad_blocks = out_grad.reshape(length_q // block_rows, block_rows, local_heads, head_dim)

    def one_block(carried, inputs):
        key_grad, value_grad = carried
        query_block, grad_block, logsum_block = inputs
        scores = (
            jnp.einsum("qhd,khd->hqk", query_block, key_heads, preferred_element_type=jnp.float32)
            * scale
        )
        scores = jnp.where(key_valid[None, None, :], scores, MASKED)
        probabilities = jnp.exp(scores - logsum_block[..., None])
        value_grad = value_grad + jnp.einsum(
            "hqk,qhd->khd",
            probabilities.astype(jnp.bfloat16),
            grad_block,
            preferred_element_type=jnp.float32,
        )
        prob_grad = jnp.einsum(
            "qhd,khd->hqk", grad_block, values, preferred_element_type=jnp.float32
        )
        row_delta = jnp.sum(probabilities * prob_grad, axis=-1, keepdims=True)
        score_grad = (probabilities * (prob_grad - row_delta)).astype(jnp.bfloat16)
        query_grad = (
            jnp.einsum("hqk,khd->qhd", score_grad, key_heads, preferred_element_type=jnp.float32)
            * scale
        )
        key_grad = (
            key_grad
            + jnp.einsum(
                "hqk,qhd->khd", score_grad, query_block, preferred_element_type=jnp.float32
            )
            * scale
        )
        return ((key_grad, value_grad), query_grad)

    zeros_kv = jnp.zeros(key_heads.shape, jnp.float32)
    carried, query_grads = lax.scan(
        one_block, (zeros_kv, zeros_kv), (query_blocks, grad_blocks, logsum)
    )
    return (query_grads.reshape(length_q, local_heads, head_dim), carried[0], carried[1])


def self_attention(inputs, gain_row, w_qkv, w_out, cosine_table, sine_table, head_count):
    frame_rows = inputs.shape[0]
    frames = frame_rows * head_count
    local_heads = HEADS // head_count
    normed, norm_saved = normalize(inputs, gain_row)
    normed_low = normed.astype(jnp.bfloat16)
    projected = jnp.dot(normed_low, w_qkv, preferred_element_type=jnp.float32).reshape(
        frame_rows, 3, HEADS, HEAD_DIM
    )
    turned = jnp.concatenate(
        [rotate(projected[:, :2], cosine_table, sine_table), projected[:, 2:]], axis=1
    )
    turned_low = turned.astype(jnp.bfloat16).reshape(frame_rows, 3, D)
    head_major = lax.all_to_all(
        turned_low, "head", split_axis=2, concat_axis=0, tiled=True
    ).reshape(frames, 3, local_heads, HEAD_DIM)
    everywhere = jnp.ones((frames,), dtype=jnp.bool_)
    attended, logsum = attend_forward(
        head_major[:, 0], head_major[:, 1], head_major[:, 2], everywhere
    )
    frame_major = lax.all_to_all(
        attended.reshape(frames, local_heads * HEAD_DIM),
        "head",
        split_axis=0,
        concat_axis=1,
        tiled=True,
    )
    branch = jnp.dot(frame_major, w_out, preferred_element_type=jnp.float32)
    return (inputs + branch, (normed_low, norm_saved, head_major, logsum, frame_major))


def cross_attention(
    inputs, gain_row, w_q2, w_kv2, w_out2, context_low, key_valid, head_count, head_index
):
    frame_rows = inputs.shape[0]
    frames = frame_rows * head_count
    local_heads = HEADS // head_count
    local_width = local_heads * HEAD_DIM
    prompt_rows = context_low.shape[0]
    normed, norm_saved = normalize(inputs, gain_row)
    normed_low = normed.astype(jnp.bfloat16)
    query_low = jnp.dot(normed_low, w_q2, preferred_element_type=jnp.float32).astype(jnp.bfloat16)
    query_heads = lax.all_to_all(
        query_low, "head", split_axis=1, concat_axis=0, tiled=True
    ).reshape(frames, local_heads, HEAD_DIM)
    own_columns = lax.dynamic_index_in_dim(
        w_kv2.reshape(CTX, 2, head_count, local_width), head_index, 2, keepdims=False
    ).reshape(CTX, 2 * local_width)
    key_value = jnp.dot(context_low, own_columns, preferred_element_type=jnp.float32).astype(
        jnp.bfloat16
    )
    key_value = key_value.reshape(prompt_rows, 2, local_heads, HEAD_DIM)
    attended, logsum = attend_forward(query_heads, key_value[:, 0], key_value[:, 1], key_valid)
    frame_major = lax.all_to_all(
        attended.reshape(frames, local_width), "head", split_axis=0, concat_axis=1, tiled=True
    )
    branch = jnp.dot(frame_major, w_out2, preferred_element_type=jnp.float32)
    return (inputs + branch, (normed_low, norm_saved, query_heads, key_value, logsum, frame_major))


def feed_forward(inputs, gain_row, w_in, w_down):
    normed, norm_saved = normalize(inputs, gain_row)
    normed_low = normed.astype(jnp.bfloat16)
    gate_up = jnp.dot(normed_low, w_in, preferred_element_type=jnp.float32)
    gate_part = gate_up[:, :FF]
    up_part = gate_up[:, FF:]
    hidden = (jax.nn.silu(gate_part) * up_part).astype(jnp.bfloat16)
    branch = jnp.dot(hidden, w_down, preferred_element_type=jnp.float32)
    return (inputs + branch, (normed_low, norm_saved, gate_part, up_part, hidden))


def forward(
    inputs, gains, weights, context_low, key_valid, cosine_table, sine_table, head_count, head_index
):
    w_qkv, w_out, w_q2, w_kv2, w_out2, w_in, w_down = weights
    first, saved_self = self_attention(
        inputs, gains[0], w_qkv, w_out, cosine_table, sine_table, head_count
    )
    second, saved_cross = cross_attention(
        first, gains[1], w_q2, w_kv2, w_out2, context_low, key_valid, head_count, head_index
    )
    third, saved_feed = feed_forward(second, gains[2], w_in, w_down)
    return (third, (saved_self, saved_cross, saved_feed))


def backward(saved, cotangent_row, gains, weights, key_valid, cosine_table, sine_table, head_count):
    full_qkv, full_out, full_q2, full_kv2, full_out2, full_in, full_down = weights
    saved_self, saved_cross, saved_feed = saved
    frame_rows = cotangent_row.shape[0]
    frames = frame_rows * head_count
    local_heads = HEADS // head_count
    local_width = local_heads * HEAD_DIM
    normed3, norm3_saved, gate_part, up_part, hidden = saved_feed
    hidden_grad = times_transposed(cotangent_row, full_down)
    sigmoid_gate = jax.nn.sigmoid(gate_part)
    silu_gate = gate_part * sigmoid_gate
    gate_grad = hidden_grad * up_part * sigmoid_gate * (1.0 + gate_part * (1.0 - sigmoid_gate))
    up_grad = hidden_grad * silu_gate
    gate_up_grad = jnp.concatenate([gate_grad, up_grad], axis=1).astype(jnp.bfloat16)
    normed_back, gain_three = normalize_back(
        times_transposed(gate_up_grad, full_in), gains[2], norm3_saved
    )
    residual_grad = cotangent_row.astype(jnp.float32) + normed_back
    normed2, norm2_saved, query_heads, key_value, cross_logsum, cross_frames = saved_cross
    cross_low = residual_grad.astype(jnp.bfloat16)
    cross_out_grad = times_transposed(cross_low, full_out2).astype(jnp.bfloat16)
    cross_grad_heads = lax.all_to_all(
        cross_out_grad, "head", split_axis=1, concat_axis=0, tiled=True
    )
    cross_grad_heads = cross_grad_heads.reshape(frames, local_heads, HEAD_DIM)
    query_grad, key_grad, value_grad = attend_backward(
        query_heads, key_value[:, 0], key_value[:, 1], key_valid, cross_logsum, cross_grad_heads
    )
    query_frames = lax.all_to_all(
        query_grad.astype(jnp.bfloat16).reshape(frames, local_width),
        "head",
        split_axis=0,
        concat_axis=1,
        tiled=True,
    )
    prompt_rows = key_value.shape[0]
    kv_grad = (
        jnp.stack([key_grad, value_grad], axis=1)
        .astype(jnp.bfloat16)
        .reshape(prompt_rows, 2 * local_width)
    )
    normed_back, gain_two = normalize_back(
        times_transposed(query_frames, full_q2), gains[1], norm2_saved
    )
    residual_grad = residual_grad + normed_back
    normed1, norm1_saved, head_major, self_logsum, self_frames = saved_self
    self_low = residual_grad.astype(jnp.bfloat16)
    self_out_grad = times_transposed(self_low, full_out).astype(jnp.bfloat16)
    self_grad_heads = lax.all_to_all(self_out_grad, "head", split_axis=1, concat_axis=0, tiled=True)
    self_grad_heads = self_grad_heads.reshape(frames, local_heads, HEAD_DIM)
    everywhere = jnp.ones((frames,), dtype=jnp.bool_)
    query_grad, key_grad, value_grad = attend_backward(
        head_major[:, 0],
        head_major[:, 1],
        head_major[:, 2],
        everywhere,
        self_logsum,
        self_grad_heads,
    )
    stacked = jnp.stack([query_grad, key_grad, value_grad], axis=1).astype(jnp.bfloat16)
    returned = lax.all_to_all(
        stacked.reshape(frames, 3, local_width), "head", split_axis=0, concat_axis=2, tiled=True
    )
    returned = returned.reshape(frame_rows, 3, HEADS, HEAD_DIM).astype(jnp.float32)
    unturned = jnp.concatenate(
        [rotate(returned[:, :2], cosine_table, -sine_table), returned[:, 2:]], axis=1
    )
    qkv_low = unturned.astype(jnp.bfloat16).reshape(frame_rows, 3 * D)
    normed_back, gain_one = normalize_back(
        times_transposed(qkv_low, full_qkv), gains[0], norm1_saved
    )
    input_grad = residual_grad + normed_back
    pairs = (
        (normed1, qkv_low),
        (self_frames, self_low),
        (normed2, query_frames),
        (None, kv_grad),
        (cross_frames, cross_low),
        (normed3, gate_up_grad),
        (hidden, cotangent_row),
    )
    return (input_grad, jnp.stack([gain_one, gain_two, gain_three]), pairs)


def general_body(
    tokens, context, lengths, norm_gains, w_qkv, w_out, w_q2, w_kv2, w_out2, w_in, w_down, cotangent
):
    head_count = lax.axis_size("head")
    head_index = lax.axis_index("head")
    frame_rows = tokens.shape[1]
    local_heads = HEADS // head_count
    local_width = local_heads * HEAD_DIM
    prompt_rows = context.shape[1]
    cosine_table, sine_table = rotary_tables(head_index * frame_rows, frame_rows)
    weights = (
        lax.all_gather(w_qkv, "dp", axis=0, tiled=True),
        lax.all_gather(w_out, "dp", axis=0, tiled=True),
        lax.all_gather(w_q2, "dp", axis=0, tiled=True),
        lax.all_gather(w_kv2, "dp", axis=0, tiled=True),
        lax.all_gather(w_out2, "dp", axis=0, tiled=True),
        lax.all_gather(w_in, "dp", axis=0, tiled=True),
        lax.all_gather(w_down, "dp", axis=0, tiled=True),
    )

    def valid_keys(sequence):
        return jnp.arange(prompt_rows, dtype=jnp.int32) < lengths[sequence]

    collected = [[] for position in range(7)]
    sequence = 0
    output, saved = forward(
        tokens[sequence].astype(jnp.float32),
        norm_gains,
        weights,
        context[sequence],
        valid_keys(sequence),
        cosine_table,
        sine_table,
        head_count,
        head_index,
    )
    outputs = [output.astype(jnp.bfloat16)]
    input_grad, gain_terms, pairs = backward(
        saved,
        cotangent[sequence],
        norm_gains,
        weights,
        valid_keys(sequence),
        cosine_table,
        sine_table,
        head_count,
    )
    input_grads = [input_grad]
    for position in range(7):
        left_part, right_part = pairs[position]
        if left_part is None:
            left_part = context[sequence]
        collected[position].append((left_part, right_part))
    owner_mask = (jnp.arange(head_count, dtype=jnp.int32) == head_index).astype(jnp.float32)

    def spread_heads(product):
        row_count = product.shape[0]
        placed = product.reshape(row_count, 2, 1, local_width) * owner_mask[None, None, :, None]
        return placed.reshape(row_count, 2 * D)

    grad_list = []
    for position in range(7):
        lefts = jnp.concatenate([pair[0] for pair in collected[position]], axis=0)
        rights = jnp.concatenate([pair[1] for pair in collected[position]], axis=0)
        lefts, rights = (lefts, rights)
        if position == 3:
            grad_list.append(weight_term(lefts, rights, spread_heads))
        else:
            grad_list.append(weight_term(lefts, rights))
    summed = (
        lax.psum(grad_list[0].astype(jnp.bfloat16), "head").astype(jnp.float32),
        lax.psum(grad_list[1].astype(jnp.bfloat16), "head").astype(jnp.float32),
        lax.psum(grad_list[2].astype(jnp.bfloat16), "head").astype(jnp.float32),
        lax.psum(grad_list[3].astype(jnp.bfloat16), "head").astype(jnp.float32),
        lax.psum(grad_list[4].astype(jnp.bfloat16), "head").astype(jnp.float32),
        lax.psum(grad_list[5].astype(jnp.bfloat16), "head").astype(jnp.float32),
        lax.psum(grad_list[6].astype(jnp.bfloat16), "head").astype(jnp.float32),
    )
    gains_grad = lax.psum(gain_terms, ("dp", "head"))
    return (
        jnp.stack(outputs),
        jnp.stack(input_grads),
        gains_grad,
        summed[0],
        summed[1],
        summed[2],
        summed[3],
        summed[4],
        summed[5],
        summed[6],
    )


LOG2E = 1.4426950408889634
LN2 = 0.6931471805599453
ROPE_BASE = 10000.0
LANES = 128
VMEM_BYTES = 48 * 1024 * 1024


def flipped(index_bit, count):
    return [(one, one ^ index_bit) for one in range(count)]


def swap_dp(value, index_bit):
    return lax.ppermute(value, "dp", flipped(index_bit, lax.axis_size("dp")))


def swap_head(value):
    return lax.ppermute(value, "head", [(0, 1), (1, 0)])


def take(value, index, axis):
    return lax.dynamic_index_in_dim(value, index, axis, keepdims=False)


def add_low(kept, received):
    return (kept.astype(jnp.float32) + received.astype(jnp.float32)).astype(jnp.bfloat16)


def reduce_rows(term):
    rows, columns = term.shape
    place = lax.axis_index("dp")
    core, at_y, z_low, z_high = place % 2, (place // 2) % 2, (place // 4) % 2, place // 8
    part = term.reshape(2, 2, 2, 2, rows // 16, columns)
    for axis, own, bit in ((3, core, 1), (2, at_y, 2), (1, z_low, 4), (0, z_high, 8)):
        received = swap_dp(take(part, 1 - own, axis), bit)
        part = add_low(take(part, own, axis), received)
    return part


def product_rows(left, right):
    return lax.dot_general(
        left, right, (((0,), (0,)), ((), ())), preferred_element_type=jnp.float32
    )


def turn(values, cosine, sine):
    lane = lax.broadcasted_iota(jnp.int32, values.shape, 1) % HEAD_DIM
    moved = jnp.where(
        lane < HEAD_DIM // 2,
        pltpu.roll(values, LANES - HEAD_DIM // 2, 1),
        pltpu.roll(values, HEAD_DIM // 2, 1),
    )
    return values * cosine + moved * sine


def lane_tables(positions):
    half_dim = HEAD_DIM // 2
    frequencies = ROPE_BASE ** (-2.0 * jnp.arange(half_dim, dtype=jnp.float32) / HEAD_DIM)
    angles = positions.astype(jnp.float32)[:, None] * frequencies[None, :]
    cosine, sine = jnp.cos(angles), jnp.sin(angles)
    return (
        jnp.concatenate([cosine] * 4, axis=1),
        jnp.concatenate([-sine, sine, -sine, sine], axis=1),
    )


def qkv_kernel(h_ref, w_ref, cosine_ref, sine_ref, out_ref):
    width = out_ref.shape[1]
    projected = jnp.dot(h_ref[...], w_ref[...], preferred_element_type=jnp.float32)
    step = pl.program_id(0)
    third = pl.num_programs(0) // 3

    @pl.when(step < 2 * third)
    def _():
        scale = jnp.where(step < third, HEAD_DIM ** (-0.5), 1.0)
        for at in range(0, width, LANES):
            turned = turn(projected[:, at : at + LANES], cosine_ref[...], sine_ref[...])
            out_ref[:, at : at + LANES] = (turned * scale).astype(jnp.bfloat16)

    @pl.when(step >= 2 * third)
    def _():
        out_ref[...] = projected.astype(jnp.bfloat16)


def project_qkv(normed, weight, cosine, sine):
    rows, depth = normed.shape
    width = weight.shape[1]
    tile = 384
    return pl.pallas_call(
        qkv_kernel,
        name="qkv_projection",
        grid=(width // tile,),
        in_specs=[
            pl.BlockSpec((rows, depth), lambda n: (0, 0)),
            pl.BlockSpec((depth, tile), lambda n: (0, n)),
            pl.BlockSpec((rows, LANES), lambda n: (0, 0)),
            pl.BlockSpec((rows, LANES), lambda n: (0, 0)),
        ],
        out_specs=pl.BlockSpec((rows, tile), lambda n: (0, n)),
        out_shape=jax.ShapeDtypeStruct((rows, width), jnp.bfloat16),
        compiler_params=pltpu.CompilerParams(vmem_limit_bytes=VMEM_BYTES),
        cost_estimate=pl.CostEstimate(
            flops=2 * rows * depth * width,
            bytes_accessed=2 * (rows * depth + depth * width + rows * width),
            transcendentals=0,
        ),
    )(normed, weight, cosine, sine)


def nt_dot(left, right):
    return lax.dot_general(
        left, right, (((1,), (1,)), ((), ())), preferred_element_type=jnp.float32
    )


def attend_kernel(masked, length_ref, q_ref, k_ref, v_ref, out_ref, lse_ref):
    for head in range(2):
        lanes = slice(head * HEAD_DIM, (head + 1) * HEAD_DIM)
        scores = nt_dot(q_ref[:, lanes], k_ref[:, lanes])
        if masked:
            key = lax.broadcasted_iota(jnp.int32, scores.shape, 1)
            scores = jnp.where(key < length_ref[0], scores, MASKED)
        row_max = jnp.max(scores, axis=1, keepdims=True)
        exponent = jnp.exp2(scores * LOG2E - row_max * LOG2E)
        total = jnp.sum(exponent, axis=1, keepdims=True)
        mixed = jnp.dot(
            exponent.astype(jnp.bfloat16), v_ref[:, lanes], preferred_element_type=jnp.float32
        )
        out_ref[:, lanes] = (mixed / total).astype(jnp.bfloat16)
        lse_ref[:, lanes] = jnp.broadcast_to(
            row_max * LOG2E + jnp.log2(total), (row_max.shape[0], HEAD_DIM)
        )


def attend(length, queries, keys, values, width, columns, masked, name):
    rows, key_rows = queries.shape[0], keys.shape[0]
    block = 512
    pairs = width // LANES
    q_at, k_at, v_at = columns
    grid_spec = pltpu.PrefetchScalarGridSpec(
        num_scalar_prefetch=1,
        grid=(pairs, rows // block),
        in_specs=[
            pl.BlockSpec((block, LANES), lambda p, i, s: (i, q_at + p)),
            pl.BlockSpec((key_rows, LANES), lambda p, i, s: (0, k_at + p)),
            pl.BlockSpec((key_rows, LANES), lambda p, i, s: (0, v_at + p)),
        ],
        out_specs=[
            pl.BlockSpec((block, LANES), lambda p, i, s: (i, p)),
            pl.BlockSpec((block, LANES), lambda p, i, s: (i, p)),
        ],
    )
    return pl.pallas_call(
        functools.partial(attend_kernel, masked),
        name=name,
        grid_spec=grid_spec,
        out_shape=[
            jax.ShapeDtypeStruct((rows, width), jnp.bfloat16),
            jax.ShapeDtypeStruct((rows, width), jnp.float32),
        ],
        compiler_params=pltpu.CompilerParams(vmem_limit_bytes=VMEM_BYTES),
        cost_estimate=pl.CostEstimate(
            flops=16 * rows * key_rows * width,
            bytes_accessed=8 * rows * width,
            transcendentals=rows * key_rows * width // HEAD_DIM,
        ),
    )(length, queries, keys, values)


def attend_back_kernel(
    masked,
    turned,
    length_ref,
    q_ref,
    k_ref,
    v_ref,
    grad_ref,
    out_ref,
    lse_ref,
    *rest,
):
    if turned:
        cosq_ref, sinq_ref, cosk_ref, sink_ref = rest[:4]
        rest = rest[4:]
    dq_ref, dk_ref, dv_ref, dk_sum, dv_sum = rest
    step, steps = pl.program_id(1), pl.num_programs(1)

    @pl.when(step == 0)
    def _():
        dk_sum[...] = jnp.zeros_like(dk_sum)
        dv_sum[...] = jnp.zeros_like(dv_sum)

    lse_rows = lse_ref[...].T
    delta_rows = (grad_ref[...].astype(jnp.float32) * out_ref[...].astype(jnp.float32)).T
    dq_parts = []
    for head in range(2):
        lanes = slice(head * HEAD_DIM, (head + 1) * HEAD_DIM)
        query, key, value = q_ref[:, lanes], k_ref[:, lanes], v_ref[:, lanes]
        grad = grad_ref[:, lanes]
        scores = nt_dot(key, query)
        if masked:
            index = lax.broadcasted_iota(jnp.int32, scores.shape, 0)
            scores = jnp.where(index < length_ref[0], scores, MASKED)
        lse = lse_rows[head * HEAD_DIM : head * HEAD_DIM + 1, :]
        delta = jnp.sum(delta_rows[lanes, :], axis=0, keepdims=True)
        weight = jnp.exp2(scores * LOG2E - lse)
        dv_sum[:, lanes] += jnp.dot(
            weight.astype(jnp.bfloat16), grad, preferred_element_type=jnp.float32
        )
        weight_grad = nt_dot(value, grad)
        score_grad = (weight * (weight_grad - delta)).astype(jnp.bfloat16)
        dk_sum[:, lanes] += jnp.dot(score_grad, query, preferred_element_type=jnp.float32)
        dq_parts.append(product_rows(score_grad, key) * HEAD_DIM ** (-0.5))
    dq = jnp.concatenate(dq_parts, axis=1).astype(jnp.bfloat16)
    if turned:
        dq = turn(dq.astype(jnp.float32), cosq_ref[...], -sinq_ref[...]).astype(jnp.bfloat16)
    dq_ref[...] = dq

    @pl.when(step == steps - 1)
    def _():
        dk = dk_sum[...].astype(jnp.bfloat16)
        if turned:
            dk = turn(dk.astype(jnp.float32), cosk_ref[...], -sink_ref[...]).astype(jnp.bfloat16)
        dk_ref[...] = dk
        dv_ref[...] = dv_sum[...].astype(jnp.bfloat16)


def attend_back(
    length, queries, keys, values, columns, grad, outputs, lse, tables, masked, name
):
    rows, key_rows = queries.shape[0], keys.shape[0]
    width = grad.shape[1]
    block = 256
    pairs = width // LANES
    q_at, k_at, v_at = columns
    by_query = pl.BlockSpec((block, LANES), lambda p, i, s: (i, p))
    by_key = pl.BlockSpec((key_rows, LANES), lambda p, i, s: (0, p))
    in_specs = [
        pl.BlockSpec((block, LANES), lambda p, i, s: (i, q_at + p)),
        pl.BlockSpec((key_rows, LANES), lambda p, i, s: (0, k_at + p)),
        pl.BlockSpec((key_rows, LANES), lambda p, i, s: (0, v_at + p)),
        by_query,
        by_query,
        by_query,
    ]
    operands = [queries, keys, values, grad, outputs, lse]
    if tables is not None:
        cosine, sine = tables
        in_specs += [pl.BlockSpec((block, LANES), lambda p, i, s: (i, 0))] * 2
        in_specs += [pl.BlockSpec((key_rows, LANES), lambda p, i, s: (0, 0))] * 2
        operands += [cosine, sine, cosine, sine]
    grid_spec = pltpu.PrefetchScalarGridSpec(
        num_scalar_prefetch=1,
        grid=(pairs, rows // block),
        in_specs=in_specs,
        out_specs=[by_query, by_key, by_key],
        scratch_shapes=[pltpu.VMEM((key_rows, LANES), jnp.float32)] * 2,
    )
    return pl.pallas_call(
        functools.partial(attend_back_kernel, masked, tables is not None),
        name=name,
        grid_spec=grid_spec,
        out_shape=[
            jax.ShapeDtypeStruct((rows, width), jnp.bfloat16),
            jax.ShapeDtypeStruct((key_rows, width), jnp.bfloat16),
            jax.ShapeDtypeStruct((key_rows, width), jnp.bfloat16),
        ],
        compiler_params=pltpu.CompilerParams(vmem_limit_bytes=VMEM_BYTES),
        cost_estimate=pl.CostEstimate(
            flops=40 * rows * key_rows * width,
            bytes_accessed=20 * rows * width,
            transcendentals=rows * key_rows * width // HEAD_DIM,
        ),
    )(length, *operands)


def feed_kernel(h_ref, cot_ref, gate_ref, up_ref, down_ref, *rest):
    hidden_ref, dgate_ref, dup_ref = rest[-3:]
    gate = jnp.dot(h_ref[...], gate_ref[...], preferred_element_type=jnp.float32)
    up = jnp.dot(h_ref[...], up_ref[...], preferred_element_type=jnp.float32)
    grad = nt_dot(cot_ref[...], down_ref[...])
    sigmoid = jax.nn.sigmoid(gate)
    silu = gate * sigmoid
    hidden_ref[...] = (silu * up).astype(jnp.bfloat16)
    dup_ref[...] = (grad * silu).astype(jnp.bfloat16)
    dgate_ref[...] = (grad * up * sigmoid * (1.0 + gate * (1.0 - sigmoid))).astype(jnp.bfloat16)


def feed(normed, cotangent, w_in, w_down, half, earlier):
    rows, depth = normed.shape
    units = w_down.shape[0]
    tile = 512
    steps = units // tile
    out_spec = pl.BlockSpec((rows, tile), lambda n: (half, n))
    in_specs = [
        pl.BlockSpec((rows, depth), lambda n: (0, 0)),
        pl.BlockSpec((rows, depth), lambda n: (0, 0)),
        pl.BlockSpec((depth, tile), lambda n: (0, n)),
        pl.BlockSpec((depth, tile), lambda n: (0, steps + n)),
        pl.BlockSpec((tile, depth), lambda n: (n, 0)),
    ]
    operands = [normed, cotangent, w_in, w_in, w_down]
    aliases = {}
    if earlier is not None:
        in_specs += [pl.BlockSpec(memory_space=pl.ANY)] * 3
        aliases = {5: 0, 6: 1, 7: 2}
        operands += list(earlier)
    return pl.pallas_call(
        feed_kernel,
        name="feed_forward",
        grid=(steps,),
        in_specs=in_specs,
        out_specs=[out_spec] * 3,
        out_shape=[jax.ShapeDtypeStruct((2 * rows, units), jnp.bfloat16)] * 3,
        input_output_aliases=aliases,
        compiler_params=pltpu.CompilerParams(vmem_limit_bytes=VMEM_BYTES),
        cost_estimate=pl.CostEstimate(
            flops=6 * rows * depth * units,
            bytes_accessed=6 * depth * units + 6 * rows * units + 4 * rows * depth,
            transcendentals=rows * units,
        ),
    )(*operands)


def paired_body(
    tokens, context, lengths, norm_gains, w_qkv, w_out, w_q2, w_kv2, w_out2, w_in, w_down, cotangent
):
    place, side = lax.axis_index("dp"), lax.axis_index("head")
    core = place % 2
    on_left = side == 0
    own = tokens[0]
    frames = own.shape[0]
    rows = w_qkv.shape[0]
    half = D // 2
    units = w_down.shape[0]

    def ordered(mine, theirs):
        return jnp.where(on_left, mine, theirs), jnp.where(on_left, theirs, mine)

    qkv_half = take(w_qkv.reshape(rows, 3, 2, half), side, 2).reshape(rows, 3 * half)
    full_qkv = lax.all_gather(qkv_half, "dp", axis=0, tiled=True)
    small = jnp.concatenate([w_out, w_q2, w_out2], axis=1)
    full_small = lax.all_gather(small, "dp", axis=0, tiled=True)
    full_out, full_q2, full_out2 = full_small[:, :D], full_small[:, D : 2 * D], full_small[:, 2 * D :]
    full_kv2 = lax.all_gather(w_kv2, "dp", axis=0, tiled=True)
    in_half = take(w_in.reshape(rows, 2, 8, 2, units), side, 3).reshape(rows, FF)
    full_in = lax.all_gather(in_half, "dp", axis=0, tiled=True)
    down_parts = w_down.reshape(2, units // 2, D)
    down_received = swap_dp(take(down_parts, 1 - core, 0), 1)
    down_half = jnp.where(core == side, take(down_parts, core, 0), down_received)
    full_down = lax.all_gather(down_half, "dp", axis=0, tiled=True)

    both_tokens = jnp.concatenate([own, swap_head(own)], axis=0).astype(jnp.float32)
    other_cot = swap_head(cotangent[0])
    frame = jnp.arange(frames, dtype=jnp.int32)
    tables = lane_tables(
        jnp.concatenate([side * frames + frame, (1 - side) * frames + frame])
    )
    normed1 = normalize(both_tokens, norm_gains[0])[0].astype(jnp.bfloat16)
    inputs = own.astype(jnp.float32)
    norm1_saved = normalize(inputs, norm_gains[0])[1]
    qkv = project_qkv(normed1, full_qkv, *tables)
    no_length = jnp.zeros((1,), jnp.int32)
    pairs = half // LANES
    self_columns = (0, pairs, 2 * pairs)
    attended, self_lse = attend(
        no_length, qkv, qkv, qkv, half, self_columns, False, "self_attention"
    )
    attended_other = swap_head(attended[frames:])
    attended_frames = jnp.concatenate(ordered(attended[:frames], attended_other), axis=1)
    first = inputs + jnp.dot(attended_frames, full_out, preferred_element_type=jnp.float32)

    normed2, norm2_saved = normalize(first, norm_gains[1])
    normed2 = normed2.astype(jnp.bfloat16)
    query2 = jnp.dot(normed2, full_q2, preferred_element_type=jnp.float32)
    query2 = (query2.astype(jnp.bfloat16) * HEAD_DIM ** (-0.5)).astype(jnp.bfloat16)
    key_value = jnp.dot(context[0], full_kv2, preferred_element_type=jnp.float32).astype(
        jnp.bfloat16
    )
    cross_columns = (0, 0, D // LANES)
    crossed, cross_lse = attend(
        lengths, query2, key_value, key_value, D, cross_columns, True, "cross_attention"
    )
    second = first + jnp.dot(crossed, full_out2, preferred_element_type=jnp.float32)

    normed3, norm3_saved = normalize(second, norm_gains[2])
    normed3 = normed3.astype(jnp.bfloat16)
    other3 = swap_head(normed3)
    own_cot = cotangent[0]
    fed = feed(normed3, own_cot, full_in, full_down, 0, None)
    hidden, dgate, dup = feed(other3, other_cot, full_in, full_down, 1, fed)
    gate_columns, up_columns = full_in[:, : FF // 2], full_in[:, FF // 2 :]

    def back_to_h3(at):
        return nt_dot(dgate[at : at + frames], gate_columns) + nt_dot(
            dup[at : at + frames], up_columns
        )

    received3 = swap_head(back_to_h3(frames).astype(jnp.bfloat16))
    normed_grad = back_to_h3(0) + received3.astype(jnp.float32)
    both_normed3 = jnp.concatenate([normed3, other3], axis=0)
    both_cot = jnp.concatenate([own_cot, other_cot], axis=0)
    down_rows = reduce_rows(product_rows(hidden, both_cot).astype(jnp.bfloat16))
    gate_rows = reduce_rows(product_rows(both_normed3, dgate).astype(jnp.bfloat16))
    up_rows = reduce_rows(product_rows(both_normed3, dup).astype(jnp.bfloat16))

    down_sent = jnp.dot(hidden[frames:], full_down, preferred_element_type=jnp.float32)
    down_received = swap_head(down_sent.astype(jnp.bfloat16))
    output = (
        second
        + jnp.dot(hidden[:frames], full_down, preferred_element_type=jnp.float32)
        + down_received.astype(jnp.float32)
    ).astype(jnp.bfloat16)

    normed_back, gain_three = normalize_back(normed_grad, norm_gains[2], norm3_saved)
    residual_grad = own_cot.astype(jnp.float32) + normed_back
    cross_low = residual_grad.astype(jnp.bfloat16)
    cross_grad = nt_dot(cross_low, full_out2).astype(jnp.bfloat16)
    query2_grad, key2_grad, value2_grad = attend_back(
        lengths,
        query2,
        key_value,
        key_value,
        cross_columns,
        cross_grad,
        crossed,
        cross_lse,
        None,
        True,
        "cross_attention_back",
    )
    out2_rows = reduce_rows(product_rows(crossed, cross_low).astype(jnp.bfloat16))
    q2_rows = reduce_rows(product_rows(normed2, query2_grad).astype(jnp.bfloat16))
    kv2_grad = jnp.concatenate([key2_grad, value2_grad], axis=1)
    kv2_rows = reduce_rows(product_rows(context[0], kv2_grad).astype(jnp.bfloat16))
    normed_back, gain_two = normalize_back(
        nt_dot(query2_grad, full_q2), norm_gains[1], norm2_saved
    )
    residual_grad = residual_grad + normed_back

    self_low = residual_grad.astype(jnp.bfloat16)
    self_grad = nt_dot(self_low, full_out).astype(jnp.bfloat16)
    left_grad, right_grad = self_grad[:, :half], self_grad[:, half:]
    grad_kept = jnp.where(on_left, left_grad, right_grad)
    grad_received = swap_head(jnp.where(on_left, right_grad, left_grad))
    heads_grad = jnp.concatenate([grad_kept, grad_received], axis=0)
    out_rows = reduce_rows(product_rows(attended_frames, self_low).astype(jnp.bfloat16))
    query_grad, key_grad, value_grad = attend_back(
        no_length,
        qkv,
        qkv,
        qkv,
        self_columns,
        heads_grad,
        attended,
        self_lse,
        tables,
        False,
        "self_attention_back",
    )
    qkv_grad = jnp.concatenate([query_grad, key_grad, value_grad], axis=1)
    sent1 = nt_dot(qkv_grad[frames:], full_qkv).astype(jnp.bfloat16)
    received1 = swap_head(sent1)
    qkv_rows = reduce_rows(product_rows(normed1, qkv_grad).astype(jnp.bfloat16))
    normed_grad = nt_dot(qkv_grad[:frames], full_qkv) + received1.astype(jnp.float32)
    normed_back, gain_one = normalize_back(normed_grad, norm_gains[0], norm1_saved)
    input_grad = residual_grad + normed_back

    gains = jnp.stack([gain_one, gain_two, gain_three])
    for bit in (1, 2, 4, 8):
        gains = gains + swap_dp(gains, bit)
    gains = gains + swap_head(gains)

    def joined(mine):
        lower, upper = ordered(mine, swap_head(mine))
        return jnp.stack([lower, upper], axis=-2)

    def added(mine):
        return mine.astype(jnp.float32) + swap_head(mine).astype(jnp.float32)

    qkv_out = joined(qkv_rows.reshape(rows, 3, half)).reshape(rows, 3 * D).astype(jnp.float32)
    in_out = jnp.concatenate(
        [
            joined(part.reshape(rows, 8, units)).reshape(rows, FF).astype(jnp.float32)
            for part in (gate_rows, up_rows)
        ],
        axis=1,
    )
    down_other = swap_dp(down_rows, 1)
    down_block = jnp.concatenate(
        [
            jnp.where(core == 0, down_rows, down_other),
            jnp.where(core == 0, down_other, down_rows),
        ],
        axis=0,
    )
    crossing = [
        (2 * at + (at % 2), 2 * at + 1 - (at % 2)) for at in range(lax.axis_size("dp"))
    ]
    down_crossed = lax.ppermute(down_block, ("dp", "head"), crossing)
    down_out = jnp.where(core == side, down_block, down_crossed).astype(jnp.float32)
    return (
        output[None],
        input_grad[None],
        gains,
        qkv_out,
        added(out_rows),
        added(q2_rows),
        added(kv2_rows),
        added(out2_rows),
        in_out,
        down_out,
    )


def body(*arrays):
    if lax.axis_size("dp") == 16 and lax.axis_size("head") == 2 and arrays[0].shape[0] == 1:
        return paired_body(*arrays)
    return general_body(*arrays)


def solution(mesh):
    placed = (
        P("dp", "head", None),
        P("dp", None, None),
        P("dp"),
        P(),
        P("dp", None),
        P("dp", None),
        P("dp", None),
        P("dp", None),
        P("dp", None),
        P("dp", None),
        P("dp", None),
        P("dp", "head", None),
    )
    return jax.shard_map(
        body,
        mesh=mesh,
        in_specs=placed,
        out_specs=(
            P("dp", "head", None),
            P("dp", "head", None),
            P(),
            P("dp", None),
            P("dp", None),
            P("dp", None),
            P("dp", None),
            P("dp", None),
            P("dp", None),
            P("dp", None),
        ),
        check_vma=False,
    )
```

```python
import functools

import jax
import jax.numpy as jnp
from jax import lax
from jax.experimental import pallas as pl
from jax.experimental.pallas import tpu as pltpu
from jax.sharding import PartitionSpec as P

D = 1536
HEADS = 24
HEAD_DIM = 64
FF = 6144
CTX = 768


EPSILON = 1e-05
MASKED = -1000000000.0


def normalize(values, gain_row):
    centred = values - jnp.mean(values, axis=-1, keepdims=True)
    inverse = lax.rsqrt(jnp.mean(centred * centred, axis=-1, keepdims=True) + EPSILON)
    scaled = centred * inverse
    return (scaled * gain_row, (scaled, inverse))


def normalize_back(grad_out, gain_row, saved):
    scaled, inverse = saved
    gain_term = jnp.sum(grad_out * scaled, axis=0)
    inner = grad_out * gain_row
    result = inverse * (
        inner
        - jnp.mean(inner, axis=-1, keepdims=True)
        - scaled * jnp.mean(inner * scaled, axis=-1, keepdims=True)
    )
    return (result, gain_term)


def rotary_tables(first_frame, frame_rows):
    half_dim = HEAD_DIM // 2
    frequencies = 10000.0 ** (-2.0 * jnp.arange(half_dim, dtype=jnp.float32) / HEAD_DIM)
    positions = (first_frame + jnp.arange(frame_rows, dtype=jnp.int32)).astype(jnp.float32)
    angles = positions[:, None] * frequencies[None, :]
    return (jnp.cos(angles)[:, None, None, :], jnp.sin(angles)[:, None, None, :])


def rotate(rotated_in, cosine_table, sine_table):
    half_dim = rotated_in.shape[-1] // 2
    first_half = rotated_in[..., :half_dim]
    second_half = rotated_in[..., half_dim:]
    return jnp.concatenate(
        [
            first_half * cosine_table - second_half * sine_table,
            second_half * cosine_table + first_half * sine_table,
        ],
        axis=-1,
    )


def times_transposed(left, weight):
    return lax.dot_general(
        left, weight, (((1,), (1,)), ((), ())), preferred_element_type=jnp.float32
    )


def weight_term(left, right, spread_columns=None):

    def term_rows():
        product = lax.dot_general(
            left, right, (((0,), (0,)), ((), ())), preferred_element_type=jnp.float32
        )
        if spread_columns is None:
            return product
        return spread_columns(product)

    return lax.psum_scatter(
        term_rows().astype(jnp.bfloat16), "dp", scatter_dimension=0, tiled=True
    ).astype(jnp.float32)


def attend_forward(queries, key_heads, values, key_valid):
    length_q, local_heads, head_dim = queries.shape
    block_rows = min(512, length_q)
    scale = head_dim ** (-0.5)

    def one_block(query_block):
        scores = (
            jnp.einsum("qhd,khd->hqk", query_block, key_heads, preferred_element_type=jnp.float32)
            * scale
        )
        scores = jnp.where(key_valid[None, None, :], scores, MASKED)
        row_max = jnp.max(scores, axis=-1, keepdims=True)
        exponent = jnp.exp(scores - row_max)
        row_total = jnp.sum(exponent, axis=-1, keepdims=True)
        weights = (exponent / row_total).astype(jnp.bfloat16)
        output = jnp.einsum("hqk,khd->qhd", weights, values, preferred_element_type=jnp.float32)
        return (output.astype(jnp.bfloat16), (row_max + jnp.log(row_total))[..., 0])

    blocks = queries.reshape(length_q // block_rows, block_rows, local_heads, head_dim)
    outputs, logsum = lax.map(one_block, blocks)
    return (outputs.reshape(length_q, local_heads, head_dim), logsum)


def attend_backward(queries, key_heads, values, key_valid, logsum, out_grad):
    length_q, local_heads, head_dim = queries.shape
    block_rows = logsum.shape[2]
    scale = head_dim ** (-0.5)
    query_blocks = queries.reshape(length_q // block_rows, block_rows, local_heads, head_dim)
    grad_blocks = out_grad.reshape(length_q // block_rows, block_rows, local_heads, head_dim)

    def one_block(carried, inputs):
        key_grad, value_grad = carried
        query_block, grad_block, logsum_block = inputs
        scores = (
            jnp.einsum("qhd,khd->hqk", query_block, key_heads, preferred_element_type=jnp.float32)
            * scale
        )
        scores = jnp.where(key_valid[None, None, :], scores, MASKED)
        probabilities = jnp.exp(scores - logsum_block[..., None])
        value_grad = value_grad + jnp.einsum(
            "hqk,qhd->khd",
            probabilities.astype(jnp.bfloat16),
            grad_block,
            preferred_element_type=jnp.float32,
        )
        prob_grad = jnp.einsum(
            "qhd,khd->hqk", grad_block, values, preferred_element_type=jnp.float32
        )
        row_delta = jnp.sum(probabilities * prob_grad, axis=-1, keepdims=True)
        score_grad = (probabilities * (prob_grad - row_delta)).astype(jnp.bfloat16)
        query_grad = (
            jnp.einsum("hqk,khd->qhd", score_grad, key_heads, preferred_element_type=jnp.float32)
            * scale
        )
        key_grad = (
            key_grad
            + jnp.einsum(
                "hqk,qhd->khd", score_grad, query_block, preferred_element_type=jnp.float32
            )
            * scale
        )
        return ((key_grad, value_grad), query_grad)

    zeros_kv = jnp.zeros(key_heads.shape, jnp.float32)
    carried, query_grads = lax.scan(
        one_block, (zeros_kv, zeros_kv), (query_blocks, grad_blocks, logsum)
    )
    return (query_grads.reshape(length_q, local_heads, head_dim), carried[0], carried[1])


def self_attention(inputs, gain_row, w_qkv, w_out, cosine_table, sine_table, head_count):
    frame_rows = inputs.shape[0]
    frames = frame_rows * head_count
    local_heads = HEADS // head_count
    normed, norm_saved = normalize(inputs, gain_row)
    normed_low = normed.astype(jnp.bfloat16)
    projected = jnp.dot(normed_low, w_qkv, preferred_element_type=jnp.float32).reshape(
        frame_rows, 3, HEADS, HEAD_DIM
    )
    turned = jnp.concatenate(
        [rotate(projected[:, :2], cosine_table, sine_table), projected[:, 2:]], axis=1
    )
    turned_low = turned.astype(jnp.bfloat16).reshape(frame_rows, 3, D)
    head_major = lax.all_to_all(
        turned_low, "head", split_axis=2, concat_axis=0, tiled=True
    ).reshape(frames, 3, local_heads, HEAD_DIM)
    everywhere = jnp.ones((frames,), dtype=jnp.bool_)
    attended, logsum = attend_forward(
        head_major[:, 0], head_major[:, 1], head_major[:, 2], everywhere
    )
    frame_major = lax.all_to_all(
        attended.reshape(frames, local_heads * HEAD_DIM),
        "head",
        split_axis=0,
        concat_axis=1,
        tiled=True,
    )
    branch = jnp.dot(frame_major, w_out, preferred_element_type=jnp.float32)
    return (inputs + branch, (normed_low, norm_saved, head_major, logsum, frame_major))


def cross_attention(
    inputs, gain_row, w_q2, w_kv2, w_out2, context_low, key_valid, head_count, head_index
):
    frame_rows = inputs.shape[0]
    frames = frame_rows * head_count
    local_heads = HEADS // head_count
    local_width = local_heads * HEAD_DIM
    prompt_rows = context_low.shape[0]
    normed, norm_saved = normalize(inputs, gain_row)
    normed_low = normed.astype(jnp.bfloat16)
    query_low = jnp.dot(normed_low, w_q2, preferred_element_type=jnp.float32).astype(jnp.bfloat16)
    query_heads = lax.all_to_all(
        query_low, "head", split_axis=1, concat_axis=0, tiled=True
    ).reshape(frames, local_heads, HEAD_DIM)
    own_columns = lax.dynamic_index_in_dim(
        w_kv2.reshape(CTX, 2, head_count, local_width), head_index, 2, keepdims=False
    ).reshape(CTX, 2 * local_width)
    key_value = jnp.dot(context_low, own_columns, preferred_element_type=jnp.float32).astype(
        jnp.bfloat16
    )
    key_value = key_value.reshape(prompt_rows, 2, local_heads, HEAD_DIM)
    attended, logsum = attend_forward(query_heads, key_value[:, 0], key_value[:, 1], key_valid)
    frame_major = lax.all_to_all(
        attended.reshape(frames, local_width), "head", split_axis=0, concat_axis=1, tiled=True
    )
    branch = jnp.dot(frame_major, w_out2, preferred_element_type=jnp.float32)
    return (inputs + branch, (normed_low, norm_saved, query_heads, key_value, logsum, frame_major))


def feed_forward(inputs, gain_row, w_in, w_down):
    normed, norm_saved = normalize(inputs, gain_row)
    normed_low = normed.astype(jnp.bfloat16)
    gate_up = jnp.dot(normed_low, w_in, preferred_element_type=jnp.float32)
    gate_part = gate_up[:, :FF]
    up_part = gate_up[:, FF:]
    hidden = (jax.nn.silu(gate_part) * up_part).astype(jnp.bfloat16)
    branch = jnp.dot(hidden, w_down, preferred_element_type=jnp.float32)
    return (inputs + branch, (normed_low, norm_saved, gate_part, up_part, hidden))


def forward(
    inputs, gains, weights, context_low, key_valid, cosine_table, sine_table, head_count, head_index
):
    w_qkv, w_out, w_q2, w_kv2, w_out2, w_in, w_down = weights
    first, saved_self = self_attention(
        inputs, gains[0], w_qkv, w_out, cosine_table, sine_table, head_count
    )
    second, saved_cross = cross_attention(
        first, gains[1], w_q2, w_kv2, w_out2, context_low, key_valid, head_count, head_index
    )
    third, saved_feed = feed_forward(second, gains[2], w_in, w_down)
    return (third, (saved_self, saved_cross, saved_feed))


def backward(saved, cotangent_row, gains, weights, key_valid, cosine_table, sine_table, head_count):
    full_qkv, full_out, full_q2, full_kv2, full_out2, full_in, full_down = weights
    saved_self, saved_cross, saved_feed = saved
    frame_rows = cotangent_row.shape[0]
    frames = frame_rows * head_count
    local_heads = HEADS // head_count
    local_width = local_heads * HEAD_DIM
    normed3, norm3_saved, gate_part, up_part, hidden = saved_feed
    hidden_grad = times_transposed(cotangent_row, full_down)
    sigmoid_gate = jax.nn.sigmoid(gate_part)
    silu_gate = gate_part * sigmoid_gate
    gate_grad = hidden_grad * up_part * sigmoid_gate * (1.0 + gate_part * (1.0 - sigmoid_gate))
    up_grad = hidden_grad * silu_gate
    gate_up_grad = jnp.concatenate([gate_grad, up_grad], axis=1).astype(jnp.bfloat16)
    normed_back, gain_three = normalize_back(
        times_transposed(gate_up_grad, full_in), gains[2], norm3_saved
    )
    residual_grad = cotangent_row.astype(jnp.float32) + normed_back
    normed2, norm2_saved, query_heads, key_value, cross_logsum, cross_frames = saved_cross
    cross_low = residual_grad.astype(jnp.bfloat16)
    cross_out_grad = times_transposed(cross_low, full_out2).astype(jnp.bfloat16)
    cross_grad_heads = lax.all_to_all(
        cross_out_grad, "head", split_axis=1, concat_axis=0, tiled=True
    )
    cross_grad_heads = cross_grad_heads.reshape(frames, local_heads, HEAD_DIM)
    query_grad, key_grad, value_grad = attend_backward(
        query_heads, key_value[:, 0], key_value[:, 1], key_valid, cross_logsum, cross_grad_heads
    )
    query_frames = lax.all_to_all(
        query_grad.astype(jnp.bfloat16).reshape(frames, local_width),
        "head",
        split_axis=0,
        concat_axis=1,
        tiled=True,
    )
    prompt_rows = key_value.shape[0]
    kv_grad = (
        jnp.stack([key_grad, value_grad], axis=1)
        .astype(jnp.bfloat16)
        .reshape(prompt_rows, 2 * local_width)
    )
    normed_back, gain_two = normalize_back(
        times_transposed(query_frames, full_q2), gains[1], norm2_saved
    )
    residual_grad = residual_grad + normed_back
    normed1, norm1_saved, head_major, self_logsum, self_frames = saved_self
    self_low = residual_grad.astype(jnp.bfloat16)
    self_out_grad = times_transposed(self_low, full_out).astype(jnp.bfloat16)
    self_grad_heads = lax.all_to_all(self_out_grad, "head", split_axis=1, concat_axis=0, tiled=True)
    self_grad_heads = self_grad_heads.reshape(frames, local_heads, HEAD_DIM)
    everywhere = jnp.ones((frames,), dtype=jnp.bool_)
    query_grad, key_grad, value_grad = attend_backward(
        head_major[:, 0],
        head_major[:, 1],
        head_major[:, 2],
        everywhere,
        self_logsum,
        self_grad_heads,
    )
    stacked = jnp.stack([query_grad, key_grad, value_grad], axis=1).astype(jnp.bfloat16)
    returned = lax.all_to_all(
        stacked.reshape(frames, 3, local_width), "head", split_axis=0, concat_axis=2, tiled=True
    )
    returned = returned.reshape(frame_rows, 3, HEADS, HEAD_DIM).astype(jnp.float32)
    unturned = jnp.concatenate(
        [rotate(returned[:, :2], cosine_table, -sine_table), returned[:, 2:]], axis=1
    )
    qkv_low = unturned.astype(jnp.bfloat16).reshape(frame_rows, 3 * D)
    normed_back, gain_one = normalize_back(
        times_transposed(qkv_low, full_qkv), gains[0], norm1_saved
    )
    input_grad = residual_grad + normed_back
    pairs = (
        (normed1, qkv_low),
        (self_frames, self_low),
        (normed2, query_frames),
        (None, kv_grad),
        (cross_frames, cross_low),
        (normed3, gate_up_grad),
        (hidden, cotangent_row),
    )
    return (input_grad, jnp.stack([gain_one, gain_two, gain_three]), pairs)


def general_body(
    tokens, context, lengths, norm_gains, w_qkv, w_out, w_q2, w_kv2, w_out2, w_in, w_down, cotangent
):
    head_count = lax.axis_size("head")
    head_index = lax.axis_index("head")
    frame_rows = tokens.shape[1]
    local_heads = HEADS // head_count
    local_width = local_heads * HEAD_DIM
    prompt_rows = context.shape[1]
    cosine_table, sine_table = rotary_tables(head_index * frame_rows, frame_rows)
    weights = (
        lax.all_gather(w_qkv, "dp", axis=0, tiled=True),
        lax.all_gather(w_out, "dp", axis=0, tiled=True),
        lax.all_gather(w_q2, "dp", axis=0, tiled=True),
        lax.all_gather(w_kv2, "dp", axis=0, tiled=True),
        lax.all_gather(w_out2, "dp", axis=0, tiled=True),
        lax.all_gather(w_in, "dp", axis=0, tiled=True),
        lax.all_gather(w_down, "dp", axis=0, tiled=True),
    )

    def valid_keys(sequence):
        return jnp.arange(prompt_rows, dtype=jnp.int32) < lengths[sequence]

    collected = [[] for position in range(7)]
    sequence = 0
    output, saved = forward(
        tokens[sequence].astype(jnp.float32),
        norm_gains,
        weights,
        context[sequence],
        valid_keys(sequence),
        cosine_table,
        sine_table,
        head_count,
        head_index,
    )
    outputs = [output.astype(jnp.bfloat16)]
    input_grad, gain_terms, pairs = backward(
        saved,
        cotangent[sequence],
        norm_gains,
        weights,
        valid_keys(sequence),
        cosine_table,
        sine_table,
        head_count,
    )
    input_grads = [input_grad]
    for position in range(7):
        left_part, right_part = pairs[position]
        if left_part is None:
            left_part = context[sequence]
        collected[position].append((left_part, right_part))
    owner_mask = (jnp.arange(head_count, dtype=jnp.int32) == head_index).astype(jnp.float32)

    def spread_heads(product):
        row_count = product.shape[0]
        placed = product.reshape(row_count, 2, 1, local_width) * owner_mask[None, None, :, None]
        return placed.reshape(row_count, 2 * D)

    grad_list = []
    for position in range(7):
        lefts = jnp.concatenate([pair[0] for pair in collected[position]], axis=0)
        rights = jnp.concatenate([pair[1] for pair in collected[position]], axis=0)
        lefts, rights = (lefts, rights)
        if position == 3:
            grad_list.append(weight_term(lefts, rights, spread_heads))
        else:
            grad_list.append(weight_term(lefts, rights))
    summed = (
        lax.psum(grad_list[0].astype(jnp.bfloat16), "head").astype(jnp.float32),
        lax.psum(grad_list[1].astype(jnp.bfloat16), "head").astype(jnp.float32),
        lax.psum(grad_list[2].astype(jnp.bfloat16), "head").astype(jnp.float32),
        lax.psum(grad_list[3].astype(jnp.bfloat16), "head").astype(jnp.float32),
        lax.psum(grad_list[4].astype(jnp.bfloat16), "head").astype(jnp.float32),
        lax.psum(grad_list[5].astype(jnp.bfloat16), "head").astype(jnp.float32),
        lax.psum(grad_list[6].astype(jnp.bfloat16), "head").astype(jnp.float32),
    )
    gains_grad = lax.psum(gain_terms, ("dp", "head"))
    return (
        jnp.stack(outputs),
        jnp.stack(input_grads),
        gains_grad,
        summed[0],
        summed[1],
        summed[2],
        summed[3],
        summed[4],
        summed[5],
        summed[6],
    )


LOG2E = 1.4426950408889634
LN2 = 0.6931471805599453
ROPE_BASE = 10000.0
LANES = 128
VMEM_BYTES = 48 * 1024 * 1024
SHARE = 1


def declared(flops, bytes_accessed, transcendentals):
    return pl.CostEstimate(
        flops=flops // SHARE,
        bytes_accessed=bytes_accessed // SHARE,
        transcendentals=transcendentals // SHARE,
    )


def in_order(*values):
    return lax.optimization_barrier(values)


def flipped(index_bit, count):
    return [(one, one ^ index_bit) for one in range(count)]


def swap_dp(value, index_bit):
    return lax.ppermute(value, "dp", flipped(index_bit, lax.axis_size("dp")))


def swap_head(value):
    return lax.ppermute(value, "head", [(0, 1), (1, 0)])


def take(value, index, axis):
    return lax.dynamic_index_in_dim(value, index, axis, keepdims=False)


def add_low(kept, received):
    return (kept.astype(jnp.float32) + received.astype(jnp.float32)).astype(jnp.bfloat16)


class RowSum:
    def __init__(self, term):
        place, count = lax.axis_index("dp"), lax.axis_size("dp")
        self.stages = [(1, (place // 4) % 2, 4), (0, place // 8, 8)]
        self.shape = (2, 2, term.shape[0] // 8, term.shape[1])
        self.kept = None
        self.received = lax.psum_scatter(
            term,
            "dp",
            scatter_dimension=0,
            axis_index_groups=[[one, one + 2] for one in range(count) if one % 4 < 2],
            tiled=True,
        )

    def step(self):
        if self.kept is None:
            self.part = self.received.reshape(self.shape)
        else:
            self.part = add_low(self.kept, self.received)
        self.received = None
        if self.stages:
            axis, own, bit = self.stages.pop(0)
            self.received = swap_dp(take(self.part, 1 - own, axis), bit)
            self.kept = take(self.part, own, axis)

    def finish(self):
        while self.received is not None:
            self.step()
        return self.part


def after(value, *sums):
    sums = [one for one in sums if one.received is not None]
    tied = lax.optimization_barrier((value, *[one.received for one in sums]))
    for one, received in zip(sums, tied[1:]):
        one.received = received
        one.step()
    return tied[0]


def place_bits():
    return (lax.axis_index("dp") % 2).reshape(1).astype(jnp.int32)


def turn_kernel(bits_ref, values_ref, mine_ref, theirs_ref):
    turned = values_ref[...].T
    block = turned.shape[0] // 16
    core = bits_ref[0]
    for at in range(8):
        first = turned[2 * at * block : (2 * at + 1) * block]
        second = turned[(2 * at + 1) * block : (2 * at + 2) * block]
        to = slice((at % 2 * 4 + at // 2) * block, (at % 2 * 4 + at // 2 + 1) * block)
        mine_ref[to, :] = jnp.where(core == 0, first, second)
        theirs_ref[to, :] = jnp.where(core == 0, second, first)


def turn_rows(values):
    frames, rows = values.shape
    step = min(frames, 512)
    grid_spec = pltpu.PrefetchScalarGridSpec(
        num_scalar_prefetch=1,
        grid=(frames // step,),
        in_specs=[pl.BlockSpec((step, rows), lambda n, s: (n, 0))],
        out_specs=[pl.BlockSpec((rows // 2, step), lambda n, s: (0, n))] * 2,
    )
    return pl.pallas_call(
        turn_kernel,
        name="turn_rows",
        grid_spec=grid_spec,
        out_shape=[jax.ShapeDtypeStruct((rows // 2, frames), jnp.bfloat16)] * 2,
        compiler_params=pltpu.CompilerParams(vmem_limit_bytes=VMEM_BYTES),
        cost_estimate=declared(0, 4 * frames * rows, 0),
    )(place_bits(), values)


def product_kernel(left_ref, right_ref, left2_ref, right2_ref, *out_refs):
    total = jnp.dot(left_ref[...], right_ref[...], preferred_element_type=jnp.float32)
    total += jnp.dot(left2_ref[...], right2_ref[...], preferred_element_type=jnp.float32)
    step, span = pl.program_id(0), pl.num_programs(0) // len(out_refs)
    for at, out_ref in enumerate(out_refs):

        @pl.when(step // span == at)
        def _():
            out_ref[...] = total.astype(jnp.bfloat16)


def products(lefts, rights, tile, name, pieces=1):
    rows, frames = lefts[0].shape
    width = rights[0].shape[1]
    span = width // tile // pieces

    def piece_at(piece):
        return lambda n: (0, jnp.clip(n - piece * span, 0, span - 1))

    left_spec = pl.BlockSpec((rows, frames), lambda n: (0, 0))
    right_spec = pl.BlockSpec((frames, tile), lambda n: (0, n))
    out = pl.pallas_call(
        product_kernel,
        name=name,
        grid=(width // tile,),
        in_specs=[left_spec, right_spec] * 2,
        out_specs=[pl.BlockSpec((rows, tile), piece_at(piece)) for piece in range(pieces)],
        out_shape=[jax.ShapeDtypeStruct((rows, width // pieces), jnp.bfloat16)] * pieces,
        compiler_params=pltpu.CompilerParams(vmem_limit_bytes=VMEM_BYTES),
        cost_estimate=declared(
            flops=4 * rows * frames * width,
            bytes_accessed=4 * rows * frames + 4 * frames * width + 2 * rows * width,
            transcendentals=0,
        ),
    )(lefts[0], rights[0], lefts[1], rights[1])
    return out if pieces > 1 else out[0]


def product_rows(left, right):
    return lax.dot_general(
        left, right, (((0,), (0,)), ((), ())), preferred_element_type=jnp.float32
    )


def turn(values, cosine, sine):
    lane = lax.broadcasted_iota(jnp.int32, values.shape, 1) % HEAD_DIM
    moved = jnp.where(
        lane < HEAD_DIM // 2,
        pltpu.roll(values, LANES - HEAD_DIM // 2, 1),
        pltpu.roll(values, HEAD_DIM // 2, 1),
    )
    return values * cosine + moved * sine


def lane_tables(positions):
    half_dim = HEAD_DIM // 2
    frequencies = ROPE_BASE ** (-2.0 * jnp.arange(half_dim, dtype=jnp.float32) / HEAD_DIM)
    angles = positions.astype(jnp.float32)[:, None] * frequencies[None, :]
    cosine, sine = jnp.cos(angles), jnp.sin(angles)
    return (
        jnp.concatenate([cosine] * 4, axis=1),
        jnp.concatenate([-sine, sine, -sine, sine], axis=1),
    )


def qkv_kernel(h_ref, w_ref, cosine_ref, sine_ref, out_ref):
    width = out_ref.shape[1]
    projected = jnp.dot(h_ref[...], w_ref[...], preferred_element_type=jnp.float32)
    step = pl.program_id(0)
    third = pl.num_programs(0) // 3

    @pl.when(step < 2 * third)
    def _():
        scale = jnp.where(step < third, HEAD_DIM ** (-0.5), 1.0)
        for at in range(0, width, LANES):
            turned = turn(projected[:, at : at + LANES], cosine_ref[...], sine_ref[...])
            out_ref[:, at : at + LANES] = (turned * scale).astype(jnp.bfloat16)

    @pl.when(step >= 2 * third)
    def _():
        out_ref[...] = projected.astype(jnp.bfloat16)


def project_qkv(normed, weight, start, width, cosine, sine):
    rows, depth = normed.shape
    tile = 384
    return pl.pallas_call(
        qkv_kernel,
        name="qkv_projection",
        grid=(width // tile,),
        in_specs=[
            pl.BlockSpec((rows, depth), lambda n: (0, 0)),
            pl.BlockSpec((depth, tile), lambda n: (0, start // tile + n)),
            pl.BlockSpec((rows, LANES), lambda n: (0, 0)),
            pl.BlockSpec((rows, LANES), lambda n: (0, 0)),
        ],
        out_specs=pl.BlockSpec((rows, tile), lambda n: (0, n)),
        out_shape=jax.ShapeDtypeStruct((rows, width), jnp.bfloat16),
        compiler_params=pltpu.CompilerParams(vmem_limit_bytes=VMEM_BYTES),
        cost_estimate=declared(
            flops=2 * rows * depth * width,
            bytes_accessed=2 * (rows * depth + depth * width + rows * width),
            transcendentals=0,
        ),
    )(normed, weight, cosine, sine)


def nt_dot(left, right):
    return lax.dot_general(
        left, right, (((1,), (1,)), ((), ())), preferred_element_type=jnp.float32
    )


def attend_kernel(masked, length_ref, q_ref, k_ref, v_ref, out_ref, lse_ref):
    for head in range(q_ref.shape[1] // HEAD_DIM):
        lanes = slice(head * HEAD_DIM, (head + 1) * HEAD_DIM)
        scores = nt_dot(q_ref[:, lanes], k_ref[:, lanes])
        if masked:
            key = lax.broadcasted_iota(jnp.int32, scores.shape, 1)
            scores = jnp.where(key < length_ref[0], scores, MASKED)
        row_max = jnp.max(scores, axis=1, keepdims=True)
        exponent = jnp.exp2(scores * LOG2E - row_max * LOG2E)
        total = jnp.sum(exponent, axis=1, keepdims=True)
        mixed = jnp.dot(
            exponent.astype(jnp.bfloat16), v_ref[:, lanes], preferred_element_type=jnp.float32
        )
        out_ref[:, lanes] = (mixed / total).astype(jnp.bfloat16)
        lse_ref[:, lanes] = jnp.broadcast_to(
            row_max * LOG2E + jnp.log2(total), (row_max.shape[0], HEAD_DIM)
        )


def attend(length, queries, keys, values, width, columns, masked, name, span, block):
    rows, key_rows = queries.shape[0], keys.shape[0]
    pairs = width // span
    q_at, k_at, v_at = columns
    grid_spec = pltpu.PrefetchScalarGridSpec(
        num_scalar_prefetch=1,
        grid=(pairs, rows // block),
        in_specs=[
            pl.BlockSpec((block, span), lambda p, i, s: (i, q_at + p)),
            pl.BlockSpec((key_rows, span), lambda p, i, s: (0, k_at + p)),
            pl.BlockSpec((key_rows, span), lambda p, i, s: (0, v_at + p)),
        ],
        out_specs=[
            pl.BlockSpec((block, span), lambda p, i, s: (i, p)),
            pl.BlockSpec((block, span), lambda p, i, s: (i, p)),
        ],
    )
    return pl.pallas_call(
        functools.partial(attend_kernel, masked),
        name=name,
        grid_spec=grid_spec,
        out_shape=[
            jax.ShapeDtypeStruct((rows, width), jnp.bfloat16),
            jax.ShapeDtypeStruct((rows, width), jnp.float32),
        ],
        compiler_params=pltpu.CompilerParams(vmem_limit_bytes=VMEM_BYTES),
        cost_estimate=declared(
            flops=16 * rows * key_rows * width,
            bytes_accessed=8 * rows * width,
            transcendentals=rows * key_rows * width // HEAD_DIM,
        ),
    )(length, queries, keys, values)


def attend_back_kernel(
    masked,
    turned,
    length_ref,
    q_ref,
    k_ref,
    v_ref,
    grad_ref,
    out_ref,
    lse_ref,
    *rest,
):
    if turned:
        cosq_ref, sinq_ref, cosk_ref, sink_ref = rest[:4]
        rest = rest[4:]
    dq_ref, dk_ref, dv_ref, dk_sum, dv_sum = rest
    step, steps = pl.program_id(1), pl.num_programs(1)

    @pl.when(step == 0)
    def _():
        dk_sum[...] = jnp.zeros_like(dk_sum)
        dv_sum[...] = jnp.zeros_like(dv_sum)

    lse_rows = lse_ref[...].T
    delta_rows = (grad_ref[...].astype(jnp.float32) * out_ref[...].astype(jnp.float32)).T
    dq_parts = []
    for head in range(q_ref.shape[1] // HEAD_DIM):
        lanes = slice(head * HEAD_DIM, (head + 1) * HEAD_DIM)
        query, key, value = q_ref[:, lanes], k_ref[:, lanes], v_ref[:, lanes]
        grad = grad_ref[:, lanes]
        scores = nt_dot(key, query)
        if masked:
            index = lax.broadcasted_iota(jnp.int32, scores.shape, 0)
            scores = jnp.where(index < length_ref[0], scores, MASKED)
        lse = lse_rows[head * HEAD_DIM : head * HEAD_DIM + 1, :]
        delta = jnp.sum(delta_rows[lanes, :], axis=0, keepdims=True)
        weight = jnp.exp2(scores * LOG2E - lse)
        dv_sum[:, lanes] += jnp.dot(
            weight.astype(jnp.bfloat16), grad, preferred_element_type=jnp.float32
        )
        weight_grad = nt_dot(value, grad)
        score_grad = (weight * (weight_grad - delta)).astype(jnp.bfloat16)
        dk_sum[:, lanes] += jnp.dot(score_grad, query, preferred_element_type=jnp.float32)
        dq_parts.append(product_rows(score_grad, key) * HEAD_DIM ** (-0.5))
    dq = jnp.concatenate(dq_parts, axis=1).astype(jnp.bfloat16)
    if turned:
        dq = turn(dq.astype(jnp.float32), cosq_ref[...], -sinq_ref[...]).astype(jnp.bfloat16)
    dq_ref[...] = dq

    @pl.when(step == steps - 1)
    def _():
        dk = dk_sum[...].astype(jnp.bfloat16)
        if turned:
            dk = turn(dk.astype(jnp.float32), cosk_ref[...], -sink_ref[...]).astype(jnp.bfloat16)
        dk_ref[...] = dk
        dv_ref[...] = dv_sum[...].astype(jnp.bfloat16)


def attend_back(
    length,
    queries,
    keys,
    values,
    columns,
    grad_at,
    width,
    grad,
    outputs,
    lse,
    tables,
    masked,
    name,
    span,
    block,
):
    rows, key_rows = queries.shape[0], keys.shape[0]
    pairs = width // span
    q_at, k_at, v_at = columns
    by_query = pl.BlockSpec((block, span), lambda p, i, s: (i, p))
    by_grad = pl.BlockSpec((block, span), lambda p, i, s: (i, grad_at + p))
    by_key = pl.BlockSpec((key_rows, span), lambda p, i, s: (0, p))
    in_specs = [
        pl.BlockSpec((block, span), lambda p, i, s: (i, q_at + p)),
        pl.BlockSpec((key_rows, span), lambda p, i, s: (0, k_at + p)),
        pl.BlockSpec((key_rows, span), lambda p, i, s: (0, v_at + p)),
        by_grad,
        by_grad,
        by_grad,
    ]
    operands = [queries, keys, values, grad, outputs, lse]
    if tables is not None:
        cosine, sine = tables
        in_specs += [pl.BlockSpec((block, LANES), lambda p, i, s: (i, 0))] * 2
        in_specs += [pl.BlockSpec((key_rows, LANES), lambda p, i, s: (0, 0))] * 2
        operands += [cosine, sine, cosine, sine]
    grid_spec = pltpu.PrefetchScalarGridSpec(
        num_scalar_prefetch=1,
        grid=(pairs, rows // block),
        in_specs=in_specs,
        out_specs=[by_query, by_key, by_key],
        scratch_shapes=[pltpu.VMEM((key_rows, span), jnp.float32)] * 2,
    )
    return pl.pallas_call(
        functools.partial(attend_back_kernel, masked, tables is not None),
        name=name,
        grid_spec=grid_spec,
        out_shape=[
            jax.ShapeDtypeStruct((rows, width), jnp.bfloat16),
            jax.ShapeDtypeStruct((key_rows, width), jnp.bfloat16),
            jax.ShapeDtypeStruct((key_rows, width), jnp.bfloat16),
        ],
        compiler_params=pltpu.CompilerParams(vmem_limit_bytes=VMEM_BYTES),
        cost_estimate=declared(
            flops=40 * rows * key_rows * width,
            bytes_accessed=20 * rows * width,
            transcendentals=rows * key_rows * width // HEAD_DIM,
        ),
    )(length, *operands)


def feed_kernel(bits_ref, h_ref, cot_ref, in_ref, down_ref, *rest):
    mine_ref, theirs_ref, dgu_ref, out_ref, down, total = rest[-6:]
    step, steps = pl.program_id(0), pl.num_programs(0)
    depth, tile = h_ref.shape[1], down.shape[0]
    piece = down_ref.shape[0] // 2
    for at in range(4):
        place, part = at // 2, at % 2
        down[at * piece : (at + 1) * piece, :] = down_ref[
            place * piece : (place + 1) * piece, part * depth : (part + 1) * depth
        ]
    @pl.when(step == 0)
    def _():
        total[...] = jnp.zeros_like(total)

    chunk = h_ref.shape[0] // 2
    for at in range(2):
        rows = slice(at * chunk, (at + 1) * chunk)
        gate_up = jnp.dot(h_ref[rows, :], in_ref[...], preferred_element_type=jnp.float32)
        grad = nt_dot(cot_ref[rows, :], down[...])
        gate, up = gate_up[:, :tile], gate_up[:, tile:]
        sigmoid = jax.nn.sigmoid(gate)
        silu = gate * sigmoid
        hidden = (silu * up).astype(jnp.bfloat16)
        turned = hidden.T
        first, second = turned[: tile // 2], turned[tile // 2 :]
        mine_ref[:, rows] = jnp.where(bits_ref[0] == 0, first, second)
        theirs_ref[:, rows] = jnp.where(bits_ref[0] == 0, second, first)
        dgu_ref[rows, tile:] = (grad * silu).astype(jnp.bfloat16)
        dgu_ref[rows, :tile] = (
            grad * up * sigmoid * (1.0 + gate * (1.0 - sigmoid))
        ).astype(jnp.bfloat16)
        total[rows, :] += jnp.dot(hidden, down[...], preferred_element_type=jnp.float32)

    @pl.when(step == steps - 1)
    def _():
        out_ref[...] = total[...].astype(out_ref.dtype)


def feed(normed, cotangent, weights, half, earlier):
    rows, depth = normed.shape
    units = FF // 2
    steps = depth // 192
    tile = units // steps
    operands = [normed, cotangent, weights, weights]
    in_specs = [
        pl.BlockSpec((rows, depth), lambda n, s: (0, 0)),
        pl.BlockSpec((rows, depth), lambda n, s: (0, 0)),
        pl.BlockSpec((depth, 2 * tile), lambda n, s: (0, n)),
        pl.BlockSpec((depth // steps, 2 * depth), lambda n, s: (n, 2)),
    ]
    aliases = {}
    if earlier is not None:
        in_specs += [pl.BlockSpec(memory_space=pl.ANY)] * 3
        aliases = {5: 0, 6: 1, 7: 2}
        operands += list(earlier)

    def turned_at(n, s):
        return (n % 2 * 4 + n // 2, half)

    grid_spec = pltpu.PrefetchScalarGridSpec(
        num_scalar_prefetch=1,
        grid=(steps,),
        in_specs=in_specs,
        out_specs=[
            pl.BlockSpec((tile // 2, rows), turned_at),
            pl.BlockSpec((tile // 2, rows), turned_at),
            pl.BlockSpec((rows, 2 * tile), lambda n, s: (half, n)),
            pl.BlockSpec((rows, depth), lambda n, s: (0, 0)),
        ],
        scratch_shapes=[
            pltpu.VMEM((tile, depth), jnp.bfloat16),
            pltpu.VMEM((rows, depth), jnp.float32),
        ],
    )
    return pl.pallas_call(
        feed_kernel,
        name="feed_forward",
        grid_spec=grid_spec,
        out_shape=[
            jax.ShapeDtypeStruct((units // 2, 2 * rows), jnp.bfloat16),
            jax.ShapeDtypeStruct((units // 2, 2 * rows), jnp.bfloat16),
            jax.ShapeDtypeStruct((2 * rows, 2 * units), jnp.bfloat16),
            jax.ShapeDtypeStruct((rows, depth), jnp.bfloat16 if half else jnp.float32),
        ],
        input_output_aliases=aliases,
        compiler_params=pltpu.CompilerParams(vmem_limit_bytes=VMEM_BYTES),
        cost_estimate=declared(
            flops=8 * rows * depth * units,
            bytes_accessed=6 * depth * units + 6 * rows * units + 8 * rows * depth,
            transcendentals=rows * units,
        ),
    )(place_bits(), *operands)


def back_kernel(left_ref, right_ref, out_ref, total):
    step, steps = pl.program_id(0), pl.num_programs(0)

    @pl.when(step == 0)
    def _():
        total[...] = jnp.zeros_like(total)

    total[...] += nt_dot(left_ref[...], right_ref[...])

    @pl.when(step == steps - 1)
    def _():
        out_ref[...] = total[...].astype(out_ref.dtype)


def times_turned(left, right, at, rows, start, width, kind, name):
    depth = right.shape[0]
    tile = 768
    return pl.pallas_call(
        back_kernel,
        name=name,
        grid=(width // tile,),
        in_specs=[
            pl.BlockSpec((rows, tile), lambda n: (at, n)),
            pl.BlockSpec((depth, tile), lambda n: (0, start // tile + n)),
        ],
        out_specs=pl.BlockSpec((rows, depth), lambda n: (0, 0)),
        out_shape=jax.ShapeDtypeStruct((rows, depth), kind),
        scratch_shapes=[pltpu.VMEM((rows, depth), jnp.float32)],
        compiler_params=pltpu.CompilerParams(vmem_limit_bytes=VMEM_BYTES),
        cost_estimate=declared(
            flops=2 * rows * depth * width,
            bytes_accessed=2 * rows * width + 2 * depth * width + 4 * rows * depth,
            transcendentals=0,
        ),
    )(left, right)


def norm_back_into(total, x_ref, gain_ref, residual_ref, sum_ref, low_ref, term_ref):
    chunk = 128
    term = jnp.zeros(term_ref.shape, jnp.float32)
    for at in range(0, total.shape[0], chunk):
        rows = slice(at, at + chunk)
        grad = total[rows, :]
        values = x_ref[rows, :]
        centred = values - jnp.mean(values, axis=1, keepdims=True)
        inverse = lax.rsqrt(jnp.mean(centred * centred, axis=1, keepdims=True) + EPSILON)
        scaled = centred * inverse
        term += jnp.sum(grad * scaled, axis=0, keepdims=True)
        inner = grad * gain_ref[...]
        back = inverse * (
            inner
            - jnp.mean(inner, axis=1, keepdims=True)
            - scaled * jnp.mean(inner * scaled, axis=1, keepdims=True)
        )
        summed = residual_ref[rows, :].astype(jnp.float32) + back
        sum_ref[rows, :] = summed
        low_ref[rows, :] = summed.astype(jnp.bfloat16)
    term_ref[...] = term


def feed_back_kernel(
    left_ref, right_ref, other_ref, x_ref, gain_ref, residual_ref, sum_ref, low_ref, term_ref, total
):
    step, steps = pl.program_id(0), pl.num_programs(0)

    @pl.when(step == 0)
    def _():
        total[...] = other_ref[...].astype(jnp.float32)

    total[...] += nt_dot(left_ref[...], right_ref[...])

    @pl.when(step == steps - 1)
    def _():
        norm_back_into(total, x_ref, gain_ref, residual_ref, sum_ref, low_ref, term_ref)


def feed_back(left, right, other, values, gain, residual):
    rows, depth = values.shape
    tile = 768
    whole = pl.BlockSpec((rows, depth), lambda n: (0, 0))
    line = pl.BlockSpec((1, depth), lambda n: (0, 0))
    return pl.pallas_call(
        feed_back_kernel,
        name="h3_back_norm",
        grid=(FF // tile,),
        in_specs=[
            pl.BlockSpec((rows, tile), lambda n: (0, n)),
            pl.BlockSpec((depth, tile), lambda n: (0, n)),
            whole,
            whole,
            line,
            whole,
        ],
        out_specs=[whole, whole, line],
        out_shape=[
            jax.ShapeDtypeStruct((rows, depth), jnp.float32),
            jax.ShapeDtypeStruct((rows, depth), jnp.bfloat16),
            jax.ShapeDtypeStruct((1, depth), jnp.float32),
        ],
        scratch_shapes=[pltpu.VMEM((rows, depth), jnp.float32)],
        compiler_params=pltpu.CompilerParams(vmem_limit_bytes=VMEM_BYTES),
        cost_estimate=declared(2 * rows * depth * FF, 2 * depth * FF, 0),
    )(left, right, other, values, gain, residual)


def cross_back_kernel(
    length_ref,
    low_ref,
    out_weight_ref,
    q_weight_ref,
    q_ref,
    k_ref,
    v_ref,
    out_ref,
    lse_ref,
    x_ref,
    gain_ref,
    residual_ref,
    dq_ref,
    dk_ref,
    dv_ref,
    sum_ref,
    new_low_ref,
    term_ref,
    total,
):
    step, steps = pl.program_id(0), pl.num_programs(0)
    grad_all = nt_dot(low_ref[...], out_weight_ref[...])
    lse_rows = lse_ref[...].T
    delta_rows = (grad_all * out_ref[...].astype(jnp.float32)).T
    grad_all = grad_all.astype(jnp.bfloat16)
    for head in range(q_ref.shape[1] // HEAD_DIM):
        lanes = slice(head * HEAD_DIM, (head + 1) * HEAD_DIM)
        query, key, value = q_ref[:, lanes], k_ref[:, lanes], v_ref[:, lanes]
        grad = grad_all[:, lanes]
        scores = nt_dot(key, query)
        index = lax.broadcasted_iota(jnp.int32, scores.shape, 0)
        scores = jnp.where(index < length_ref[0], scores, MASKED)
        lse = lse_rows[head * HEAD_DIM : head * HEAD_DIM + 1, :]
        delta = jnp.sum(delta_rows[lanes, :], axis=0, keepdims=True)
        weight = jnp.exp2(scores * LOG2E - lse)
        dv = jnp.dot(weight.astype(jnp.bfloat16), grad, preferred_element_type=jnp.float32)
        dv_ref[:, lanes] = dv.astype(jnp.bfloat16)
        score_grad = (weight * (nt_dot(value, grad) - delta)).astype(jnp.bfloat16)
        dk = jnp.dot(score_grad, query, preferred_element_type=jnp.float32)
        dk_ref[:, lanes] = dk.astype(jnp.bfloat16)
        dq = product_rows(score_grad, key) * HEAD_DIM ** (-0.5)
        dq_ref[:, lanes] = dq.astype(jnp.bfloat16)
    back = nt_dot(dq_ref[...], q_weight_ref[...])

    @pl.when(step == 0)
    def _():
        total[...] = back

    @pl.when(step > 0)
    def _():
        total[...] += back

    @pl.when(step == steps - 1)
    def _():
        norm_back_into(total, x_ref, gain_ref, residual_ref, sum_ref, new_low_ref, term_ref)


def cross_back(length, low, weights, query, key, value, outputs, lse, values, gain, residual):
    rows, depth = values.shape
    key_rows = key.shape[0]
    tile = 384
    steps = depth // tile
    whole = pl.BlockSpec((rows, depth), lambda n, s: (0, 0))
    line = pl.BlockSpec((1, depth), lambda n, s: (0, 0))
    by_query = pl.BlockSpec((rows, tile), lambda n, s: (0, n))
    by_key = pl.BlockSpec((key_rows, tile), lambda n, s: (0, n))
    grid_spec = pltpu.PrefetchScalarGridSpec(
        num_scalar_prefetch=1,
        grid=(steps,),
        in_specs=[
            whole,
            pl.BlockSpec((tile, depth), lambda n, s: (n, 2)),
            pl.BlockSpec((depth, tile), lambda n, s: (0, steps + n)),
            by_query,
            by_key,
            by_key,
            by_query,
            by_query,
            whole,
            line,
            whole,
        ],
        out_specs=[by_query, by_key, by_key, whole, whole, line],
        scratch_shapes=[pltpu.VMEM((rows, depth), jnp.float32)],
    )
    return pl.pallas_call(
        cross_back_kernel,
        name="cross_back",
        grid_spec=grid_spec,
        out_shape=[
            jax.ShapeDtypeStruct((rows, depth), jnp.bfloat16),
            jax.ShapeDtypeStruct((key_rows, depth), jnp.bfloat16),
            jax.ShapeDtypeStruct((key_rows, depth), jnp.bfloat16),
            jax.ShapeDtypeStruct((rows, depth), jnp.float32),
            jax.ShapeDtypeStruct((rows, depth), jnp.bfloat16),
            jax.ShapeDtypeStruct((1, depth), jnp.float32),
        ],
        compiler_params=pltpu.CompilerParams(vmem_limit_bytes=VMEM_BYTES),
        cost_estimate=declared(4 * rows * depth * depth, 8 * depth * depth, 0),
    )(length, low, weights, weights, query, key, value, outputs, lse, values, gain, residual)


def split_back_kernel(side_ref, left_ref, right_ref, kept_ref, sent_ref):
    half = kept_ref.shape[1]
    lower = nt_dot(left_ref[...], right_ref[:half, :]).astype(jnp.bfloat16)
    upper = nt_dot(left_ref[...], right_ref[half:, :]).astype(jnp.bfloat16)
    kept_ref[...] = jnp.where(side_ref[0] == 0, lower, upper)
    sent_ref[...] = jnp.where(side_ref[0] == 0, upper, lower)


def split_back(side, left, weights):
    rows, depth = left.shape
    return pl.pallas_call(
        split_back_kernel,
        name="attention_grad",
        grid=(1,),
        in_specs=[
            pl.BlockSpec(memory_space=pltpu.SMEM),
            pl.BlockSpec((rows, depth), lambda n: (0, 0)),
            pl.BlockSpec((depth, depth), lambda n: (0, 0)),
        ],
        out_specs=[pl.BlockSpec((rows, depth // 2), lambda n: (0, 0))] * 2,
        out_shape=[jax.ShapeDtypeStruct((rows, depth // 2), jnp.bfloat16)] * 2,
        compiler_params=pltpu.CompilerParams(vmem_limit_bytes=VMEM_BYTES),
        cost_estimate=declared(2 * rows * depth * depth, 2 * depth * depth, 0),
    )(side.reshape(1).astype(jnp.int32), left, weights)


def in_grad_kernel(side_ref, *refs):
    out_ref = refs[-1]
    unit = refs[0].shape[1] // 8
    for part in range(2):
        mine_ref, theirs_ref = refs[2 * part], refs[2 * part + 1]
        for at in range(8):
            mine = mine_ref[:, at * unit : (at + 1) * unit].astype(jnp.float32)
            theirs = theirs_ref[:, at * unit : (at + 1) * unit].astype(jnp.float32)
            tile, gate_or_up = part * 4 + at // 2, at % 2
            to = (gate_or_up * 8 + tile) * 2 * unit
            out_ref[:, to : to + unit] = jnp.where(side_ref[0] == 0, mine, theirs)
            out_ref[:, to + unit : to + 2 * unit] = jnp.where(side_ref[0] == 0, theirs, mine)


def assemble_in_grad(side, parts):
    rows, width = parts[0].shape
    whole = pl.BlockSpec(memory_space=pltpu.VMEM)
    return pl.pallas_call(
        in_grad_kernel,
        name="in_grad_rows",
        in_specs=[pl.BlockSpec(memory_space=pltpu.SMEM)] + [whole] * 4,
        out_specs=whole,
        out_shape=jax.ShapeDtypeStruct((rows, 4 * width), jnp.float32),
        compiler_params=pltpu.CompilerParams(vmem_limit_bytes=VMEM_BYTES),
        cost_estimate=declared(0, 16 * rows * width, 0),
    )(side.reshape(1).astype(jnp.int32), *parts)


def paired_body(
    tokens, context, lengths, norm_gains, w_qkv, w_out, w_q2, w_kv2, w_out2, w_in, w_down, cotangent
):
    place, side = lax.axis_index("dp"), lax.axis_index("head")
    core = place % 2
    on_left = side == 0
    own = tokens[0]
    frames = own.shape[0]
    rows = w_qkv.shape[0]
    half = D // 2
    units = w_down.shape[0]

    def ordered(mine, theirs):
        return jnp.where(on_left, mine, theirs), jnp.where(on_left, theirs, mine)

    qkv_half = take(w_qkv.reshape(rows, 3, 2, half), side, 2).reshape(rows, 3 * half)
    kv2_rows = jnp.concatenate([w_kv2[:, :D], w_kv2[:, D:]], axis=0)
    full_first = lax.all_gather(
        jnp.concatenate([w_out, w_q2, w_out2, kv2_rows, qkv_half], axis=1),
        "dp",
        axis=0,
        tiled=True,
    )
    full_out, full_q2, full_out2, full_kv2 = [
        full_first[:, one * D : (one + 1) * D] for one in range(4)
    ]
    full_kv2 = full_kv2.reshape(rows // 6, 2, rows // 2, D)
    key_weight, value_weight = full_kv2[:, 0].reshape(D // 2, D), full_kv2[:, 1].reshape(D // 2, D)
    in_half = take(w_in.reshape(rows, 2, 8, 2, units), side, 3)
    in_half = jnp.swapaxes(in_half, 1, 2).reshape(rows, FF)
    down_parts = w_down.reshape(2, units // 2, D)
    down_received = swap_dp(take(down_parts, 1 - core, 0), 1)
    down_half = jnp.where(core == side, take(down_parts, core, 0), down_received)
    full_feed = lax.all_gather(
        jnp.concatenate([in_half, down_half[:rows], down_half[rows:]], axis=1),
        "dp",
        axis=0,
        tiled=True,
    )
    full_in = full_feed[:, :FF]

    both_tokens = jnp.concatenate([own, swap_head(own)], axis=0).astype(jnp.float32)
    own_cot, other_cot = cotangent[0], swap_head(cotangent[0])
    both_cot = jnp.concatenate([own_cot, other_cot], axis=0)
    frame = jnp.arange(frames, dtype=jnp.int32)
    tables = lane_tables(
        jnp.concatenate([side * frames + frame, (1 - side) * frames + frame])
    )
    normed1 = normalize(both_tokens, norm_gains[0])[0].astype(jnp.bfloat16)
    inputs = own.astype(jnp.float32)
    norm1_saved = normalize(inputs, norm_gains[0])[1]
    qkv = project_qkv(normed1, full_first, 4 * D, 3 * half, *tables)
    no_length = jnp.zeros((1,), jnp.int32)
    pairs = half // LANES
    self_columns = (0, pairs, 2 * pairs)
    attended, self_lse = attend(
        no_length, qkv, qkv, qkv, half, self_columns, False, "self_attention", LANES, 512
    )
    attended_other = swap_head(attended[frames:])
    attended_frames = jnp.concatenate(ordered(attended[:frames], attended_other), axis=1)
    first = inputs + jnp.dot(attended_frames, full_out, preferred_element_type=jnp.float32)

    normed2, norm2_saved = normalize(first, norm_gains[1])
    normed2 = normed2.astype(jnp.bfloat16)
    query2 = jnp.dot(normed2, full_q2, preferred_element_type=jnp.float32)
    query2 = (query2.astype(jnp.bfloat16) * HEAD_DIM ** (-0.5)).astype(jnp.bfloat16)
    key2, value2 = [
        jnp.dot(context[0], weight, preferred_element_type=jnp.float32).astype(jnp.bfloat16)
        for weight in (key_weight, value_weight)
    ]
    crossed, cross_lse = attend(
        lengths, query2, key2, value2, D, (0, 0, 0), True, "cross_attention", 3 * LANES, frames
    )
    second = first + jnp.dot(crossed, full_out2, preferred_element_type=jnp.float32)

    def left_pair(values):
        mine, theirs = turn_rows(values)
        return mine, swap_dp(theirs, 1)

    lefts1 = left_pair(normed1)
    lefts_out = left_pair(attended_frames)
    lefts2 = left_pair(normed2)
    lefts_cross = left_pair(crossed)
    lefts_context = left_pair(context[0])
    cots = both_cot, swap_dp(both_cot, 1)

    normed3, norm3_saved = normalize(second, norm_gains[2])
    normed3 = normed3.astype(jnp.bfloat16)
    other3 = swap_head(normed3)
    *fed, own_out = feed(normed3, own_cot, full_feed, 0, None)
    fed, lefts1, lefts_out, lefts2, lefts_cross, lefts_context, cots = in_order(
        fed, lefts1, lefts_out, lefts2, lefts_cross, lefts_context, cots
    )
    hidden, hidden_theirs, dgu, other_out = feed(other3, other_cot, full_feed, 1, fed)
    lefts3 = left_pair(jnp.concatenate([normed3, other3], axis=0))
    hidden, dgu = in_order(hidden, dgu)
    hiddens = hidden, swap_dp(hidden_theirs, 1)
    dgus = dgu, swap_dp(dgu, 1)
    sent3 = times_turned(dgu, full_feed, 1, frames, 0, FF, jnp.bfloat16, "h3_back")
    hiddens, sent3 = in_order(hiddens, sent3)
    received3 = swap_head(sent3)
    down_term = products(hiddens, cots, 512, "down_grad")
    dgus, down_term = in_order(dgus, down_term)
    down_sum = RowSum(down_term)
    in_terms = products(lefts3, dgus, 512, "in_grad", 2)
    in_terms, dgu = in_order(in_terms, dgu)
    residual3, cross_low, gain_three = feed_back(
        dgu, full_feed, received3, second, norm_gains[2:], own_cot
    )
    cross_low, in_terms = in_order(cross_low, in_terms)
    in_sums = [RowSum(one) for one in in_terms]
    cross_low = after(cross_low, down_sum)
    output = (second + own_out + swap_head(other_out).astype(jnp.float32)).astype(jnp.bfloat16)

    query2_grad, key2_grad, value2_grad, residual2, self_low, gain_two = cross_back(
        lengths,
        cross_low,
        full_first,
        query2,
        key2,
        value2,
        crossed,
        cross_lse,
        first,
        norm_gains[1:2],
        residual3,
    )
    grad_kept, grad_sent = split_back(side, self_low, full_first)
    grad_kept = after(grad_kept, down_sum)
    grad_received = swap_head(grad_sent)
    kv2_grad = jnp.concatenate([key2_grad, value2_grad], axis=1)

    def square(lefts, right, name):
        return products(lefts, (right, swap_dp(right, 1)), 512, name)

    def meet(lower, upper):
        return (
            jnp.where(on_left, lower, upper),
            swap_head(jnp.where(on_left, upper, lower)),
        )

    def met(terms):
        return RowSum(add_low(*terms))

    query2_grad, cross_low, kv2_grad, grad_kept = in_order(
        query2_grad, cross_low, kv2_grad, grad_kept
    )
    out2_terms = square(lefts_cross, cross_low, "out2_grad")
    q2_terms = square(lefts2, query2_grad, "q2_grad")
    out2_terms, q2_terms, self_low, kv2_grad = in_order(out2_terms, q2_terms, self_low, kv2_grad)
    cross_terms = meet(out2_terms, q2_terms)
    kv2_terms = square(lefts_context, kv2_grad, "kv2_grad").reshape(8, rows // 2, 2, D)
    kv2_terms = jnp.swapaxes(kv2_terms, 1, 2).reshape(8 * rows, D)
    out_terms = square(lefts_out, self_low, "out_grad")
    kv2_terms, out_terms, grad_kept = in_order(kv2_terms, out_terms, grad_kept)
    self_terms = meet(out_terms, kv2_terms)
    heads_grad = jnp.concatenate([grad_kept, grad_received], axis=0)
    heads_grad = after(heads_grad, down_sum, in_sums[0])

    def heads_back(part):
        columns = [column + part * (pairs // 2) for column in self_columns]
        return attend_back(
            no_length,
            qkv,
            qkv,
            qkv,
            columns,
            part * (pairs // 2),
            half // 2,
            heads_grad,
            attended,
            self_lse,
            tables,
            False,
            "self_attention_back",
            LANES,
            256,
        )

    early = heads_back(0)
    early = after(early, in_sums[0], in_sums[1])
    early, cross_terms = in_order(early, cross_terms)
    cross_sum = met(cross_terms)
    early_columns = jnp.concatenate(early, axis=1)
    early_both = early_columns, swap_dp(early_columns, 1)
    early_terms = products(lefts1, early_both, 384, "qkv_grad")
    heads_grad, early_terms = in_order(heads_grad, early_terms)
    qkv_sums = [RowSum(early_terms)]
    late = heads_back(1)
    late = after(late, *in_sums, cross_sum)
    late, self_terms = in_order(late, self_terms)
    self_sum = met(self_terms)
    late_columns = jnp.concatenate(late, axis=1)
    late_both = late_columns, swap_dp(late_columns, 1)
    qkv_grad = jnp.concatenate(
        [
            one[:, at : at + half // 2]
            for at in range(0, 3 * half // 2, half // 2)
            for one in (early_columns, late_columns)
        ],
        axis=1,
    )
    sent1 = times_turned(qkv_grad, full_first, 1, frames, 4 * D, 3 * half, jnp.bfloat16, "h1_back")
    sent1, late_both = in_order(sent1, late_both)
    received1 = swap_head(sent1)
    late_terms = products(lefts1, late_both, 384, "qkv_grad")
    qkv_grad, late_terms = in_order(qkv_grad, late_terms)
    qkv_sums.append(RowSum(late_terms))
    own1 = times_turned(qkv_grad, full_first, 0, frames, 4 * D, 3 * half, jnp.float32, "h1_back")
    own1, received1 = after((own1, received1), cross_sum, self_sum, *qkv_sums, *in_sums)
    normed_grad = own1 + received1.astype(jnp.float32)
    normed_back, gain_one = normalize_back(normed_grad, norm_gains[0], norm1_saved)
    input_grad = residual2 + normed_back

    gains = jnp.concatenate([gain_one[None], gain_two, gain_three], axis=0)
    for bit in (1, 2, 4, 8):
        gains = gains + swap_dp(gains, bit)
    gains = gains + swap_head(gains)

    gains = after(gains, *qkv_sums, self_sum, cross_sum)
    gains = after(gains, *qkv_sums, self_sum)
    def joined(mine):
        lower, upper = ordered(mine, swap_head(mine))
        return jnp.stack([lower, upper], axis=-2)

    down_rows = down_sum.finish()
    down_other = swap_dp(down_rows, 1)
    down_block = jnp.concatenate(
        [
            jnp.where(core == 0, down_rows, down_other),
            jnp.where(core == 0, down_other, down_rows),
        ],
        axis=0,
    )
    crossing = [
        (2 * one + (one % 2), 2 * one + 1 - (one % 2)) for one in range(lax.axis_size("dp"))
    ]
    down_crossed = lax.ppermute(down_block, ("dp", "head"), crossing)
    down_out = jnp.where(core == side, down_block, down_crossed).astype(jnp.float32)
    in_parts = []
    for one in in_sums:
        mine = one.finish()
        in_parts += [mine, swap_head(mine)]
    in_out = assemble_in_grad(side, in_parts)
    qkv_out = jnp.concatenate([one.finish().reshape(rows, 3, half // 2) for one in qkv_sums], axis=2)
    qkv_out = joined(qkv_out).reshape(rows, 3 * D)
    cross_rows = joined(cross_sum.finish()).astype(jnp.float32)
    self_rows = joined(self_sum.finish()).astype(jnp.float32)
    kv2_out = jnp.swapaxes(self_rows[:, 1].reshape(2, rows // 2, D), 0, 1).reshape(rows // 2, 2 * D)
    return (
        output[None],
        input_grad[None],
        gains,
        qkv_out.astype(jnp.float32),
        self_rows[:, 0],
        cross_rows[:, 1],
        kv2_out,
        cross_rows[:, 0],
        in_out,
        down_out,
    )


def body(*arrays):
    if lax.axis_size("dp") == 16 and lax.axis_size("head") == 2 and arrays[0].shape[0] == 1:
        return paired_body(*arrays)
    return general_body(*arrays)


def solution(mesh):
    placed = (
        P("dp", "head", None),
        P("dp", None, None),
        P("dp"),
        P(),
        P("dp", None),
        P("dp", None),
        P("dp", None),
        P("dp", None),
        P("dp", None),
        P("dp", None),
        P("dp", None),
        P("dp", "head", None),
    )
    return jax.shard_map(
        body,
        mesh=mesh,
        in_specs=placed,
        out_specs=(
            P("dp", "head", None),
            P("dp", "head", None),
            P(),
            P("dp", None),
            P("dp", None),
            P("dp", None),
            P("dp", None),
            P("dp", None),
            P("dp", None),
            P("dp", None),
        ),
        check_vma=False,
    )
```

```python
import functools

import jax
import jax.numpy as jnp
from jax import lax
from jax.experimental import pallas as pl
from jax.experimental.pallas import tpu as pltpu
from jax.sharding import PartitionSpec as P

D = 1536
HEADS = 24
HEAD_DIM = 64
FF = 6144
CTX = 768


EPSILON = 1e-05
MASKED = -1000000000.0


def normalize(values, gain_row):
    centred = values - jnp.mean(values, axis=-1, keepdims=True)
    inverse = lax.rsqrt(jnp.mean(centred * centred, axis=-1, keepdims=True) + EPSILON)
    scaled = centred * inverse
    return (scaled * gain_row, (scaled, inverse))


def normalize_back(grad_out, gain_row, saved):
    scaled, inverse = saved
    gain_term = jnp.sum(grad_out * scaled, axis=0)
    inner = grad_out * gain_row
    result = inverse * (
        inner
        - jnp.mean(inner, axis=-1, keepdims=True)
        - scaled * jnp.mean(inner * scaled, axis=-1, keepdims=True)
    )
    return (result, gain_term)


def rotary_tables(first_frame, frame_rows):
    half_dim = HEAD_DIM // 2
    frequencies = 10000.0 ** (-2.0 * jnp.arange(half_dim, dtype=jnp.float32) / HEAD_DIM)
    positions = (first_frame + jnp.arange(frame_rows, dtype=jnp.int32)).astype(jnp.float32)
    angles = positions[:, None] * frequencies[None, :]
    return (jnp.cos(angles)[:, None, None, :], jnp.sin(angles)[:, None, None, :])


def rotate(rotated_in, cosine_table, sine_table):
    half_dim = rotated_in.shape[-1] // 2
    first_half = rotated_in[..., :half_dim]
    second_half = rotated_in[..., half_dim:]
    return jnp.concatenate(
        [
            first_half * cosine_table - second_half * sine_table,
            second_half * cosine_table + first_half * sine_table,
        ],
        axis=-1,
    )


def times_transposed(left, weight):
    return lax.dot_general(
        left, weight, (((1,), (1,)), ((), ())), preferred_element_type=jnp.float32
    )


def weight_term(left, right, spread_columns=None):

    def term_rows():
        product = lax.dot_general(
            left, right, (((0,), (0,)), ((), ())), preferred_element_type=jnp.float32
        )
        if spread_columns is None:
            return product
        return spread_columns(product)

    return lax.psum_scatter(
        term_rows().astype(jnp.bfloat16), "dp", scatter_dimension=0, tiled=True
    ).astype(jnp.float32)


def attend_forward(queries, key_heads, values, key_valid):
    length_q, local_heads, head_dim = queries.shape
    block_rows = min(512, length_q)
    scale = head_dim ** (-0.5)

    def one_block(query_block):
        scores = (
            jnp.einsum("qhd,khd->hqk", query_block, key_heads, preferred_element_type=jnp.float32)
            * scale
        )
        scores = jnp.where(key_valid[None, None, :], scores, MASKED)
        row_max = jnp.max(scores, axis=-1, keepdims=True)
        exponent = jnp.exp(scores - row_max)
        row_total = jnp.sum(exponent, axis=-1, keepdims=True)
        weights = (exponent / row_total).astype(jnp.bfloat16)
        output = jnp.einsum("hqk,khd->qhd", weights, values, preferred_element_type=jnp.float32)
        return (output.astype(jnp.bfloat16), (row_max + jnp.log(row_total))[..., 0])

    blocks = queries.reshape(length_q // block_rows, block_rows, local_heads, head_dim)
    outputs, logsum = lax.map(one_block, blocks)
    return (outputs.reshape(length_q, local_heads, head_dim), logsum)


def attend_backward(queries, key_heads, values, key_valid, logsum, out_grad):
    length_q, local_heads, head_dim = queries.shape
    block_rows = logsum.shape[2]
    scale = head_dim ** (-0.5)
    query_blocks = queries.reshape(length_q // block_rows, block_rows, local_heads, head_dim)
    grad_blocks = out_grad.reshape(length_q // block_rows, block_rows, local_heads, head_dim)

    def one_block(carried, inputs):
        key_grad, value_grad = carried
        query_block, grad_block, logsum_block = inputs
        scores = (
            jnp.einsum("qhd,khd->hqk", query_block, key_heads, preferred_element_type=jnp.float32)
            * scale
        )
        scores = jnp.where(key_valid[None, None, :], scores, MASKED)
        probabilities = jnp.exp(scores - logsum_block[..., None])
        value_grad = value_grad + jnp.einsum(
            "hqk,qhd->khd",
            probabilities.astype(jnp.bfloat16),
            grad_block,
            preferred_element_type=jnp.float32,
        )
        prob_grad = jnp.einsum(
            "qhd,khd->hqk", grad_block, values, preferred_element_type=jnp.float32
        )
        row_delta = jnp.sum(probabilities * prob_grad, axis=-1, keepdims=True)
        score_grad = (probabilities * (prob_grad - row_delta)).astype(jnp.bfloat16)
        query_grad = (
            jnp.einsum("hqk,khd->qhd", score_grad, key_heads, preferred_element_type=jnp.float32)
            * scale
        )
        key_grad = (
            key_grad
            + jnp.einsum(
                "hqk,qhd->khd", score_grad, query_block, preferred_element_type=jnp.float32
            )
            * scale
        )
        return ((key_grad, value_grad), query_grad)

    zeros_kv = jnp.zeros(key_heads.shape, jnp.float32)
    carried, query_grads = lax.scan(
        one_block, (zeros_kv, zeros_kv), (query_blocks, grad_blocks, logsum)
    )
    return (query_grads.reshape(length_q, local_heads, head_dim), carried[0], carried[1])


def self_attention(inputs, gain_row, w_qkv, w_out, cosine_table, sine_table, head_count):
    frame_rows = inputs.shape[0]
    frames = frame_rows * head_count
    local_heads = HEADS // head_count
    normed, norm_saved = normalize(inputs, gain_row)
    normed_low = normed.astype(jnp.bfloat16)
    projected = jnp.dot(normed_low, w_qkv, preferred_element_type=jnp.float32).reshape(
        frame_rows, 3, HEADS, HEAD_DIM
    )
    turned = jnp.concatenate(
        [rotate(projected[:, :2], cosine_table, sine_table), projected[:, 2:]], axis=1
    )
    turned_low = turned.astype(jnp.bfloat16).reshape(frame_rows, 3, D)
    head_major = lax.all_to_all(
        turned_low, "head", split_axis=2, concat_axis=0, tiled=True
    ).reshape(frames, 3, local_heads, HEAD_DIM)
    everywhere = jnp.ones((frames,), dtype=jnp.bool_)
    attended, logsum = attend_forward(
        head_major[:, 0], head_major[:, 1], head_major[:, 2], everywhere
    )
    frame_major = lax.all_to_all(
        attended.reshape(frames, local_heads * HEAD_DIM),
        "head",
        split_axis=0,
        concat_axis=1,
        tiled=True,
    )
    branch = jnp.dot(frame_major, w_out, preferred_element_type=jnp.float32)
    return (inputs + branch, (normed_low, norm_saved, head_major, logsum, frame_major))


def cross_attention(
    inputs, gain_row, w_q2, w_kv2, w_out2, context_low, key_valid, head_count, head_index
):
    frame_rows = inputs.shape[0]
    frames = frame_rows * head_count
    local_heads = HEADS // head_count
    local_width = local_heads * HEAD_DIM
    prompt_rows = context_low.shape[0]
    normed, norm_saved = normalize(inputs, gain_row)
    normed_low = normed.astype(jnp.bfloat16)
    query_low = jnp.dot(normed_low, w_q2, preferred_element_type=jnp.float32).astype(jnp.bfloat16)
    query_heads = lax.all_to_all(
        query_low, "head", split_axis=1, concat_axis=0, tiled=True
    ).reshape(frames, local_heads, HEAD_DIM)
    own_columns = lax.dynamic_index_in_dim(
        w_kv2.reshape(CTX, 2, head_count, local_width), head_index, 2, keepdims=False
    ).reshape(CTX, 2 * local_width)
    key_value = jnp.dot(context_low, own_columns, preferred_element_type=jnp.float32).astype(
        jnp.bfloat16
    )
    key_value = key_value.reshape(prompt_rows, 2, local_heads, HEAD_DIM)
    attended, logsum = attend_forward(query_heads, key_value[:, 0], key_value[:, 1], key_valid)
    frame_major = lax.all_to_all(
        attended.reshape(frames, local_width), "head", split_axis=0, concat_axis=1, tiled=True
    )
    branch = jnp.dot(frame_major, w_out2, preferred_element_type=jnp.float32)
    return (inputs + branch, (normed_low, norm_saved, query_heads, key_value, logsum, frame_major))


def feed_forward(inputs, gain_row, w_in, w_down):
    normed, norm_saved = normalize(inputs, gain_row)
    normed_low = normed.astype(jnp.bfloat16)
    gate_up = jnp.dot(normed_low, w_in, preferred_element_type=jnp.float32)
    gate_part = gate_up[:, :FF]
    up_part = gate_up[:, FF:]
    hidden = (jax.nn.silu(gate_part) * up_part).astype(jnp.bfloat16)
    branch = jnp.dot(hidden, w_down, preferred_element_type=jnp.float32)
    return (inputs + branch, (normed_low, norm_saved, gate_part, up_part, hidden))


def forward(
    inputs, gains, weights, context_low, key_valid, cosine_table, sine_table, head_count, head_index
):
    w_qkv, w_out, w_q2, w_kv2, w_out2, w_in, w_down = weights
    first, saved_self = self_attention(
        inputs, gains[0], w_qkv, w_out, cosine_table, sine_table, head_count
    )
    second, saved_cross = cross_attention(
        first, gains[1], w_q2, w_kv2, w_out2, context_low, key_valid, head_count, head_index
    )
    third, saved_feed = feed_forward(second, gains[2], w_in, w_down)
    return (third, (saved_self, saved_cross, saved_feed))


def backward(saved, cotangent_row, gains, weights, key_valid, cosine_table, sine_table, head_count):
    full_qkv, full_out, full_q2, full_kv2, full_out2, full_in, full_down = weights
    saved_self, saved_cross, saved_feed = saved
    frame_rows = cotangent_row.shape[0]
    frames = frame_rows * head_count
    local_heads = HEADS // head_count
    local_width = local_heads * HEAD_DIM
    normed3, norm3_saved, gate_part, up_part, hidden = saved_feed
    hidden_grad = times_transposed(cotangent_row, full_down)
    sigmoid_gate = jax.nn.sigmoid(gate_part)
    silu_gate = gate_part * sigmoid_gate
    gate_grad = hidden_grad * up_part * sigmoid_gate * (1.0 + gate_part * (1.0 - sigmoid_gate))
    up_grad = hidden_grad * silu_gate
    gate_up_grad = jnp.concatenate([gate_grad, up_grad], axis=1).astype(jnp.bfloat16)
    normed_back, gain_three = normalize_back(
        times_transposed(gate_up_grad, full_in), gains[2], norm3_saved
    )
    residual_grad = cotangent_row.astype(jnp.float32) + normed_back
    normed2, norm2_saved, query_heads, key_value, cross_logsum, cross_frames = saved_cross
    cross_low = residual_grad.astype(jnp.bfloat16)
    cross_out_grad = times_transposed(cross_low, full_out2).astype(jnp.bfloat16)
    cross_grad_heads = lax.all_to_all(
        cross_out_grad, "head", split_axis=1, concat_axis=0, tiled=True
    )
    cross_grad_heads = cross_grad_heads.reshape(frames, local_heads, HEAD_DIM)
    query_grad, key_grad, value_grad = attend_backward(
        query_heads, key_value[:, 0], key_value[:, 1], key_valid, cross_logsum, cross_grad_heads
    )
    query_frames = lax.all_to_all(
        query_grad.astype(jnp.bfloat16).reshape(frames, local_width),
        "head",
        split_axis=0,
        concat_axis=1,
        tiled=True,
    )
    prompt_rows = key_value.shape[0]
    kv_grad = (
        jnp.stack([key_grad, value_grad], axis=1)
        .astype(jnp.bfloat16)
        .reshape(prompt_rows, 2 * local_width)
    )
    normed_back, gain_two = normalize_back(
        times_transposed(query_frames, full_q2), gains[1], norm2_saved
    )
    residual_grad = residual_grad + normed_back
    normed1, norm1_saved, head_major, self_logsum, self_frames = saved_self
    self_low = residual_grad.astype(jnp.bfloat16)
    self_out_grad = times_transposed(self_low, full_out).astype(jnp.bfloat16)
    self_grad_heads = lax.all_to_all(self_out_grad, "head", split_axis=1, concat_axis=0, tiled=True)
    self_grad_heads = self_grad_heads.reshape(frames, local_heads, HEAD_DIM)
    everywhere = jnp.ones((frames,), dtype=jnp.bool_)
    query_grad, key_grad, value_grad = attend_backward(
        head_major[:, 0],
        head_major[:, 1],
        head_major[:, 2],
        everywhere,
        self_logsum,
        self_grad_heads,
    )
    stacked = jnp.stack([query_grad, key_grad, value_grad], axis=1).astype(jnp.bfloat16)
    returned = lax.all_to_all(
        stacked.reshape(frames, 3, local_width), "head", split_axis=0, concat_axis=2, tiled=True
    )
    returned = returned.reshape(frame_rows, 3, HEADS, HEAD_DIM).astype(jnp.float32)
    unturned = jnp.concatenate(
        [rotate(returned[:, :2], cosine_table, -sine_table), returned[:, 2:]], axis=1
    )
    qkv_low = unturned.astype(jnp.bfloat16).reshape(frame_rows, 3 * D)
    normed_back, gain_one = normalize_back(
        times_transposed(qkv_low, full_qkv), gains[0], norm1_saved
    )
    input_grad = residual_grad + normed_back
    pairs = (
        (normed1, qkv_low),
        (self_frames, self_low),
        (normed2, query_frames),
        (None, kv_grad),
        (cross_frames, cross_low),
        (normed3, gate_up_grad),
        (hidden, cotangent_row),
    )
    return (input_grad, jnp.stack([gain_one, gain_two, gain_three]), pairs)


def general_body(
    tokens, context, lengths, norm_gains, w_qkv, w_out, w_q2, w_kv2, w_out2, w_in, w_down, cotangent
):
    head_count = lax.axis_size("head")
    head_index = lax.axis_index("head")
    frame_rows = tokens.shape[1]
    local_heads = HEADS // head_count
    local_width = local_heads * HEAD_DIM
    prompt_rows = context.shape[1]
    cosine_table, sine_table = rotary_tables(head_index * frame_rows, frame_rows)
    weights = (
        lax.all_gather(w_qkv, "dp", axis=0, tiled=True),
        lax.all_gather(w_out, "dp", axis=0, tiled=True),
        lax.all_gather(w_q2, "dp", axis=0, tiled=True),
        lax.all_gather(w_kv2, "dp", axis=0, tiled=True),
        lax.all_gather(w_out2, "dp", axis=0, tiled=True),
        lax.all_gather(w_in, "dp", axis=0, tiled=True),
        lax.all_gather(w_down, "dp", axis=0, tiled=True),
    )

    def valid_keys(sequence):
        return jnp.arange(prompt_rows, dtype=jnp.int32) < lengths[sequence]

    collected = [[] for position in range(7)]
    sequence = 0
    output, saved = forward(
        tokens[sequence].astype(jnp.float32),
        norm_gains,
        weights,
        context[sequence],
        valid_keys(sequence),
        cosine_table,
        sine_table,
        head_count,
        head_index,
    )
    outputs = [output.astype(jnp.bfloat16)]
    input_grad, gain_terms, pairs = backward(
        saved,
        cotangent[sequence],
        norm_gains,
        weights,
        valid_keys(sequence),
        cosine_table,
        sine_table,
        head_count,
    )
    input_grads = [input_grad]
    for position in range(7):
        left_part, right_part = pairs[position]
        if left_part is None:
            left_part = context[sequence]
        collected[position].append((left_part, right_part))
    owner_mask = (jnp.arange(head_count, dtype=jnp.int32) == head_index).astype(jnp.float32)

    def spread_heads(product):
        row_count = product.shape[0]
        placed = product.reshape(row_count, 2, 1, local_width) * owner_mask[None, None, :, None]
        return placed.reshape(row_count, 2 * D)

    grad_list = []
    for position in range(7):
        lefts = jnp.concatenate([pair[0] for pair in collected[position]], axis=0)
        rights = jnp.concatenate([pair[1] for pair in collected[position]], axis=0)
        lefts, rights = (lefts, rights)
        if position == 3:
            grad_list.append(weight_term(lefts, rights, spread_heads))
        else:
            grad_list.append(weight_term(lefts, rights))
    summed = (
        lax.psum(grad_list[0].astype(jnp.bfloat16), "head").astype(jnp.float32),
        lax.psum(grad_list[1].astype(jnp.bfloat16), "head").astype(jnp.float32),
        lax.psum(grad_list[2].astype(jnp.bfloat16), "head").astype(jnp.float32),
        lax.psum(grad_list[3].astype(jnp.bfloat16), "head").astype(jnp.float32),
        lax.psum(grad_list[4].astype(jnp.bfloat16), "head").astype(jnp.float32),
        lax.psum(grad_list[5].astype(jnp.bfloat16), "head").astype(jnp.float32),
        lax.psum(grad_list[6].astype(jnp.bfloat16), "head").astype(jnp.float32),
    )
    gains_grad = lax.psum(gain_terms, ("dp", "head"))
    return (
        jnp.stack(outputs),
        jnp.stack(input_grads),
        gains_grad,
        summed[0],
        summed[1],
        summed[2],
        summed[3],
        summed[4],
        summed[5],
        summed[6],
    )


LOG2E = 1.4426950408889634
LN2 = 0.6931471805599453
ROPE_BASE = 10000.0
LANES = 128
VMEM_BYTES = 48 * 1024 * 1024
SHARE = 1


def declared(flops, bytes_accessed, transcendentals):
    return pl.CostEstimate(
        flops=flops // SHARE,
        bytes_accessed=bytes_accessed // SHARE,
        transcendentals=transcendentals // SHARE,
    )


def in_order(*values):
    return lax.optimization_barrier(values)


def flipped(index_bit, count):
    return [(one, one ^ index_bit) for one in range(count)]


def swap_dp(value, index_bit):
    return lax.ppermute(value, "dp", flipped(index_bit, lax.axis_size("dp")))


def swap_head(value):
    return lax.ppermute(value, "head", [(0, 1), (1, 0)])


def take(value, index, axis):
    return lax.dynamic_index_in_dim(value, index, axis, keepdims=False)


def add_low(kept, received):
    return (kept.astype(jnp.float32) + received.astype(jnp.float32)).astype(jnp.bfloat16)


class RowSum:
    def __init__(self, term, z_first=False):
        place, count = lax.axis_index("dp"), lax.axis_size("dp")
        at_y, z_low, z_high = (place // 2) % 2, (place // 4) % 2, place // 8
        self.kept = None
        if z_first:
            self.stages = [(2, z_low, 4), (1, z_high, 8), (0, at_y, 2)]
            self.part = term.reshape(2, 2, 2, term.shape[0] // 8, term.shape[1])
            self.send()
            return
        self.stages = [(1, z_low, 4), (0, z_high, 8)]
        self.shape = (2, 2, term.shape[0] // 8, term.shape[1])
        self.received = lax.psum_scatter(
            term,
            "dp",
            scatter_dimension=0,
            axis_index_groups=[[one, one + 2] for one in range(count) if one % 4 < 2],
            tiled=True,
        )

    def send(self):
        axis, own, bit = self.stages.pop(0)
        self.received = swap_dp(take(self.part, 1 - own, axis), bit)
        self.kept = take(self.part, own, axis)

    def step(self):
        if self.kept is None:
            self.part = self.received.reshape(self.shape)
        else:
            self.part = add_low(self.kept, self.received)
        self.received = None
        if self.stages:
            self.send()

    def finish(self):
        while self.received is not None:
            self.step()
        return self.part


def arrived(value, *sums):
    tied = lax.optimization_barrier((value, *[one.received for one in sums]))
    for one, received in zip(sums, tied[1:]):
        one.received = received
    return tied[0]


def after(value, *sums):
    sums = [one for one in sums if one.received is not None]
    tied = lax.optimization_barrier((value, *[one.received for one in sums]))
    for one, received in zip(sums, tied[1:]):
        one.received = received
        one.step()
    return tied[0]


def place_bits():
    return (lax.axis_index("dp") % 2).reshape(1).astype(jnp.int32)


def turn_kernel(bits_ref, values_ref, mine_ref, theirs_ref):
    turned = values_ref[...].T
    block = turned.shape[0] // 16
    core = bits_ref[0]
    for at in range(8):
        first = turned[2 * at * block : (2 * at + 1) * block]
        second = turned[(2 * at + 1) * block : (2 * at + 2) * block]
        to = slice((at % 2 * 4 + at // 2) * block, (at % 2 * 4 + at // 2 + 1) * block)
        mine_ref[to, :] = jnp.where(core == 0, first, second)
        theirs_ref[to, :] = jnp.where(core == 0, second, first)


def turn_rows(values):
    frames, rows = values.shape
    step = min(frames, 512)
    grid_spec = pltpu.PrefetchScalarGridSpec(
        num_scalar_prefetch=1,
        grid=(frames // step,),
        in_specs=[pl.BlockSpec((step, rows), lambda n, s: (n, 0))],
        out_specs=[pl.BlockSpec((rows // 2, step), lambda n, s: (0, n))] * 2,
    )
    return pl.pallas_call(
        turn_kernel,
        name="turn_rows",
        grid_spec=grid_spec,
        out_shape=[jax.ShapeDtypeStruct((rows // 2, frames), jnp.bfloat16)] * 2,
        compiler_params=pltpu.CompilerParams(vmem_limit_bytes=VMEM_BYTES),
        cost_estimate=declared(0, 4 * frames * rows, 0),
    )(place_bits(), values)


def product_kernel(left_ref, right_ref, left2_ref, right2_ref, *out_refs):
    total = jnp.dot(left_ref[...], right_ref[...], preferred_element_type=jnp.float32)
    total += jnp.dot(left2_ref[...], right2_ref[...], preferred_element_type=jnp.float32)
    step, span = pl.program_id(0), pl.num_programs(0) // len(out_refs)
    for at, out_ref in enumerate(out_refs):

        @pl.when(step // span == at)
        def _():
            out_ref[...] = total.astype(jnp.bfloat16)


def products(lefts, rights, tile, name, pieces=1):
    rows, frames = lefts[0].shape
    width = rights[0].shape[1]
    span = width // tile // pieces

    def piece_at(piece):
        return lambda n: (0, jnp.clip(n - piece * span, 0, span - 1))

    left_spec = pl.BlockSpec((rows, frames), lambda n: (0, 0))
    right_spec = pl.BlockSpec((frames, tile), lambda n: (0, n))
    out = pl.pallas_call(
        product_kernel,
        name=name,
        grid=(width // tile,),
        in_specs=[left_spec, right_spec] * 2,
        out_specs=[pl.BlockSpec((rows, tile), piece_at(piece)) for piece in range(pieces)],
        out_shape=[jax.ShapeDtypeStruct((rows, width // pieces), jnp.bfloat16)] * pieces,
        compiler_params=pltpu.CompilerParams(vmem_limit_bytes=VMEM_BYTES),
        cost_estimate=declared(
            flops=4 * rows * frames * width,
            bytes_accessed=4 * rows * frames + 4 * frames * width + 2 * rows * width,
            transcendentals=0,
        ),
    )(lefts[0], rights[0], lefts[1], rights[1])
    return out if pieces > 1 else out[0]


def product_rows(left, right):
    return lax.dot_general(
        left, right, (((0,), (0,)), ((), ())), preferred_element_type=jnp.float32
    )


def turn(values, cosine, sine):
    width, quarter = values.shape[1], HEAD_DIM // 2
    lane = lax.broadcasted_iota(jnp.int32, values.shape, 1) % HEAD_DIM
    moved = jnp.where(
        lane < quarter,
        pltpu.roll(values, width - quarter, 1),
        pltpu.roll(values, quarter, 1),
    )
    if width > LANES:
        cosine = jnp.concatenate([cosine] * (width // LANES), axis=1)
        sine = jnp.concatenate([sine] * (width // LANES), axis=1)
    return values * cosine + moved * sine


def lane_tables(positions):
    half_dim = HEAD_DIM // 2
    frequencies = ROPE_BASE ** (-2.0 * jnp.arange(half_dim, dtype=jnp.float32) / HEAD_DIM)
    angles = positions.astype(jnp.float32)[:, None] * frequencies[None, :]
    cosine, sine = jnp.cos(angles), jnp.sin(angles)
    return (
        jnp.concatenate([cosine] * 4, axis=1),
        jnp.concatenate([-sine, sine, -sine, sine], axis=1),
    )


def qkv_kernel(h_ref, w_ref, cosine_ref, sine_ref, out_ref):
    width = out_ref.shape[1]
    projected = jnp.dot(h_ref[...], w_ref[...], preferred_element_type=jnp.float32)
    step = pl.program_id(0)
    third = pl.num_programs(0) // 3

    @pl.when(step < 2 * third)
    def _():
        scale = jnp.where(step < third, HEAD_DIM ** (-0.5), 1.0)
        for at in range(0, width, LANES):
            turned = turn(projected[:, at : at + LANES], cosine_ref[...], sine_ref[...])
            out_ref[:, at : at + LANES] = (turned * scale).astype(jnp.bfloat16)

    @pl.when(step >= 2 * third)
    def _():
        out_ref[...] = projected.astype(jnp.bfloat16)


def project_qkv(normed, weight, start, width, cosine, sine):
    rows, depth = normed.shape
    tile = 384
    return pl.pallas_call(
        qkv_kernel,
        name="qkv_projection",
        grid=(width // tile,),
        in_specs=[
            pl.BlockSpec((rows, depth), lambda n: (0, 0)),
            pl.BlockSpec((depth, tile), lambda n: (0, start // tile + n)),
            pl.BlockSpec((rows, LANES), lambda n: (0, 0)),
            pl.BlockSpec((rows, LANES), lambda n: (0, 0)),
        ],
        out_specs=pl.BlockSpec((rows, tile), lambda n: (0, n)),
        out_shape=jax.ShapeDtypeStruct((rows, width), jnp.bfloat16),
        compiler_params=pltpu.CompilerParams(vmem_limit_bytes=VMEM_BYTES),
        cost_estimate=declared(
            flops=2 * rows * depth * width,
            bytes_accessed=2 * (rows * depth + depth * width + rows * width),
            transcendentals=0,
        ),
    )(normed, weight, cosine, sine)


def nt_dot(left, right):
    return lax.dot_general(
        left, right, (((1,), (1,)), ((), ())), preferred_element_type=jnp.float32
    )


def attend_kernel(masked, length_ref, q_ref, k_ref, v_ref, out_ref, lse_ref):
    for head in range(q_ref.shape[1] // HEAD_DIM):
        lanes = slice(head * HEAD_DIM, (head + 1) * HEAD_DIM)
        scores = nt_dot(q_ref[:, lanes], k_ref[:, lanes])
        if masked:
            key = lax.broadcasted_iota(jnp.int32, scores.shape, 1)
            scores = jnp.where(key < length_ref[0], scores, MASKED)
        row_max = jnp.max(scores, axis=1, keepdims=True)
        exponent = jnp.exp2(scores * LOG2E - row_max * LOG2E)
        total = jnp.sum(exponent, axis=1, keepdims=True)
        mixed = jnp.dot(
            exponent.astype(jnp.bfloat16), v_ref[:, lanes], preferred_element_type=jnp.float32
        )
        out_ref[:, lanes] = (mixed / total).astype(jnp.bfloat16)
        lse_ref[:, lanes] = jnp.broadcast_to(
            row_max * LOG2E + jnp.log2(total), (row_max.shape[0], HEAD_DIM)
        )


def attend(length, queries, keys, values, width, columns, masked, name, span, block):
    rows, key_rows = queries.shape[0], keys.shape[0]
    pairs = width // span
    q_at, k_at, v_at = columns
    grid_spec = pltpu.PrefetchScalarGridSpec(
        num_scalar_prefetch=1,
        grid=(pairs, rows // block),
        in_specs=[
            pl.BlockSpec((block, span), lambda p, i, s: (i, q_at + p)),
            pl.BlockSpec((key_rows, span), lambda p, i, s: (0, k_at + p)),
            pl.BlockSpec((key_rows, span), lambda p, i, s: (0, v_at + p)),
        ],
        out_specs=[
            pl.BlockSpec((block, span), lambda p, i, s: (i, p)),
            pl.BlockSpec((block, span), lambda p, i, s: (i, p)),
        ],
    )
    return pl.pallas_call(
        functools.partial(attend_kernel, masked),
        name=name,
        grid_spec=grid_spec,
        out_shape=[
            jax.ShapeDtypeStruct((rows, width), jnp.bfloat16),
            jax.ShapeDtypeStruct((rows, width), jnp.float32),
        ],
        compiler_params=pltpu.CompilerParams(vmem_limit_bytes=VMEM_BYTES),
        cost_estimate=declared(
            flops=16 * rows * key_rows * width,
            bytes_accessed=8 * rows * width,
            transcendentals=rows * key_rows * width // HEAD_DIM,
        ),
    )(length, queries, keys, values)


def attend_back_kernel(
    masked,
    turned,
    length_ref,
    q_ref,
    k_ref,
    v_ref,
    grad_ref,
    out_ref,
    lse_ref,
    *rest,
):
    if turned:
        cosq_ref, sinq_ref, cosk_ref, sink_ref = rest[:4]
        rest = rest[4:]
    dq_ref, dk_ref, dv_ref, dk_sum, dv_sum = rest
    step, steps = pl.program_id(1), pl.num_programs(1)

    @pl.when(step == 0)
    def _():
        dk_sum[...] = jnp.zeros_like(dk_sum)
        dv_sum[...] = jnp.zeros_like(dv_sum)

    lse_rows = lse_ref[...].T
    delta_rows = (grad_ref[...].astype(jnp.float32) * out_ref[...].astype(jnp.float32)).T
    dq_parts = []
    for head in range(q_ref.shape[1] // HEAD_DIM):
        lanes = slice(head * HEAD_DIM, (head + 1) * HEAD_DIM)
        query, key, value = q_ref[:, lanes], k_ref[:, lanes], v_ref[:, lanes]
        grad = grad_ref[:, lanes]
        scores = nt_dot(key, query)
        if masked:
            index = lax.broadcasted_iota(jnp.int32, scores.shape, 0)
            scores = jnp.where(index < length_ref[0], scores, MASKED)
        lse = lse_rows[head * HEAD_DIM : head * HEAD_DIM + 1, :]
        delta = jnp.sum(delta_rows[lanes, :], axis=0, keepdims=True)
        weight = jnp.exp2(scores * LOG2E - lse)
        dv_sum[:, lanes] += jnp.dot(
            weight.astype(jnp.bfloat16), grad, preferred_element_type=jnp.float32
        )
        weight_grad = nt_dot(value, grad)
        score_grad = (weight * (weight_grad - delta)).astype(jnp.bfloat16)
        dk_sum[:, lanes] += jnp.dot(score_grad, query, preferred_element_type=jnp.float32)
        dq_parts.append(product_rows(score_grad, key) * HEAD_DIM ** (-0.5))
    dq = jnp.concatenate(dq_parts, axis=1).astype(jnp.bfloat16)
    if turned:
        dq = turn(dq.astype(jnp.float32), cosq_ref[...], -sinq_ref[...]).astype(jnp.bfloat16)
    dq_ref[...] = dq

    @pl.when(step == steps - 1)
    def _():
        dk = dk_sum[...].astype(jnp.bfloat16)
        if turned:
            dk = turn(dk.astype(jnp.float32), cosk_ref[...], -sink_ref[...]).astype(jnp.bfloat16)
        dk_ref[...] = dk
        dv_ref[...] = dv_sum[...].astype(jnp.bfloat16)


def attend_back(
    length,
    queries,
    keys,
    values,
    columns,
    grad_at,
    width,
    grad,
    outputs,
    lse,
    tables,
    masked,
    name,
    span,
    block,
):
    rows, key_rows = queries.shape[0], keys.shape[0]
    pairs = width // span
    q_at, k_at, v_at = columns
    by_query = pl.BlockSpec((block, span), lambda p, i, s: (i, p))
    by_grad = pl.BlockSpec((block, span), lambda p, i, s: (i, grad_at + p))
    by_key = pl.BlockSpec((key_rows, span), lambda p, i, s: (0, p))
    in_specs = [
        pl.BlockSpec((block, span), lambda p, i, s: (i, q_at + p)),
        pl.BlockSpec((key_rows, span), lambda p, i, s: (0, k_at + p)),
        pl.BlockSpec((key_rows, span), lambda p, i, s: (0, v_at + p)),
        by_grad,
        by_grad,
        by_grad,
    ]
    operands = [queries, keys, values, grad, outputs, lse]
    if tables is not None:
        cosine, sine = tables
        in_specs += [pl.BlockSpec((block, LANES), lambda p, i, s: (i, 0))] * 2
        in_specs += [pl.BlockSpec((key_rows, LANES), lambda p, i, s: (0, 0))] * 2
        operands += [cosine, sine, cosine, sine]
    grid_spec = pltpu.PrefetchScalarGridSpec(
        num_scalar_prefetch=1,
        grid=(pairs, rows // block),
        in_specs=in_specs,
        out_specs=[by_query, by_key, by_key],
        scratch_shapes=[pltpu.VMEM((key_rows, span), jnp.float32)] * 2,
    )
    return pl.pallas_call(
        functools.partial(attend_back_kernel, masked, tables is not None),
        name=name,
        grid_spec=grid_spec,
        out_shape=[
            jax.ShapeDtypeStruct((rows, width), jnp.bfloat16),
            jax.ShapeDtypeStruct((key_rows, width), jnp.bfloat16),
            jax.ShapeDtypeStruct((key_rows, width), jnp.bfloat16),
        ],
        compiler_params=pltpu.CompilerParams(vmem_limit_bytes=VMEM_BYTES),
        cost_estimate=declared(
            flops=40 * rows * key_rows * width,
            bytes_accessed=20 * rows * width,
            transcendentals=rows * key_rows * width // HEAD_DIM,
        ),
    )(length, *operands)


def feed_kernel(bits_ref, h_ref, cot_ref, in_ref, down_ref, *rest):
    mine_ref, theirs_ref, dgu_ref, out_ref, down, total = rest[-6:]
    step, steps = pl.program_id(0), pl.num_programs(0)
    depth, tile = h_ref.shape[1], down.shape[0]
    piece = down_ref.shape[0] // 2
    for at in range(4):
        place, part = at // 2, at % 2
        down[at * piece : (at + 1) * piece, :] = down_ref[
            place * piece : (place + 1) * piece, part * depth : (part + 1) * depth
        ]
    @pl.when(step == 0)
    def _():
        total[...] = jnp.zeros_like(total)

    chunk = h_ref.shape[0] // 2
    for at in range(2):
        rows = slice(at * chunk, (at + 1) * chunk)
        gate_up = jnp.dot(h_ref[rows, :], in_ref[...], preferred_element_type=jnp.float32)
        grad = nt_dot(cot_ref[rows, :], down[...])
        gate, up = gate_up[:, :tile], gate_up[:, tile:]
        sigmoid = jax.nn.sigmoid(gate)
        silu = gate * sigmoid
        hidden = (silu * up).astype(jnp.bfloat16)
        turned = hidden.T
        first, second = turned[: tile // 2], turned[tile // 2 :]
        mine_ref[:, rows] = jnp.where(bits_ref[0] == 0, first, second)
        theirs_ref[:, rows] = jnp.where(bits_ref[0] == 0, second, first)
        dgu_ref[rows, tile:] = (grad * silu).astype(jnp.bfloat16)
        dgu_ref[rows, :tile] = (
            grad * up * sigmoid * (1.0 + gate * (1.0 - sigmoid))
        ).astype(jnp.bfloat16)
        total[rows, :] += jnp.dot(hidden, down[...], preferred_element_type=jnp.float32)

    @pl.when(step == steps - 1)
    def _():
        out_ref[...] = total[...].astype(out_ref.dtype)


def feed(normed, cotangent, weights, half, earlier):
    rows, depth = normed.shape
    units = FF // 2
    steps = depth // 192
    tile = units // steps
    operands = [normed, cotangent, weights, weights]
    in_specs = [
        pl.BlockSpec((rows, depth), lambda n, s: (0, 0)),
        pl.BlockSpec((rows, depth), lambda n, s: (0, 0)),
        pl.BlockSpec((depth, 2 * tile), lambda n, s: (0, n)),
        pl.BlockSpec((depth // steps, 2 * depth), lambda n, s: (n, 2)),
    ]
    aliases = {}
    if earlier is not None:
        in_specs += [pl.BlockSpec(memory_space=pl.ANY)] * 3
        aliases = {5: 0, 6: 1, 7: 2}
        operands += list(earlier)

    def turned_at(n, s):
        return (n % 2 * 4 + n // 2, half)

    grid_spec = pltpu.PrefetchScalarGridSpec(
        num_scalar_prefetch=1,
        grid=(steps,),
        in_specs=in_specs,
        out_specs=[
            pl.BlockSpec((tile // 2, rows), turned_at),
            pl.BlockSpec((tile // 2, rows), turned_at),
            pl.BlockSpec((rows, 2 * tile), lambda n, s: (half, n)),
            pl.BlockSpec((rows, depth), lambda n, s: (0, 0)),
        ],
        scratch_shapes=[
            pltpu.VMEM((tile, depth), jnp.bfloat16),
            pltpu.VMEM((rows, depth), jnp.float32),
        ],
    )
    return pl.pallas_call(
        feed_kernel,
        name="feed_forward",
        grid_spec=grid_spec,
        out_shape=[
            jax.ShapeDtypeStruct((units // 2, 2 * rows), jnp.bfloat16),
            jax.ShapeDtypeStruct((units // 2, 2 * rows), jnp.bfloat16),
            jax.ShapeDtypeStruct((2 * rows, 2 * units), jnp.bfloat16),
            jax.ShapeDtypeStruct((rows, depth), jnp.bfloat16 if half else jnp.float32),
        ],
        input_output_aliases=aliases,
        compiler_params=pltpu.CompilerParams(vmem_limit_bytes=VMEM_BYTES),
        cost_estimate=declared(
            flops=8 * rows * depth * units,
            bytes_accessed=6 * depth * units + 6 * rows * units + 8 * rows * depth,
            transcendentals=rows * units,
        ),
    )(place_bits(), *operands)


def back_kernel(left_ref, right_ref, out_ref, total):
    step, steps = pl.program_id(0), pl.num_programs(0)

    @pl.when(step == 0)
    def _():
        total[...] = jnp.zeros_like(total)

    total[...] += nt_dot(left_ref[...], right_ref[...])

    @pl.when(step == steps - 1)
    def _():
        out_ref[...] = total[...].astype(out_ref.dtype)


def times_turned(left, right, at, rows, start, width, kind, name):
    depth = right.shape[0]
    tile = 1536 if width % 1536 == 0 else 768
    return pl.pallas_call(
        back_kernel,
        name=name,
        grid=(width // tile,),
        in_specs=[
            pl.BlockSpec((rows, tile), lambda n: (at, n)),
            pl.BlockSpec((depth, tile), lambda n: (0, start // tile + n)),
        ],
        out_specs=pl.BlockSpec((rows, depth), lambda n: (0, 0)),
        out_shape=jax.ShapeDtypeStruct((rows, depth), kind),
        scratch_shapes=[pltpu.VMEM((rows, depth), jnp.float32)],
        compiler_params=pltpu.CompilerParams(vmem_limit_bytes=VMEM_BYTES),
        cost_estimate=declared(
            flops=2 * rows * depth * width,
            bytes_accessed=2 * rows * width + 2 * depth * width + 4 * rows * depth,
            transcendentals=0,
        ),
    )(left, right)


def norm_back_into(total, x_ref, gain_ref, residual_ref, sum_ref, low_ref, term_ref):
    chunk = 128
    term = jnp.zeros(term_ref.shape, jnp.float32)
    for at in range(0, total.shape[0], chunk):
        rows = slice(at, at + chunk)
        grad = total[rows, :]
        values = x_ref[rows, :]
        centred = values - jnp.mean(values, axis=1, keepdims=True)
        inverse = lax.rsqrt(jnp.mean(centred * centred, axis=1, keepdims=True) + EPSILON)
        scaled = centred * inverse
        term += jnp.sum(grad * scaled, axis=0, keepdims=True)
        inner = grad * gain_ref[...]
        back = inverse * (
            inner
            - jnp.mean(inner, axis=1, keepdims=True)
            - scaled * jnp.mean(inner * scaled, axis=1, keepdims=True)
        )
        summed = residual_ref[rows, :].astype(jnp.float32) + back
        sum_ref[rows, :] = summed
        low_ref[rows, :] = summed.astype(jnp.bfloat16)
    term_ref[...] = term


def feed_back_kernel(
    left_ref, right_ref, other_ref, x_ref, gain_ref, residual_ref, sum_ref, low_ref, term_ref, total
):
    step, steps = pl.program_id(0), pl.num_programs(0)

    @pl.when(step == 0)
    def _():
        total[...] = other_ref[...].astype(jnp.float32)

    total[...] += nt_dot(left_ref[...], right_ref[...])

    @pl.when(step == steps - 1)
    def _():
        norm_back_into(total, x_ref, gain_ref, residual_ref, sum_ref, low_ref, term_ref)


def feed_back(left, right, other, values, gain, residual):
    rows, depth = values.shape
    tile = 1536
    whole = pl.BlockSpec((rows, depth), lambda n: (0, 0))
    line = pl.BlockSpec((1, depth), lambda n: (0, 0))
    return pl.pallas_call(
        feed_back_kernel,
        name="h3_back_norm",
        grid=(FF // tile,),
        in_specs=[
            pl.BlockSpec((rows, tile), lambda n: (0, n)),
            pl.BlockSpec((depth, tile), lambda n: (0, n)),
            whole,
            whole,
            line,
            whole,
        ],
        out_specs=[whole, whole, line],
        out_shape=[
            jax.ShapeDtypeStruct((rows, depth), jnp.float32),
            jax.ShapeDtypeStruct((rows, depth), jnp.bfloat16),
            jax.ShapeDtypeStruct((1, depth), jnp.float32),
        ],
        scratch_shapes=[pltpu.VMEM((rows, depth), jnp.float32)],
        compiler_params=pltpu.CompilerParams(vmem_limit_bytes=VMEM_BYTES),
        cost_estimate=declared(2 * rows * depth * FF, 2 * depth * FF, 0),
    )(left, right, other, values, gain, residual)


def cross_back_kernel(
    length_ref,
    low_ref,
    out_weight_ref,
    q_weight_ref,
    q_ref,
    k_ref,
    v_ref,
    out_ref,
    lse_ref,
    x_ref,
    gain_ref,
    residual_ref,
    dq_ref,
    dk_ref,
    dv_ref,
    sum_ref,
    new_low_ref,
    term_ref,
    total,
):
    step, steps = pl.program_id(0), pl.num_programs(0)
    grad_all = nt_dot(low_ref[...], out_weight_ref[...])
    lse_rows = lse_ref[...].T
    delta_rows = (grad_all * out_ref[...].astype(jnp.float32)).T
    grad_all = grad_all.astype(jnp.bfloat16)
    for head in range(q_ref.shape[1] // HEAD_DIM):
        lanes = slice(head * HEAD_DIM, (head + 1) * HEAD_DIM)
        query, key, value = q_ref[:, lanes], k_ref[:, lanes], v_ref[:, lanes]
        grad = grad_all[:, lanes]
        scores = nt_dot(key, query)
        index = lax.broadcasted_iota(jnp.int32, scores.shape, 0)
        scores = jnp.where(index < length_ref[0], scores, MASKED)
        lse = lse_rows[head * HEAD_DIM : head * HEAD_DIM + 1, :]
        delta = jnp.sum(delta_rows[lanes, :], axis=0, keepdims=True)
        weight = jnp.exp2(scores * LOG2E - lse)
        dv = jnp.dot(weight.astype(jnp.bfloat16), grad, preferred_element_type=jnp.float32)
        dv_ref[:, lanes] = dv.astype(jnp.bfloat16)
        score_grad = (weight * (nt_dot(value, grad) - delta)).astype(jnp.bfloat16)
        dk = jnp.dot(score_grad, query, preferred_element_type=jnp.float32)
        dk_ref[:, lanes] = dk.astype(jnp.bfloat16)
        dq = product_rows(score_grad, key) * HEAD_DIM ** (-0.5)
        dq_ref[:, lanes] = dq.astype(jnp.bfloat16)
    back = nt_dot(dq_ref[...], q_weight_ref[...])

    @pl.when(step == 0)
    def _():
        total[...] = back

    @pl.when(step > 0)
    def _():
        total[...] += back

    @pl.when(step == steps - 1)
    def _():
        norm_back_into(total, x_ref, gain_ref, residual_ref, sum_ref, new_low_ref, term_ref)


def cross_back(length, low, out_weight, q_weight, query, key, value, outputs, lse, values, gain, residual):
    rows, depth = values.shape
    key_rows = key.shape[0]
    tile = 384
    steps = depth // tile
    whole = pl.BlockSpec((rows, depth), lambda n, s: (0, 0))
    line = pl.BlockSpec((1, depth), lambda n, s: (0, 0))
    by_query = pl.BlockSpec((rows, tile), lambda n, s: (0, n))
    by_key = pl.BlockSpec((key_rows, tile), lambda n, s: (0, n))
    grid_spec = pltpu.PrefetchScalarGridSpec(
        num_scalar_prefetch=1,
        grid=(steps,),
        in_specs=[
            whole,
            pl.BlockSpec((tile, depth), lambda n, s: (n, 0)),
            pl.BlockSpec((depth, tile), lambda n, s: (0, n)),
            by_query,
            by_key,
            by_key,
            by_query,
            by_query,
            whole,
            line,
            whole,
        ],
        out_specs=[by_query, by_key, by_key, whole, whole, line],
        scratch_shapes=[pltpu.VMEM((rows, depth), jnp.float32)],
    )
    return pl.pallas_call(
        cross_back_kernel,
        name="cross_back",
        grid_spec=grid_spec,
        out_shape=[
            jax.ShapeDtypeStruct((rows, depth), jnp.bfloat16),
            jax.ShapeDtypeStruct((key_rows, depth), jnp.bfloat16),
            jax.ShapeDtypeStruct((key_rows, depth), jnp.bfloat16),
            jax.ShapeDtypeStruct((rows, depth), jnp.float32),
            jax.ShapeDtypeStruct((rows, depth), jnp.bfloat16),
            jax.ShapeDtypeStruct((1, depth), jnp.float32),
        ],
        compiler_params=pltpu.CompilerParams(vmem_limit_bytes=VMEM_BYTES),
        cost_estimate=declared(4 * rows * depth * depth, 8 * depth * depth, 0),
    )(length, low, out_weight, q_weight, query, key, value, outputs, lse, values, gain, residual)


def split_back_kernel(side_ref, left_ref, right_ref, kept_ref, sent_ref):
    half = kept_ref.shape[1]
    lower = nt_dot(left_ref[...], right_ref[:half, :]).astype(jnp.bfloat16)
    upper = nt_dot(left_ref[...], right_ref[half:, :]).astype(jnp.bfloat16)
    kept_ref[...] = jnp.where(side_ref[0] == 0, lower, upper)
    sent_ref[...] = jnp.where(side_ref[0] == 0, upper, lower)


def split_back(side, left, weights):
    rows, depth = left.shape
    return pl.pallas_call(
        split_back_kernel,
        name="attention_grad",
        grid=(1,),
        in_specs=[
            pl.BlockSpec(memory_space=pltpu.SMEM),
            pl.BlockSpec((rows, depth), lambda n: (0, 0)),
            pl.BlockSpec((depth, depth), lambda n: (0, 0)),
        ],
        out_specs=[pl.BlockSpec((rows, depth // 2), lambda n: (0, 0))] * 2,
        out_shape=[jax.ShapeDtypeStruct((rows, depth // 2), jnp.bfloat16)] * 2,
        compiler_params=pltpu.CompilerParams(vmem_limit_bytes=VMEM_BYTES),
        cost_estimate=declared(2 * rows * depth * depth, 2 * depth * depth, 0),
    )(side.reshape(1).astype(jnp.int32), left, weights)


def in_grad_kernel(side_ref, *refs):
    out_ref = refs[-1]
    unit = refs[0].shape[1] // 8
    for part in range(2):
        mine_ref, theirs_ref = refs[2 * part], refs[2 * part + 1]
        for at in range(8):
            mine = mine_ref[:, at * unit : (at + 1) * unit].astype(jnp.float32)
            theirs = theirs_ref[:, at * unit : (at + 1) * unit].astype(jnp.float32)
            tile, gate_or_up = part * 4 + at // 2, at % 2
            to = (gate_or_up * 8 + tile) * 2 * unit
            out_ref[:, to : to + unit] = jnp.where(side_ref[0] == 0, mine, theirs)
            out_ref[:, to + unit : to + 2 * unit] = jnp.where(side_ref[0] == 0, theirs, mine)


def assemble_in_grad(side, parts):
    rows, width = parts[0].shape
    whole = pl.BlockSpec(memory_space=pltpu.VMEM)
    return pl.pallas_call(
        in_grad_kernel,
        name="in_grad_rows",
        in_specs=[pl.BlockSpec(memory_space=pltpu.SMEM)] + [whole] * 4,
        out_specs=whole,
        out_shape=jax.ShapeDtypeStruct((rows, 4 * width), jnp.float32),
        compiler_params=pltpu.CompilerParams(vmem_limit_bytes=VMEM_BYTES),
        cost_estimate=declared(0, 16 * rows * width, 0),
    )(side.reshape(1).astype(jnp.int32), *parts)


def paired_body(
    tokens, context, lengths, norm_gains, w_qkv, w_out, w_q2, w_kv2, w_out2, w_in, w_down, cotangent
):
    place, side = lax.axis_index("dp"), lax.axis_index("head")
    core = place % 2
    on_left = side == 0
    own = tokens[0]
    frames = own.shape[0]
    rows = w_qkv.shape[0]
    half = D // 2
    units = w_down.shape[0]

    def ordered(mine, theirs):
        return jnp.where(on_left, mine, theirs), jnp.where(on_left, theirs, mine)

    qkv_half = take(w_qkv.reshape(rows, 3, 2, half), side, 2).reshape(rows, 3 * half)
    q2_half, out2_half = [take(one.reshape(rows, 2, half), side, 1) for one in (w_q2, w_out2)]
    kv2_half = take(w_kv2.reshape(rows // 2, 2, 2, half), side, 2)
    kv2_half = jnp.concatenate([kv2_half[:, 0], kv2_half[:, 1]], axis=0)
    full_first = lax.all_gather(
        jnp.concatenate([w_out, qkv_half, q2_half, out2_half, kv2_half], axis=1),
        "dp",
        axis=0,
        tiled=True,
    )
    full_out = full_first[:, :D]
    own_halves = full_first[:, D + 3 * half : D + 5 * half]
    core_rows = swap_head(take(own_halves.reshape(2, half, D), core, 0))
    kv2_half = full_first[:, D + 5 * half :].reshape(rows // 6, 2, rows // 2, half)
    kv2_weights = [kv2_half[:, one].reshape(D // 2, half) for one in range(2)]
    in_half = take(w_in.reshape(rows, 2, 8, 2, units), side, 3)
    in_half = jnp.swapaxes(in_half, 1, 2).reshape(rows, FF)
    down_parts = w_down.reshape(2, units // 2, D)
    down_received = swap_dp(take(down_parts, 1 - core, 0), 1)
    down_half = jnp.where(core == side, take(down_parts, core, 0), down_received)
    full_feed = lax.all_gather(
        jnp.concatenate([in_half, down_half[:rows], down_half[rows:]], axis=1),
        "dp",
        axis=0,
        tiled=True,
    )
    full_in = full_feed[:, :FF]

    both_tokens = jnp.concatenate([own, swap_head(own)], axis=0).astype(jnp.float32)
    own_cot, other_cot = cotangent[0], swap_head(cotangent[0])
    both_cot = jnp.concatenate([own_cot, other_cot], axis=0)
    frame = jnp.arange(frames, dtype=jnp.int32)
    tables = lane_tables(
        jnp.concatenate([side * frames + frame, (1 - side) * frames + frame])
    )
    normed1 = normalize(both_tokens, norm_gains[0])[0].astype(jnp.bfloat16)
    inputs = own.astype(jnp.float32)
    norm1_saved = normalize(inputs, norm_gains[0])[1]
    qkv = project_qkv(normed1, full_first, D, 3 * half, *tables)
    no_length = jnp.zeros((1,), jnp.int32)
    pairs = half // (2 * LANES)
    self_columns = (0, pairs, 2 * pairs)
    attended, self_lse = attend(
        no_length, qkv, qkv, qkv, half, self_columns, False, "self_attention", 2 * LANES, 512
    )
    key_value = jnp.stack(
        [
            jnp.dot(context[0], weight, preferred_element_type=jnp.float32).astype(jnp.bfloat16)
            for weight in kv2_weights
        ]
    )
    attended, core_rows, key_value_other = in_order(attended, core_rows, swap_head(key_value))
    attended_other = swap_head(attended[frames:])
    sibling_rows = swap_dp(core_rows, 1)
    other_halves = jnp.where(
        core == 0,
        jnp.concatenate([core_rows, sibling_rows], axis=0),
        jnp.concatenate([sibling_rows, core_rows], axis=0),
    )
    full_q2, full_out2 = in_order(
        *[
            jnp.concatenate(
                ordered(own_halves[:, at : at + half], other_halves[:, at : at + half]), axis=1
            )
            for at in (0, half)
        ]
    )
    attended_frames = jnp.concatenate(ordered(attended[:frames], attended_other), axis=1)
    first = inputs + jnp.dot(attended_frames, full_out, preferred_element_type=jnp.float32)

    normed2, norm2_saved = normalize(first, norm_gains[1])
    normed2 = normed2.astype(jnp.bfloat16)
    query2 = jnp.dot(normed2, full_q2, preferred_element_type=jnp.float32)
    query2 = (query2.astype(jnp.bfloat16) * HEAD_DIM ** (-0.5)).astype(jnp.bfloat16)
    key2, value2 = jnp.concatenate(ordered(key_value, key_value_other), axis=2)
    crossed, cross_lse = attend(
        lengths, query2, key2, value2, D, (0, 0, 0), True, "cross_attention", 3 * LANES, frames
    )
    second = first + jnp.dot(crossed, full_out2, preferred_element_type=jnp.float32)

    def left_pair(values):
        mine, theirs = turn_rows(values)
        return mine, swap_dp(theirs, 1)

    lefts1 = left_pair(normed1)
    lefts_out = left_pair(attended_frames)
    lefts2 = left_pair(normed2)
    lefts_cross = left_pair(crossed)
    lefts_context = left_pair(context[0])
    cots = both_cot, swap_dp(both_cot, 1)

    normed3, norm3_saved = normalize(second, norm_gains[2])
    normed3 = normed3.astype(jnp.bfloat16)
    other3 = swap_head(normed3)
    *fed, own_out = feed(normed3, own_cot, full_feed, 0, None)
    fed, lefts1, lefts_out, lefts2, lefts_cross, lefts_context, cots = in_order(
        fed, lefts1, lefts_out, lefts2, lefts_cross, lefts_context, cots
    )
    hidden, hidden_theirs, dgu, other_out = feed(other3, other_cot, full_feed, 1, fed)
    lefts3 = left_pair(jnp.concatenate([normed3, other3], axis=0))
    hidden, dgu = in_order(hidden, dgu)
    hiddens = hidden, swap_dp(hidden_theirs, 1)
    dgus = dgu, swap_dp(dgu, 1)
    sent3 = times_turned(dgu, full_feed, 1, frames, 0, FF, jnp.bfloat16, "h3_back")
    hiddens, sent3 = in_order(hiddens, sent3)
    received3 = swap_head(sent3)
    down_term = products(hiddens, cots, 512, "down_grad")
    dgus, down_term = in_order(dgus, down_term)
    down_sum = RowSum(down_term)
    in_terms = products(lefts3, dgus, 512, "in_grad", 2)
    in_terms, dgu = in_order(in_terms, dgu)
    residual3, cross_low, gain_three = feed_back(
        dgu, full_feed, received3, second, norm_gains[2:], own_cot
    )
    cross_low, in_terms = in_order(cross_low, in_terms)
    in_sums = [RowSum(one) for one in in_terms]
    cross_low = after(cross_low, down_sum)
    received_out = swap_head(other_out)

    query2_grad, key2_grad, value2_grad, residual2, self_low, gain_two = cross_back(
        lengths,
        cross_low,
        full_out2,
        full_q2,
        query2,
        key2,
        value2,
        crossed,
        cross_lse,
        first,
        norm_gains[1:2],
        residual3,
    )
    grad_kept, grad_sent = split_back(side, self_low, full_first)
    grad_kept, received_out = in_order(grad_kept, received_out)
    grad_kept = after(grad_kept, down_sum)
    output = (second + own_out + received_out.astype(jnp.float32)).astype(jnp.bfloat16)
    grad_received = swap_head(grad_sent)
    kv2_grad = jnp.concatenate([key2_grad, value2_grad], axis=1)

    def square(lefts, right, name):
        return products(lefts, (right, swap_dp(right, 1)), 512, name)

    def meet(lower, upper):
        sent, middle = jnp.where(on_left, upper, lower), lower.shape[0] // 2
        return (
            jnp.where(on_left, lower, upper),
            swap_head(sent[:middle]),
            swap_head(sent[middle:]),
        )

    def met(terms, z_first):
        return RowSum(add_low(terms[0], jnp.concatenate(terms[1:], axis=0)), z_first)

    query2_grad, cross_low, kv2_grad, grad_kept = in_order(
        query2_grad, cross_low, kv2_grad, grad_kept
    )
    out2_terms = square(lefts_cross, cross_low, "out2_grad")
    q2_terms = square(lefts2, query2_grad, "q2_grad")
    out2_terms, q2_terms, self_low, kv2_grad = in_order(out2_terms, q2_terms, self_low, kv2_grad)
    cross_terms = meet(out2_terms, q2_terms)
    kv2_terms = square(lefts_context, kv2_grad, "kv2_grad").reshape(8, rows // 2, 2, D)
    kv2_terms = jnp.swapaxes(kv2_terms, 1, 2).reshape(8 * rows, D)
    out_terms = square(lefts_out, self_low, "out_grad")
    kv2_terms, out_terms, grad_kept = in_order(kv2_terms, out_terms, grad_kept)
    self_terms = meet(out_terms, kv2_terms)
    heads_grad = jnp.concatenate([grad_kept, grad_received], axis=0)
    heads_grad = after(heads_grad, down_sum, in_sums[0])

    def heads_back(part):
        count = half // LANES // 2
        return attend_back(
            no_length,
            qkv,
            qkv,
            qkv,
            [2 * one + part * count for one in self_columns],
            part * count,
            half // 2,
            heads_grad,
            attended,
            self_lse,
            tables,
            False,
            "self_attention_back",
            LANES,
            512,
        )

    early = heads_back(0)
    early = after(early, *in_sums)
    early, cross_terms = in_order(early, cross_terms)
    cross_sum = met(cross_terms, False)
    early, heads_grad = in_order(early, heads_grad)
    late = heads_back(1)
    late = arrived(late, in_sums[0])
    heads_back = [one for pair in zip(early, late) for one in pair]
    heads_back, cross_terms, early = in_order(heads_back, cross_terms, self_terms[1])
    self_terms = self_terms[0], early, self_terms[2]
    cross_sum = met(cross_terms, False)
    qkv_grad = jnp.concatenate(heads_back, axis=1)
    qkv_grads = qkv_grad, swap_dp(qkv_grad, 1)
    sent1 = times_turned(qkv_grad, full_first, 1, frames, D, 3 * half, jnp.bfloat16, "h1_back")
    sent1 = arrived(sent1, in_sums[1], cross_sum)
    sent1, qkv_grads = in_order(sent1, qkv_grads)
    received1 = swap_head(sent1)
    qkv_term = products(lefts1, qkv_grads, 768, "qkv_grad")
    qkv_grad, qkv_term = in_order(qkv_grad, qkv_term)
    qkv_sum = RowSum(qkv_term)
    own1 = times_turned(qkv_grad, full_first, 0, frames, D, 3 * half, jnp.float32, "h1_back")
    own1, self_terms = in_order(own1, self_terms)
    self_sum = met(self_terms, True)
    own1, received1 = after((own1, received1), *in_sums, cross_sum)
    normed_grad = own1 + received1.astype(jnp.float32)
    normed_back, gain_one = normalize_back(normed_grad, norm_gains[0], norm1_saved)
    input_grad = residual2 + normed_back

    gains = jnp.concatenate([gain_one[None], gain_two, gain_three], axis=0)
    gains = gains + swap_dp(gains, 1)
    gains = gains + swap_dp(gains, 2)
    gains_received = after(swap_dp(gains, 4), cross_sum, qkv_sum, self_sum, in_sums[1])
    gains = gains + gains_received
    gains_received = after(swap_dp(gains, 8), cross_sum, qkv_sum, self_sum)
    gains = gains + gains_received
    gains = gains + swap_head(gains)

    def joined(mine):
        lower, upper = ordered(mine, swap_head(mine))
        return jnp.stack([lower, upper], axis=-2)

    down_rows, own1 = in_order(down_sum.finish(), own1)
    down_other = swap_dp(down_rows, 1)
    down_block = jnp.concatenate(
        [
            jnp.where(core == 0, down_rows, down_other),
            jnp.where(core == 0, down_other, down_rows),
        ],
        axis=0,
    )
    crossing = [
        (2 * one + (one % 2), 2 * one + 1 - (one % 2)) for one in range(lax.axis_size("dp"))
    ]
    down_crossed = lax.ppermute(down_block, ("dp", "head"), crossing)
    down_out = jnp.where(core == side, down_block, down_crossed).astype(jnp.float32)
    in_parts = []
    for one in in_sums:
        mine = one.finish()
        in_parts += [mine, swap_head(mine)]
    in_out = assemble_in_grad(side, in_parts)
    qkv_out = joined(qkv_sum.finish().reshape(rows, 3, half)).reshape(rows, 3 * D)
    cross_rows = joined(cross_sum.finish()).astype(jnp.float32)
    self_rows = joined(self_sum.finish()).astype(jnp.float32)
    kv2_out = jnp.swapaxes(self_rows[:, 1].reshape(2, rows // 2, D), 0, 1).reshape(rows // 2, 2 * D)
    return (
        output[None],
        input_grad[None],
        gains,
        qkv_out.astype(jnp.float32),
        self_rows[:, 0],
        cross_rows[:, 1],
        kv2_out,
        cross_rows[:, 0],
        in_out,
        down_out,
    )


def body(*arrays):
    if lax.axis_size("dp") == 16 and lax.axis_size("head") == 2 and arrays[0].shape[0] == 1:
        return paired_body(*arrays)
    return general_body(*arrays)


def solution(mesh):
    placed = (
        P("dp", "head", None),
        P("dp", None, None),
        P("dp"),
        P(),
        P("dp", None),
        P("dp", None),
        P("dp", None),
        P("dp", None),
        P("dp", None),
        P("dp", None),
        P("dp", None),
        P("dp", "head", None),
    )
    return jax.shard_map(
        body,
        mesh=mesh,
        in_specs=placed,
        out_specs=(
            P("dp", "head", None),
            P("dp", "head", None),
            P(),
            P("dp", None),
            P("dp", None),
            P("dp", None),
            P("dp", None),
            P("dp", None),
            P("dp", None),
            P("dp", None),
        ),
        check_vma=False,
    )
```

```python
import functools

import jax
import jax.numpy as jnp
from jax import lax
from jax.experimental import pallas as pl
from jax.experimental.pallas import tpu as pltpu
from jax.sharding import PartitionSpec as P

D = 1536
HEADS = 24
HEAD_DIM = 64
FF = 6144
CTX = 768


EPSILON = 1e-05
MASKED = -1000000000.0


def normalize(values, gain_row):
    centred = values - jnp.mean(values, axis=-1, keepdims=True)
    inverse = lax.rsqrt(jnp.mean(centred * centred, axis=-1, keepdims=True) + EPSILON)
    scaled = centred * inverse
    return (scaled * gain_row, (scaled, inverse))


def normalize_back(grad_out, gain_row, saved):
    scaled, inverse = saved
    gain_term = jnp.sum(grad_out * scaled, axis=0)
    inner = grad_out * gain_row
    result = inverse * (
        inner
        - jnp.mean(inner, axis=-1, keepdims=True)
        - scaled * jnp.mean(inner * scaled, axis=-1, keepdims=True)
    )
    return (result, gain_term)


def rotary_tables(first_frame, frame_rows):
    half_dim = HEAD_DIM // 2
    frequencies = 10000.0 ** (-2.0 * jnp.arange(half_dim, dtype=jnp.float32) / HEAD_DIM)
    positions = (first_frame + jnp.arange(frame_rows, dtype=jnp.int32)).astype(jnp.float32)
    angles = positions[:, None] * frequencies[None, :]
    return (jnp.cos(angles)[:, None, None, :], jnp.sin(angles)[:, None, None, :])


def rotate(rotated_in, cosine_table, sine_table):
    half_dim = rotated_in.shape[-1] // 2
    first_half = rotated_in[..., :half_dim]
    second_half = rotated_in[..., half_dim:]
    return jnp.concatenate(
        [
            first_half * cosine_table - second_half * sine_table,
            second_half * cosine_table + first_half * sine_table,
        ],
        axis=-1,
    )


def times_transposed(left, weight):
    return lax.dot_general(
        left, weight, (((1,), (1,)), ((), ())), preferred_element_type=jnp.float32
    )


def weight_term(left, right, spread_columns=None):

    def term_rows():
        product = lax.dot_general(
            left, right, (((0,), (0,)), ((), ())), preferred_element_type=jnp.float32
        )
        if spread_columns is None:
            return product
        return spread_columns(product)

    return lax.psum_scatter(
        term_rows().astype(jnp.bfloat16), "dp", scatter_dimension=0, tiled=True
    ).astype(jnp.float32)


def attend_forward(queries, key_heads, values, key_valid):
    length_q, local_heads, head_dim = queries.shape
    block_rows = min(512, length_q)
    scale = head_dim ** (-0.5)

    def one_block(query_block):
        scores = (
            jnp.einsum("qhd,khd->hqk", query_block, key_heads, preferred_element_type=jnp.float32)
            * scale
        )
        scores = jnp.where(key_valid[None, None, :], scores, MASKED)
        row_max = jnp.max(scores, axis=-1, keepdims=True)
        exponent = jnp.exp(scores - row_max)
        row_total = jnp.sum(exponent, axis=-1, keepdims=True)
        weights = (exponent / row_total).astype(jnp.bfloat16)
        output = jnp.einsum("hqk,khd->qhd", weights, values, preferred_element_type=jnp.float32)
        return (output.astype(jnp.bfloat16), (row_max + jnp.log(row_total))[..., 0])

    blocks = queries.reshape(length_q // block_rows, block_rows, local_heads, head_dim)
    outputs, logsum = lax.map(one_block, blocks)
    return (outputs.reshape(length_q, local_heads, head_dim), logsum)


def attend_backward(queries, key_heads, values, key_valid, logsum, out_grad):
    length_q, local_heads, head_dim = queries.shape
    block_rows = logsum.shape[2]
    scale = head_dim ** (-0.5)
    query_blocks = queries.reshape(length_q // block_rows, block_rows, local_heads, head_dim)
    grad_blocks = out_grad.reshape(length_q // block_rows, block_rows, local_heads, head_dim)

    def one_block(carried, inputs):
        key_grad, value_grad = carried
        query_block, grad_block, logsum_block = inputs
        scores = (
            jnp.einsum("qhd,khd->hqk", query_block, key_heads, preferred_element_type=jnp.float32)
            * scale
        )
        scores = jnp.where(key_valid[None, None, :], scores, MASKED)
        probabilities = jnp.exp(scores - logsum_block[..., None])
        value_grad = value_grad + jnp.einsum(
            "hqk,qhd->khd",
            probabilities.astype(jnp.bfloat16),
            grad_block,
            preferred_element_type=jnp.float32,
        )
        prob_grad = jnp.einsum(
            "qhd,khd->hqk", grad_block, values, preferred_element_type=jnp.float32
        )
        row_delta = jnp.sum(probabilities * prob_grad, axis=-1, keepdims=True)
        score_grad = (probabilities * (prob_grad - row_delta)).astype(jnp.bfloat16)
        query_grad = (
            jnp.einsum("hqk,khd->qhd", score_grad, key_heads, preferred_element_type=jnp.float32)
            * scale
        )
        key_grad = (
            key_grad
            + jnp.einsum(
                "hqk,qhd->khd", score_grad, query_block, preferred_element_type=jnp.float32
            )
            * scale
        )
        return ((key_grad, value_grad), query_grad)

    zeros_kv = jnp.zeros(key_heads.shape, jnp.float32)
    carried, query_grads = lax.scan(
        one_block, (zeros_kv, zeros_kv), (query_blocks, grad_blocks, logsum)
    )
    return (query_grads.reshape(length_q, local_heads, head_dim), carried[0], carried[1])


def self_attention(inputs, gain_row, w_qkv, w_out, cosine_table, sine_table, head_count):
    frame_rows = inputs.shape[0]
    frames = frame_rows * head_count
    local_heads = HEADS // head_count
    normed, norm_saved = normalize(inputs, gain_row)
    normed_low = normed.astype(jnp.bfloat16)
    projected = jnp.dot(normed_low, w_qkv, preferred_element_type=jnp.float32).reshape(
        frame_rows, 3, HEADS, HEAD_DIM
    )
    turned = jnp.concatenate(
        [rotate(projected[:, :2], cosine_table, sine_table), projected[:, 2:]], axis=1
    )
    turned_low = turned.astype(jnp.bfloat16).reshape(frame_rows, 3, D)
    head_major = lax.all_to_all(
        turned_low, "head", split_axis=2, concat_axis=0, tiled=True
    ).reshape(frames, 3, local_heads, HEAD_DIM)
    everywhere = jnp.ones((frames,), dtype=jnp.bool_)
    attended, logsum = attend_forward(
        head_major[:, 0], head_major[:, 1], head_major[:, 2], everywhere
    )
    frame_major = lax.all_to_all(
        attended.reshape(frames, local_heads * HEAD_DIM),
        "head",
        split_axis=0,
        concat_axis=1,
        tiled=True,
    )
    branch = jnp.dot(frame_major, w_out, preferred_element_type=jnp.float32)
    return (inputs + branch, (normed_low, norm_saved, head_major, logsum, frame_major))


def cross_attention(
    inputs, gain_row, w_q2, w_kv2, w_out2, context_low, key_valid, head_count, head_index
):
    frame_rows = inputs.shape[0]
    frames = frame_rows * head_count
    local_heads = HEADS // head_count
    local_width = local_heads * HEAD_DIM
    prompt_rows = context_low.shape[0]
    normed, norm_saved = normalize(inputs, gain_row)
    normed_low = normed.astype(jnp.bfloat16)
    query_low = jnp.dot(normed_low, w_q2, preferred_element_type=jnp.float32).astype(jnp.bfloat16)
    query_heads = lax.all_to_all(
        query_low, "head", split_axis=1, concat_axis=0, tiled=True
    ).reshape(frames, local_heads, HEAD_DIM)
    own_columns = lax.dynamic_index_in_dim(
        w_kv2.reshape(CTX, 2, head_count, local_width), head_index, 2, keepdims=False
    ).reshape(CTX, 2 * local_width)
    key_value = jnp.dot(context_low, own_columns, preferred_element_type=jnp.float32).astype(
        jnp.bfloat16
    )
    key_value = key_value.reshape(prompt_rows, 2, local_heads, HEAD_DIM)
    attended, logsum = attend_forward(query_heads, key_value[:, 0], key_value[:, 1], key_valid)
    frame_major = lax.all_to_all(
        attended.reshape(frames, local_width), "head", split_axis=0, concat_axis=1, tiled=True
    )
    branch = jnp.dot(frame_major, w_out2, preferred_element_type=jnp.float32)
    return (inputs + branch, (normed_low, norm_saved, query_heads, key_value, logsum, frame_major))


def feed_forward(inputs, gain_row, w_in, w_down):
    normed, norm_saved = normalize(inputs, gain_row)
    normed_low = normed.astype(jnp.bfloat16)
    gate_up = jnp.dot(normed_low, w_in, preferred_element_type=jnp.float32)
    gate_part = gate_up[:, :FF]
    up_part = gate_up[:, FF:]
    hidden = (jax.nn.silu(gate_part) * up_part).astype(jnp.bfloat16)
    branch = jnp.dot(hidden, w_down, preferred_element_type=jnp.float32)
    return (inputs + branch, (normed_low, norm_saved, gate_part, up_part, hidden))


def forward(
    inputs, gains, weights, context_low, key_valid, cosine_table, sine_table, head_count, head_index
):
    w_qkv, w_out, w_q2, w_kv2, w_out2, w_in, w_down = weights
    first, saved_self = self_attention(
        inputs, gains[0], w_qkv, w_out, cosine_table, sine_table, head_count
    )
    second, saved_cross = cross_attention(
        first, gains[1], w_q2, w_kv2, w_out2, context_low, key_valid, head_count, head_index
    )
    third, saved_feed = feed_forward(second, gains[2], w_in, w_down)
    return (third, (saved_self, saved_cross, saved_feed))


def backward(saved, cotangent_row, gains, weights, key_valid, cosine_table, sine_table, head_count):
    full_qkv, full_out, full_q2, full_kv2, full_out2, full_in, full_down = weights
    saved_self, saved_cross, saved_feed = saved
    frame_rows = cotangent_row.shape[0]
    frames = frame_rows * head_count
    local_heads = HEADS // head_count
    local_width = local_heads * HEAD_DIM
    normed3, norm3_saved, gate_part, up_part, hidden = saved_feed
    hidden_grad = times_transposed(cotangent_row, full_down)
    sigmoid_gate = jax.nn.sigmoid(gate_part)
    silu_gate = gate_part * sigmoid_gate
    gate_grad = hidden_grad * up_part * sigmoid_gate * (1.0 + gate_part * (1.0 - sigmoid_gate))
    up_grad = hidden_grad * silu_gate
    gate_up_grad = jnp.concatenate([gate_grad, up_grad], axis=1).astype(jnp.bfloat16)
    normed_back, gain_three = normalize_back(
        times_transposed(gate_up_grad, full_in), gains[2], norm3_saved
    )
    residual_grad = cotangent_row.astype(jnp.float32) + normed_back
    normed2, norm2_saved, query_heads, key_value, cross_logsum, cross_frames = saved_cross
    cross_low = residual_grad.astype(jnp.bfloat16)
    cross_out_grad = times_transposed(cross_low, full_out2).astype(jnp.bfloat16)
    cross_grad_heads = lax.all_to_all(
        cross_out_grad, "head", split_axis=1, concat_axis=0, tiled=True
    )
    cross_grad_heads = cross_grad_heads.reshape(frames, local_heads, HEAD_DIM)
    query_grad, key_grad, value_grad = attend_backward(
        query_heads, key_value[:, 0], key_value[:, 1], key_valid, cross_logsum, cross_grad_heads
    )
    query_frames = lax.all_to_all(
        query_grad.astype(jnp.bfloat16).reshape(frames, local_width),
        "head",
        split_axis=0,
        concat_axis=1,
        tiled=True,
    )
    prompt_rows = key_value.shape[0]
    kv_grad = (
        jnp.stack([key_grad, value_grad], axis=1)
        .astype(jnp.bfloat16)
        .reshape(prompt_rows, 2 * local_width)
    )
    normed_back, gain_two = normalize_back(
        times_transposed(query_frames, full_q2), gains[1], norm2_saved
    )
    residual_grad = residual_grad + normed_back
    normed1, norm1_saved, head_major, self_logsum, self_frames = saved_self
    self_low = residual_grad.astype(jnp.bfloat16)
    self_out_grad = times_transposed(self_low, full_out).astype(jnp.bfloat16)
    self_grad_heads = lax.all_to_all(self_out_grad, "head", split_axis=1, concat_axis=0, tiled=True)
    self_grad_heads = self_grad_heads.reshape(frames, local_heads, HEAD_DIM)
    everywhere = jnp.ones((frames,), dtype=jnp.bool_)
    query_grad, key_grad, value_grad = attend_backward(
        head_major[:, 0],
        head_major[:, 1],
        head_major[:, 2],
        everywhere,
        self_logsum,
        self_grad_heads,
    )
    stacked = jnp.stack([query_grad, key_grad, value_grad], axis=1).astype(jnp.bfloat16)
    returned = lax.all_to_all(
        stacked.reshape(frames, 3, local_width), "head", split_axis=0, concat_axis=2, tiled=True
    )
    returned = returned.reshape(frame_rows, 3, HEADS, HEAD_DIM).astype(jnp.float32)
    unturned = jnp.concatenate(
        [rotate(returned[:, :2], cosine_table, -sine_table), returned[:, 2:]], axis=1
    )
    qkv_low = unturned.astype(jnp.bfloat16).reshape(frame_rows, 3 * D)
    normed_back, gain_one = normalize_back(
        times_transposed(qkv_low, full_qkv), gains[0], norm1_saved
    )
    input_grad = residual_grad + normed_back
    pairs = (
        (normed1, qkv_low),
        (self_frames, self_low),
        (normed2, query_frames),
        (None, kv_grad),
        (cross_frames, cross_low),
        (normed3, gate_up_grad),
        (hidden, cotangent_row),
    )
    return (input_grad, jnp.stack([gain_one, gain_two, gain_three]), pairs)


def general_body(
    tokens, context, lengths, norm_gains, w_qkv, w_out, w_q2, w_kv2, w_out2, w_in, w_down, cotangent
):
    head_count = lax.axis_size("head")
    head_index = lax.axis_index("head")
    frame_rows = tokens.shape[1]
    local_heads = HEADS // head_count
    local_width = local_heads * HEAD_DIM
    prompt_rows = context.shape[1]
    cosine_table, sine_table = rotary_tables(head_index * frame_rows, frame_rows)
    weights = (
        lax.all_gather(w_qkv, "dp", axis=0, tiled=True),
        lax.all_gather(w_out, "dp", axis=0, tiled=True),
        lax.all_gather(w_q2, "dp", axis=0, tiled=True),
        lax.all_gather(w_kv2, "dp", axis=0, tiled=True),
        lax.all_gather(w_out2, "dp", axis=0, tiled=True),
        lax.all_gather(w_in, "dp", axis=0, tiled=True),
        lax.all_gather(w_down, "dp", axis=0, tiled=True),
    )

    def valid_keys(sequence):
        return jnp.arange(prompt_rows, dtype=jnp.int32) < lengths[sequence]

    collected = [[] for position in range(7)]
    sequence = 0
    output, saved = forward(
        tokens[sequence].astype(jnp.float32),
        norm_gains,
        weights,
        context[sequence],
        valid_keys(sequence),
        cosine_table,
        sine_table,
        head_count,
        head_index,
    )
    outputs = [output.astype(jnp.bfloat16)]
    input_grad, gain_terms, pairs = backward(
        saved,
        cotangent[sequence],
        norm_gains,
        weights,
        valid_keys(sequence),
        cosine_table,
        sine_table,
        head_count,
    )
    input_grads = [input_grad]
    for position in range(7):
        left_part, right_part = pairs[position]
        if left_part is None:
            left_part = context[sequence]
        collected[position].append((left_part, right_part))
    owner_mask = (jnp.arange(head_count, dtype=jnp.int32) == head_index).astype(jnp.float32)

    def spread_heads(product):
        row_count = product.shape[0]
        placed = product.reshape(row_count, 2, 1, local_width) * owner_mask[None, None, :, None]
        return placed.reshape(row_count, 2 * D)

    grad_list = []
    for position in range(7):
        lefts = jnp.concatenate([pair[0] for pair in collected[position]], axis=0)
        rights = jnp.concatenate([pair[1] for pair in collected[position]], axis=0)
        lefts, rights = (lefts, rights)
        if position == 3:
            grad_list.append(weight_term(lefts, rights, spread_heads))
        else:
            grad_list.append(weight_term(lefts, rights))
    summed = (
        lax.psum(grad_list[0].astype(jnp.bfloat16), "head").astype(jnp.float32),
        lax.psum(grad_list[1].astype(jnp.bfloat16), "head").astype(jnp.float32),
        lax.psum(grad_list[2].astype(jnp.bfloat16), "head").astype(jnp.float32),
        lax.psum(grad_list[3].astype(jnp.bfloat16), "head").astype(jnp.float32),
        lax.psum(grad_list[4].astype(jnp.bfloat16), "head").astype(jnp.float32),
        lax.psum(grad_list[5].astype(jnp.bfloat16), "head").astype(jnp.float32),
        lax.psum(grad_list[6].astype(jnp.bfloat16), "head").astype(jnp.float32),
    )
    gains_grad = lax.psum(gain_terms, ("dp", "head"))
    return (
        jnp.stack(outputs),
        jnp.stack(input_grads),
        gains_grad,
        summed[0],
        summed[1],
        summed[2],
        summed[3],
        summed[4],
        summed[5],
        summed[6],
    )


LOG2E = 1.4426950408889634
LN2 = 0.6931471805599453
ROPE_BASE = 10000.0
LANES = 128
VMEM_BYTES = 48 * 1024 * 1024
SHARE = 1


def declared(flops, bytes_accessed, transcendentals):
    return pl.CostEstimate(
        flops=flops // SHARE,
        bytes_accessed=bytes_accessed // SHARE,
        transcendentals=transcendentals // SHARE,
    )


def in_order(*values):
    return lax.optimization_barrier(values)


def flipped(index_bit, count):
    return [(one, one ^ index_bit) for one in range(count)]


def swap_dp(value, index_bit):
    return lax.ppermute(value, "dp", flipped(index_bit, lax.axis_size("dp")))


def swap_head(value):
    return lax.ppermute(value, "head", [(0, 1), (1, 0)])


def take(value, index, axis):
    return lax.dynamic_index_in_dim(value, index, axis, keepdims=False)


def add_low(kept, received):
    return (kept.astype(jnp.float32) + received.astype(jnp.float32)).astype(jnp.bfloat16)


class RowSum:
    def __init__(self, term, z_first=False):
        place, count = lax.axis_index("dp"), lax.axis_size("dp")
        at_y, z_low, z_high = (place // 2) % 2, (place // 4) % 2, place // 8
        self.kept = None
        if z_first:
            self.stages = [(2, z_low, 4), (1, z_high, 8), (0, at_y, 2)]
            self.part = term.reshape(2, 2, 2, term.shape[0] // 8, term.shape[1])
            self.send()
            return
        self.stages = [(1, z_low, 4), (0, z_high, 8)]
        self.shape = (2, 2, term.shape[0] // 8, term.shape[1])
        self.received = lax.psum_scatter(
            term,
            "dp",
            scatter_dimension=0,
            axis_index_groups=[[one, one + 2] for one in range(count) if one % 4 < 2],
            tiled=True,
        )

    def send(self):
        axis, own, bit = self.stages.pop(0)
        self.received = swap_dp(take(self.part, 1 - own, axis), bit)
        self.kept = take(self.part, own, axis)

    def step(self):
        if self.kept is None:
            self.part = self.received.reshape(self.shape)
        else:
            self.part = add_low(self.kept, self.received)
        self.received = None
        if self.stages:
            self.send()

    def finish(self):
        while self.received is not None:
            self.step()
        return self.part


def arrived(value, *sums):
    tied = lax.optimization_barrier((value, *[one.received for one in sums]))
    for one, received in zip(sums, tied[1:]):
        one.received = received
    return tied[0]


def after(value, *sums):
    sums = [one for one in sums if one.received is not None]
    tied = lax.optimization_barrier((value, *[one.received for one in sums]))
    for one, received in zip(sums, tied[1:]):
        one.received = received
        one.step()
    return tied[0]


def place_bits():
    return (lax.axis_index("dp") % 2).reshape(1).astype(jnp.int32)


def turn_kernel(bits_ref, values_ref, mine_ref, theirs_ref):
    turned = values_ref[...].T
    block = turned.shape[0] // 16
    core = bits_ref[0]
    for at in range(8):
        first = turned[2 * at * block : (2 * at + 1) * block]
        second = turned[(2 * at + 1) * block : (2 * at + 2) * block]
        to = slice((at % 2 * 4 + at // 2) * block, (at % 2 * 4 + at // 2 + 1) * block)
        mine_ref[to, :] = jnp.where(core == 0, first, second)
        theirs_ref[to, :] = jnp.where(core == 0, second, first)


def turn_rows(values):
    frames, rows = values.shape
    step = min(frames, 512)
    grid_spec = pltpu.PrefetchScalarGridSpec(
        num_scalar_prefetch=1,
        grid=(frames // step,),
        in_specs=[pl.BlockSpec((step, rows), lambda n, s: (n, 0))],
        out_specs=[pl.BlockSpec((rows // 2, step), lambda n, s: (0, n))] * 2,
    )
    return pl.pallas_call(
        turn_kernel,
        name="turn_rows",
        grid_spec=grid_spec,
        out_shape=[jax.ShapeDtypeStruct((rows // 2, frames), jnp.bfloat16)] * 2,
        compiler_params=pltpu.CompilerParams(vmem_limit_bytes=VMEM_BYTES),
        cost_estimate=declared(0, 4 * frames * rows, 0),
    )(place_bits(), values)


def product_kernel(terms, *refs):
    total = jnp.dot(refs[0][...], refs[terms][...], preferred_element_type=jnp.float32)
    for at in range(1, terms):
        total += jnp.dot(refs[at][...], refs[terms + at][...], preferred_element_type=jnp.float32)
    out_refs = refs[2 * terms :]
    step, span = pl.program_id(0), pl.num_programs(0) // len(out_refs)
    for at, out_ref in enumerate(out_refs):

        @pl.when(step // span == at)
        def _():
            out_ref[...] = total.astype(jnp.bfloat16)


def parts_kernel(left_ref, left2_ref, *refs):
    out_ref = refs[-1]
    for at in range(3):

        @pl.when(pl.program_id(0) == at)
        def _():
            total = jnp.dot(left_ref[...], refs[at][...], preferred_element_type=jnp.float32)
            total += jnp.dot(
                left2_ref[...], refs[3 + at][...], preferred_element_type=jnp.float32
            )
            out_ref[...] = total.astype(jnp.bfloat16)


def products_of_parts(lefts, parts, parts2, name):
    rows, frames = lefts[0].shape
    width = parts[0].shape[1]
    left_spec = pl.BlockSpec((rows, frames), lambda n: (0, 0))
    right_spec = pl.BlockSpec((frames, width), lambda n: (0, 0))
    return pl.pallas_call(
        parts_kernel,
        name=name,
        grid=(3,),
        in_specs=[left_spec] * 2 + [right_spec] * 6,
        out_specs=pl.BlockSpec((rows, width), lambda n: (0, n)),
        out_shape=jax.ShapeDtypeStruct((rows, 3 * width), jnp.bfloat16),
        compiler_params=pltpu.CompilerParams(vmem_limit_bytes=VMEM_BYTES),
        cost_estimate=declared(
            flops=12 * rows * frames * width,
            bytes_accessed=4 * rows * frames + 12 * frames * width + 6 * rows * width,
            transcendentals=0,
        ),
    )(*lefts, *parts, *parts2)


def parts_back_kernel(*refs):
    right_ref, out_ref, total = refs[3:]
    step = pl.program_id(0)
    for at in range(3):

        @pl.when(step == at)
        def _():
            back = nt_dot(refs[at][...], right_ref[...])
            total[...] = back if at == 0 else total[...] + back

    @pl.when(step == 2)
    def _():
        out_ref[...] = total[...].astype(out_ref.dtype)


def parts_turned(parts, right, at, rows, start, kind, name):
    depth, width = right.shape[0], parts[0].shape[1]
    return pl.pallas_call(
        parts_back_kernel,
        name=name,
        grid=(3,),
        in_specs=[pl.BlockSpec((rows, width), lambda n: (at, 0))] * 3
        + [pl.BlockSpec((depth, width), lambda n: (0, start // width + n))],
        out_specs=pl.BlockSpec((rows, depth), lambda n: (0, 0)),
        out_shape=jax.ShapeDtypeStruct((rows, depth), kind),
        scratch_shapes=[pltpu.VMEM((rows, depth), jnp.float32)],
        compiler_params=pltpu.CompilerParams(vmem_limit_bytes=VMEM_BYTES),
        cost_estimate=declared(
            flops=6 * rows * depth * width,
            bytes_accessed=6 * rows * width + 6 * depth * width + 4 * rows * depth,
            transcendentals=0,
        ),
    )(*parts, right)


def products(lefts, rights, tile, name, pieces=1):
    frames = lefts[0].shape[1]
    blocks = rights[0].shape[0] // frames
    terms = len(lefts)
    rows, width = lefts[0].shape[0], rights[0].shape[1]
    span = width // tile // pieces

    def piece_at(piece):
        return lambda n: (0, jnp.clip(n - piece * span, 0, span - 1))

    def rows_at(block):
        return lambda n: (block, n)

    left_spec = pl.BlockSpec((rows, frames), lambda n: (0, 0))
    right_specs = [pl.BlockSpec((frames, tile), rows_at(at % blocks)) for at in range(terms)]
    out = pl.pallas_call(
        functools.partial(product_kernel, terms),
        name=name,
        grid=(width // tile,),
        in_specs=[left_spec] * terms + right_specs,
        out_specs=[pl.BlockSpec((rows, tile), piece_at(piece)) for piece in range(pieces)],
        out_shape=[jax.ShapeDtypeStruct((rows, width // pieces), jnp.bfloat16)] * pieces,
        compiler_params=pltpu.CompilerParams(vmem_limit_bytes=VMEM_BYTES),
        cost_estimate=declared(
            flops=2 * terms * rows * frames * width,
            bytes_accessed=2 * terms * (rows + width) * frames + 2 * rows * width,
            transcendentals=0,
        ),
    )(*lefts, *[rights[at // blocks] for at in range(terms)])
    return out if pieces > 1 else out[0]


def product_rows(left, right):
    return lax.dot_general(
        left, right, (((0,), (0,)), ((), ())), preferred_element_type=jnp.float32
    )


def turn(values, cosine, sine):
    width, quarter = values.shape[1], HEAD_DIM // 2
    lane = lax.broadcasted_iota(jnp.int32, values.shape, 1) % HEAD_DIM
    moved = jnp.where(
        lane < quarter,
        pltpu.roll(values, width - quarter, 1),
        pltpu.roll(values, quarter, 1),
    )
    if width > LANES:
        cosine = jnp.concatenate([cosine] * (width // LANES), axis=1)
        sine = jnp.concatenate([sine] * (width // LANES), axis=1)
    return values * cosine + moved * sine


def lane_tables(positions):
    half_dim = HEAD_DIM // 2
    frequencies = ROPE_BASE ** (-2.0 * jnp.arange(half_dim, dtype=jnp.float32) / HEAD_DIM)
    angles = positions.astype(jnp.float32)[:, None] * frequencies[None, :]
    cosine, sine = jnp.cos(angles), jnp.sin(angles)
    return (
        jnp.concatenate([cosine] * 4, axis=1),
        jnp.concatenate([-sine, sine, -sine, sine], axis=1),
    )


def qkv_kernel(h_ref, w_ref, cosine_ref, sine_ref, out_ref):
    width = out_ref.shape[1]
    projected = jnp.dot(h_ref[...], w_ref[...], preferred_element_type=jnp.float32)
    step = pl.program_id(0)
    third = pl.num_programs(0) // 3

    @pl.when(step < 2 * third)
    def _():
        scale = jnp.where(step < third, HEAD_DIM ** (-0.5), 1.0)
        for at in range(0, width, LANES):
            turned = turn(projected[:, at : at + LANES], cosine_ref[...], sine_ref[...])
            out_ref[:, at : at + LANES] = (turned * scale).astype(jnp.bfloat16)

    @pl.when(step >= 2 * third)
    def _():
        out_ref[...] = projected.astype(jnp.bfloat16)


def project_qkv(normed, weight, start, width, cosine, sine):
    rows, depth = normed.shape
    tile = 384
    return pl.pallas_call(
        qkv_kernel,
        name="qkv_projection",
        grid=(width // tile,),
        in_specs=[
            pl.BlockSpec((rows, depth), lambda n: (0, 0)),
            pl.BlockSpec((depth, tile), lambda n: (0, start // tile + n)),
            pl.BlockSpec((rows, LANES), lambda n: (0, 0)),
            pl.BlockSpec((rows, LANES), lambda n: (0, 0)),
        ],
        out_specs=pl.BlockSpec((rows, tile), lambda n: (0, n)),
        out_shape=jax.ShapeDtypeStruct((rows, width), jnp.bfloat16),
        compiler_params=pltpu.CompilerParams(vmem_limit_bytes=VMEM_BYTES),
        cost_estimate=declared(
            flops=2 * rows * depth * width,
            bytes_accessed=2 * (rows * depth + depth * width + rows * width),
            transcendentals=0,
        ),
    )(normed, weight, cosine, sine)


def nt_dot(left, right):
    return lax.dot_general(
        left, right, (((1,), (1,)), ((), ())), preferred_element_type=jnp.float32
    )


def attend_kernel(masked, length_ref, q_ref, k_ref, v_ref, out_ref, lse_ref):
    for head in range(q_ref.shape[1] // HEAD_DIM):
        lanes = slice(head * HEAD_DIM, (head + 1) * HEAD_DIM)
        scores = nt_dot(q_ref[:, lanes], k_ref[:, lanes])
        if masked:
            key = lax.broadcasted_iota(jnp.int32, scores.shape, 1)
            scores = jnp.where(key < length_ref[0], scores, MASKED)
        row_max = jnp.max(scores, axis=1, keepdims=True)
        exponent = jnp.exp2(scores * LOG2E - row_max * LOG2E)
        total = jnp.sum(exponent, axis=1, keepdims=True)
        mixed = jnp.dot(
            exponent.astype(jnp.bfloat16), v_ref[:, lanes], preferred_element_type=jnp.float32
        )
        out_ref[:, lanes] = (mixed / total).astype(jnp.bfloat16)
        lse_ref[:, lanes] = jnp.broadcast_to(
            row_max * LOG2E + jnp.log2(total), (row_max.shape[0], HEAD_DIM)
        )


def attend(length, queries, keys, values, width, columns, masked, name, span, block):
    rows, key_rows = queries.shape[0], keys.shape[0]
    pairs = width // span
    q_at, k_at, v_at = columns
    grid_spec = pltpu.PrefetchScalarGridSpec(
        num_scalar_prefetch=1,
        grid=(pairs, rows // block),
        in_specs=[
            pl.BlockSpec((block, span), lambda p, i, s: (i, q_at + p)),
            pl.BlockSpec((key_rows, span), lambda p, i, s: (0, k_at + p)),
            pl.BlockSpec((key_rows, span), lambda p, i, s: (0, v_at + p)),
        ],
        out_specs=[
            pl.BlockSpec((block, span), lambda p, i, s: (i, p)),
            pl.BlockSpec((block, span), lambda p, i, s: (i, p)),
        ],
    )
    return pl.pallas_call(
        functools.partial(attend_kernel, masked),
        name=name,
        grid_spec=grid_spec,
        out_shape=[
            jax.ShapeDtypeStruct((rows, width), jnp.bfloat16),
            jax.ShapeDtypeStruct((rows, width), jnp.float32),
        ],
        compiler_params=pltpu.CompilerParams(vmem_limit_bytes=VMEM_BYTES),
        cost_estimate=declared(
            flops=16 * rows * key_rows * width,
            bytes_accessed=8 * rows * width,
            transcendentals=rows * key_rows * width // HEAD_DIM,
        ),
    )(length, queries, keys, values)


def attend_back_kernel(
    masked,
    turned,
    length_ref,
    q_ref,
    k_ref,
    v_ref,
    grad_ref,
    out_ref,
    lse_ref,
    *rest,
):
    if turned:
        cosq_ref, sinq_ref, cosk_ref, sink_ref = rest[:4]
        rest = rest[4:]
    dq_ref, dk_ref, dv_ref, dk_sum, dv_sum = rest[-5:]
    step, steps = pl.program_id(1), pl.num_programs(1)

    @pl.when(step == 0)
    def _():
        dk_sum[...] = jnp.zeros_like(dk_sum)
        dv_sum[...] = jnp.zeros_like(dv_sum)

    lse_rows = lse_ref[...].T
    delta_rows = (grad_ref[...].astype(jnp.float32) * out_ref[...].astype(jnp.float32)).T
    dq_parts = []
    for head in range(q_ref.shape[1] // HEAD_DIM):
        lanes = slice(head * HEAD_DIM, (head + 1) * HEAD_DIM)
        query, key, value = q_ref[:, lanes], k_ref[:, lanes], v_ref[:, lanes]
        grad = grad_ref[:, lanes]
        scores = nt_dot(key, query)
        if masked:
            index = lax.broadcasted_iota(jnp.int32, scores.shape, 0)
            scores = jnp.where(index < length_ref[0], scores, MASKED)
        lse = lse_rows[head * HEAD_DIM : head * HEAD_DIM + 1, :]
        delta = jnp.sum(delta_rows[lanes, :], axis=0, keepdims=True)
        weight = jnp.exp2(scores * LOG2E - lse)
        dv_sum[:, lanes] += jnp.dot(
            weight.astype(jnp.bfloat16), grad, preferred_element_type=jnp.float32
        )
        weight_grad = nt_dot(value, grad)
        score_grad = (weight * (weight_grad - delta)).astype(jnp.bfloat16)
        dk_sum[:, lanes] += jnp.dot(score_grad, query, preferred_element_type=jnp.float32)
        dq_parts.append(product_rows(score_grad, key) * HEAD_DIM ** (-0.5))
    dq = jnp.concatenate(dq_parts, axis=1).astype(jnp.bfloat16)
    if turned:
        dq = turn(dq.astype(jnp.float32), cosq_ref[...], -sinq_ref[...]).astype(jnp.bfloat16)
    dq_ref[...] = dq

    @pl.when(step == steps - 1)
    def _():
        dk = dk_sum[...].astype(jnp.bfloat16)
        if turned:
            dk = turn(dk.astype(jnp.float32), cosk_ref[...], -sink_ref[...]).astype(jnp.bfloat16)
        dk_ref[...] = dk
        dv_ref[...] = dv_sum[...].astype(jnp.bfloat16)


def attend_back(
    length,
    queries,
    keys,
    values,
    columns,
    part,
    part_count,
    earlier,
    grad,
    outputs,
    lse,
    tables,
    masked,
    name,
    span,
    block,
):
    rows, key_rows = queries.shape[0], keys.shape[0]
    width = grad.shape[1]
    pairs = width // span // part_count
    grad_at = part * pairs
    q_at, k_at, v_at = columns
    by_grad = pl.BlockSpec((block, span), lambda p, i, s: (i, grad_at + p))
    by_key = pl.BlockSpec((key_rows, span), lambda p, i, s: (0, grad_at + p))
    in_specs = [
        pl.BlockSpec((block, span), lambda p, i, s: (i, q_at + grad_at + p)),
        pl.BlockSpec((key_rows, span), lambda p, i, s: (0, k_at + grad_at + p)),
        pl.BlockSpec((key_rows, span), lambda p, i, s: (0, v_at + grad_at + p)),
        by_grad,
        by_grad,
        by_grad,
    ]
    operands = [queries, keys, values, grad, outputs, lse]
    if tables is not None:
        cosine, sine = tables
        in_specs += [pl.BlockSpec((block, LANES), lambda p, i, s: (i, 0))] * 2
        in_specs += [pl.BlockSpec((key_rows, LANES), lambda p, i, s: (0, 0))] * 2
        operands += [cosine, sine, cosine, sine]
    aliases = {}
    if earlier is not None:
        aliases = {len(operands) + 1 + at: at for at in range(3)}
        in_specs += [pl.BlockSpec(memory_space=pl.ANY)] * 3
        operands += list(earlier)
    grid_spec = pltpu.PrefetchScalarGridSpec(
        num_scalar_prefetch=1,
        grid=(pairs, rows // block),
        in_specs=in_specs,
        out_specs=[by_grad, by_key, by_key],
        scratch_shapes=[pltpu.VMEM((key_rows, span), jnp.float32)] * 2,
    )
    return pl.pallas_call(
        functools.partial(attend_back_kernel, masked, tables is not None),
        name=name,
        grid_spec=grid_spec,
        out_shape=[
            jax.ShapeDtypeStruct((rows, width), jnp.bfloat16),
            jax.ShapeDtypeStruct((key_rows, width), jnp.bfloat16),
            jax.ShapeDtypeStruct((key_rows, width), jnp.bfloat16),
        ],
        input_output_aliases=aliases,
        compiler_params=pltpu.CompilerParams(vmem_limit_bytes=VMEM_BYTES),
        cost_estimate=declared(
            flops=40 * rows * key_rows * width // part_count,
            bytes_accessed=20 * rows * width // part_count,
            transcendentals=rows * key_rows * width // HEAD_DIM // part_count,
        ),
    )(length, *operands)


def feed_kernel(bits_ref, h_ref, cot_ref, in_ref, down_ref, *rest):
    mine_ref, theirs_ref, dgu_ref, out_ref, down, total = rest[-6:]
    step, steps = pl.program_id(0), pl.num_programs(0)
    depth, tile = h_ref.shape[1], down.shape[0]
    piece = down_ref.shape[0] // 2
    for at in range(4):
        place, part = at // 2, at % 2
        down[at * piece : (at + 1) * piece, :] = down_ref[
            place * piece : (place + 1) * piece, part * depth : (part + 1) * depth
        ]
    @pl.when(step == 0)
    def _():
        total[...] = jnp.zeros_like(total)

    chunk = h_ref.shape[0] // 2
    for at in range(2):
        rows = slice(at * chunk, (at + 1) * chunk)
        gate_up = jnp.dot(h_ref[rows, :], in_ref[...], preferred_element_type=jnp.float32)
        grad = nt_dot(cot_ref[rows, :], down[...])
        gate, up = gate_up[:, :tile], gate_up[:, tile:]
        sigmoid = jax.nn.sigmoid(gate)
        silu = gate * sigmoid
        hidden = (silu * up).astype(jnp.bfloat16)
        turned = hidden.T
        first, second = turned[: tile // 2], turned[tile // 2 :]
        mine_ref[:, rows] = jnp.where(bits_ref[0] == 0, first, second)
        theirs_ref[:, rows] = jnp.where(bits_ref[0] == 0, second, first)
        dgu_ref[rows, tile:] = (grad * silu).astype(jnp.bfloat16)
        dgu_ref[rows, :tile] = (
            grad * up * sigmoid * (1.0 + gate * (1.0 - sigmoid))
        ).astype(jnp.bfloat16)
        total[rows, :] += jnp.dot(hidden, down[...], preferred_element_type=jnp.float32)

    @pl.when(step == steps - 1)
    def _():
        out_ref[...] = total[...].astype(out_ref.dtype)


def feed(normed, cotangent, weights, half, earlier):
    rows, depth = normed.shape
    units = FF // 2
    steps = depth // 192
    tile = units // steps
    operands = [normed, cotangent, weights, weights]
    in_specs = [
        pl.BlockSpec((rows, depth), lambda n, s: (0, 0)),
        pl.BlockSpec((rows, depth), lambda n, s: (0, 0)),
        pl.BlockSpec((depth, 2 * tile), lambda n, s: (0, n)),
        pl.BlockSpec((depth // steps, 2 * depth), lambda n, s: (n, 2)),
    ]
    aliases = {}
    if earlier is not None:
        in_specs += [pl.BlockSpec(memory_space=pl.ANY)] * 3
        aliases = {5: 0, 6: 1, 7: 2}
        operands += list(earlier)

    def turned_at(n, s):
        return (n % 2 * 4 + n // 2, half)

    grid_spec = pltpu.PrefetchScalarGridSpec(
        num_scalar_prefetch=1,
        grid=(steps,),
        in_specs=in_specs,
        out_specs=[
            pl.BlockSpec((tile // 2, rows), turned_at),
            pl.BlockSpec((tile // 2, rows), turned_at),
            pl.BlockSpec((rows, 2 * tile), lambda n, s: (half, n)),
            pl.BlockSpec((rows, depth), lambda n, s: (0, 0)),
        ],
        scratch_shapes=[
            pltpu.VMEM((tile, depth), jnp.bfloat16),
            pltpu.VMEM((rows, depth), jnp.float32),
        ],
    )
    return pl.pallas_call(
        feed_kernel,
        name="feed_forward",
        grid_spec=grid_spec,
        out_shape=[
            jax.ShapeDtypeStruct((units // 2, 2 * rows), jnp.bfloat16),
            jax.ShapeDtypeStruct((units // 2, 2 * rows), jnp.bfloat16),
            jax.ShapeDtypeStruct((2 * rows, 2 * units), jnp.bfloat16),
            jax.ShapeDtypeStruct((rows, depth), jnp.bfloat16 if half else jnp.float32),
        ],
        input_output_aliases=aliases,
        compiler_params=pltpu.CompilerParams(vmem_limit_bytes=VMEM_BYTES),
        cost_estimate=declared(
            flops=8 * rows * depth * units,
            bytes_accessed=6 * depth * units + 6 * rows * units + 8 * rows * depth,
            transcendentals=rows * units,
        ),
    )(place_bits(), *operands)


def back_kernel(left_ref, right_ref, out_ref, total):
    step, steps = pl.program_id(0), pl.num_programs(0)

    @pl.when(step == 0)
    def _():
        total[...] = jnp.zeros_like(total)

    total[...] += nt_dot(left_ref[...], right_ref[...])

    @pl.when(step == steps - 1)
    def _():
        out_ref[...] = total[...].astype(out_ref.dtype)


def times_turned(left, right, at, rows, start, width, kind, name):
    depth = right.shape[0]
    tile = 1536 if width % 1536 == 0 else 768
    return pl.pallas_call(
        back_kernel,
        name=name,
        grid=(width // tile,),
        in_specs=[
            pl.BlockSpec((rows, tile), lambda n: (at, n)),
            pl.BlockSpec((depth, tile), lambda n: (0, start // tile + n)),
        ],
        out_specs=pl.BlockSpec((rows, depth), lambda n: (0, 0)),
        out_shape=jax.ShapeDtypeStruct((rows, depth), kind),
        scratch_shapes=[pltpu.VMEM((rows, depth), jnp.float32)],
        compiler_params=pltpu.CompilerParams(vmem_limit_bytes=VMEM_BYTES),
        cost_estimate=declared(
            flops=2 * rows * depth * width,
            bytes_accessed=2 * rows * width + 2 * depth * width + 4 * rows * depth,
            transcendentals=0,
        ),
    )(left, right)


def norm_back_into(total, x_ref, gain_ref, residual_ref, sum_ref, low_ref, term_ref):
    chunk = 128
    term = jnp.zeros(term_ref.shape, jnp.float32)
    for at in range(0, total.shape[0], chunk):
        rows = slice(at, at + chunk)
        grad = total[rows, :]
        values = x_ref[rows, :]
        centred = values - jnp.mean(values, axis=1, keepdims=True)
        inverse = lax.rsqrt(jnp.mean(centred * centred, axis=1, keepdims=True) + EPSILON)
        scaled = centred * inverse
        term += jnp.sum(grad * scaled, axis=0, keepdims=True)
        inner = grad * gain_ref[...]
        back = inverse * (
            inner
            - jnp.mean(inner, axis=1, keepdims=True)
            - scaled * jnp.mean(inner * scaled, axis=1, keepdims=True)
        )
        summed = residual_ref[rows, :].astype(jnp.float32) + back
        sum_ref[rows, :] = summed
        low_ref[rows, :] = summed.astype(jnp.bfloat16)
    term_ref[...] = term


def feed_back_kernel(
    left_ref, right_ref, other_ref, x_ref, gain_ref, residual_ref, sum_ref, low_ref, term_ref, total
):
    step, steps = pl.program_id(0), pl.num_programs(0)

    @pl.when(step == 0)
    def _():
        total[...] = other_ref[...].astype(jnp.float32)

    total[...] += nt_dot(left_ref[...], right_ref[...])

    @pl.when(step == steps - 1)
    def _():
        norm_back_into(total, x_ref, gain_ref, residual_ref, sum_ref, low_ref, term_ref)


def feed_back(left, right, other, values, gain, residual):
    rows, depth = values.shape
    tile = 1536
    whole = pl.BlockSpec((rows, depth), lambda n: (0, 0))
    line = pl.BlockSpec((1, depth), lambda n: (0, 0))
    return pl.pallas_call(
        feed_back_kernel,
        name="h3_back_norm",
        grid=(FF // tile,),
        in_specs=[
            pl.BlockSpec((rows, tile), lambda n: (0, n)),
            pl.BlockSpec((depth, tile), lambda n: (0, n)),
            whole,
            whole,
            line,
            whole,
        ],
        out_specs=[whole, whole, line],
        out_shape=[
            jax.ShapeDtypeStruct((rows, depth), jnp.float32),
            jax.ShapeDtypeStruct((rows, depth), jnp.bfloat16),
            jax.ShapeDtypeStruct((1, depth), jnp.float32),
        ],
        scratch_shapes=[pltpu.VMEM((rows, depth), jnp.float32)],
        compiler_params=pltpu.CompilerParams(vmem_limit_bytes=VMEM_BYTES),
        cost_estimate=declared(2 * rows * depth * FF, 2 * depth * FF, 0),
    )(left, right, other, values, gain, residual)


def cross_back_kernel(
    length_ref,
    low_ref,
    out_weight_ref,
    q_weight_ref,
    q_ref,
    k_ref,
    v_ref,
    out_ref,
    lse_ref,
    x_ref,
    gain_ref,
    residual_ref,
    dq_ref,
    dk_ref,
    dv_ref,
    sum_ref,
    new_low_ref,
    term_ref,
    total,
):
    step, steps = pl.program_id(0), pl.num_programs(0)
    grad_all = nt_dot(low_ref[...], out_weight_ref[...])
    lse_rows = lse_ref[...].T
    delta_rows = (grad_all * out_ref[...].astype(jnp.float32)).T
    grad_all = grad_all.astype(jnp.bfloat16)
    for head in range(q_ref.shape[1] // HEAD_DIM):
        lanes = slice(head * HEAD_DIM, (head + 1) * HEAD_DIM)
        query, key, value = q_ref[:, lanes], k_ref[:, lanes], v_ref[:, lanes]
        grad = grad_all[:, lanes]
        scores = nt_dot(key, query)
        index = lax.broadcasted_iota(jnp.int32, scores.shape, 0)
        scores = jnp.where(index < length_ref[0], scores, MASKED)
        lse = lse_rows[head * HEAD_DIM : head * HEAD_DIM + 1, :]
        delta = jnp.sum(delta_rows[lanes, :], axis=0, keepdims=True)
        weight = jnp.exp2(scores * LOG2E - lse)
        dv = jnp.dot(weight.astype(jnp.bfloat16), grad, preferred_element_type=jnp.float32)
        dv_ref[:, lanes] = dv.astype(jnp.bfloat16)
        score_grad = (weight * (nt_dot(value, grad) - delta)).astype(jnp.bfloat16)
        dk = jnp.dot(score_grad, query, preferred_element_type=jnp.float32)
        dk_ref[:, lanes] = dk.astype(jnp.bfloat16)
        dq = product_rows(score_grad, key) * HEAD_DIM ** (-0.5)
        dq_ref[:, lanes] = dq.astype(jnp.bfloat16)
    back = nt_dot(dq_ref[...], q_weight_ref[...])

    @pl.when(step == 0)
    def _():
        total[...] = back

    @pl.when(step > 0)
    def _():
        total[...] += back

    @pl.when(step == steps - 1)
    def _():
        norm_back_into(total, x_ref, gain_ref, residual_ref, sum_ref, new_low_ref, term_ref)


def cross_back(length, low, out_weight, q_weight, query, key, value, outputs, lse, values, gain, residual):
    rows, depth = values.shape
    key_rows = key.shape[0]
    tile = 384
    steps = depth // tile
    whole = pl.BlockSpec((rows, depth), lambda n, s: (0, 0))
    line = pl.BlockSpec((1, depth), lambda n, s: (0, 0))
    by_query = pl.BlockSpec((rows, tile), lambda n, s: (0, n))
    by_key = pl.BlockSpec((key_rows, tile), lambda n, s: (0, n))
    grid_spec = pltpu.PrefetchScalarGridSpec(
        num_scalar_prefetch=1,
        grid=(steps,),
        in_specs=[
            whole,
            pl.BlockSpec((tile, depth), lambda n, s: (n, 0)),
            pl.BlockSpec((depth, tile), lambda n, s: (0, n)),
            by_query,
            by_key,
            by_key,
            by_query,
            by_query,
            whole,
            line,
            whole,
        ],
        out_specs=[by_query, by_key, by_key, whole, whole, line],
        scratch_shapes=[pltpu.VMEM((rows, depth), jnp.float32)],
    )
    return pl.pallas_call(
        cross_back_kernel,
        name="cross_back",
        grid_spec=grid_spec,
        out_shape=[
            jax.ShapeDtypeStruct((rows, depth), jnp.bfloat16),
            jax.ShapeDtypeStruct((key_rows, depth), jnp.bfloat16),
            jax.ShapeDtypeStruct((key_rows, depth), jnp.bfloat16),
            jax.ShapeDtypeStruct((rows, depth), jnp.float32),
            jax.ShapeDtypeStruct((rows, depth), jnp.bfloat16),
            jax.ShapeDtypeStruct((1, depth), jnp.float32),
        ],
        compiler_params=pltpu.CompilerParams(vmem_limit_bytes=VMEM_BYTES),
        cost_estimate=declared(4 * rows * depth * depth, 8 * depth * depth, 0),
    )(length, low, out_weight, q_weight, query, key, value, outputs, lse, values, gain, residual)


def split_back_kernel(side_ref, left_ref, right_ref, kept_ref, sent_ref):
    half = kept_ref.shape[1]
    lower = nt_dot(left_ref[...], right_ref[:half, :]).astype(jnp.bfloat16)
    upper = nt_dot(left_ref[...], right_ref[half:, :]).astype(jnp.bfloat16)
    kept_ref[...] = jnp.where(side_ref[0] == 0, lower, upper)
    sent_ref[...] = jnp.where(side_ref[0] == 0, upper, lower)


def split_back(side, left, weights):
    rows, depth = left.shape
    return pl.pallas_call(
        split_back_kernel,
        name="attention_grad",
        grid=(1,),
        in_specs=[
            pl.BlockSpec(memory_space=pltpu.SMEM),
            pl.BlockSpec((rows, depth), lambda n: (0, 0)),
            pl.BlockSpec((depth, depth), lambda n: (0, 0)),
        ],
        out_specs=[pl.BlockSpec((rows, depth // 2), lambda n: (0, 0))] * 2,
        out_shape=[jax.ShapeDtypeStruct((rows, depth // 2), jnp.bfloat16)] * 2,
        compiler_params=pltpu.CompilerParams(vmem_limit_bytes=VMEM_BYTES),
        cost_estimate=declared(2 * rows * depth * depth, 2 * depth * depth, 0),
    )(side.reshape(1).astype(jnp.int32), left, weights)


def in_grad_kernel(side_ref, *refs):
    out_ref = refs[-1]
    unit = refs[0].shape[1] // 8
    for part in range(2):
        mine_ref, theirs_ref = refs[2 * part], refs[2 * part + 1]
        for at in range(8):
            mine = mine_ref[:, at * unit : (at + 1) * unit].astype(jnp.float32)
            theirs = theirs_ref[:, at * unit : (at + 1) * unit].astype(jnp.float32)
            tile, gate_or_up = part * 4 + at // 2, at % 2
            to = (gate_or_up * 8 + tile) * 2 * unit
            out_ref[:, to : to + unit] = jnp.where(side_ref[0] == 0, mine, theirs)
            out_ref[:, to + unit : to + 2 * unit] = jnp.where(side_ref[0] == 0, theirs, mine)


def assemble_in_grad(side, parts):
    rows, width = parts[0].shape
    whole = pl.BlockSpec(memory_space=pltpu.VMEM)
    return pl.pallas_call(
        in_grad_kernel,
        name="in_grad_rows",
        in_specs=[pl.BlockSpec(memory_space=pltpu.SMEM)] + [whole] * 4,
        out_specs=whole,
        out_shape=jax.ShapeDtypeStruct((rows, 4 * width), jnp.float32),
        compiler_params=pltpu.CompilerParams(vmem_limit_bytes=VMEM_BYTES),
        cost_estimate=declared(0, 16 * rows * width, 0),
    )(side.reshape(1).astype(jnp.int32), *parts)


def pack_kernel(side_ref, out_w_ref, qkv_ref, q2_ref, out2_ref, kv2_ref, packed_ref):
    left = side_ref[0] == 0
    half = q2_ref.shape[1] // 2
    rows = kv2_ref.shape[0]
    whole = out_w_ref.shape[1]
    packed_ref[:, :whole] = out_w_ref[...]

    def chosen(ref, at):
        return jnp.where(left, ref[:, at : at + half], ref[:, at + half : at + 2 * half])

    for one in range(3):
        at = whole + one * half
        packed_ref[:, at : at + half] = chosen(qkv_ref, 2 * one * half)
    for one, ref in enumerate((q2_ref, out2_ref)):
        at = whole + (3 + one) * half
        packed_ref[:, at : at + half] = chosen(ref, 0)
    at = whole + 5 * half
    packed_ref[:rows, at : at + half] = chosen(kv2_ref, 0)
    packed_ref[rows:, at : at + half] = chosen(kv2_ref, 2 * half)


def pack_first(side, w_out, w_qkv, w_q2, w_out2, w_kv2):
    rows, depth = w_out.shape
    whole = pl.BlockSpec(memory_space=pltpu.VMEM)
    return pl.pallas_call(
        pack_kernel,
        name="pack_first",
        in_specs=[pl.BlockSpec(memory_space=pltpu.SMEM)] + [whole] * 5,
        out_specs=whole,
        out_shape=jax.ShapeDtypeStruct((rows, 4 * depth), jnp.bfloat16),
        compiler_params=pltpu.CompilerParams(vmem_limit_bytes=VMEM_BYTES),
        cost_estimate=declared(0, 24 * rows * depth, 0),
    )(side.reshape(1).astype(jnp.int32), w_out, w_qkv, w_q2, w_out2, w_kv2)


def paired_body(
    tokens, context, lengths, norm_gains, w_qkv, w_out, w_q2, w_kv2, w_out2, w_in, w_down, cotangent
):
    place, side = lax.axis_index("dp"), lax.axis_index("head")
    core = place % 2
    on_left = side == 0
    own = tokens[0]
    frames = own.shape[0]
    rows = w_qkv.shape[0]
    half = D // 2
    units = w_down.shape[0]

    def ordered(mine, theirs):
        return jnp.where(on_left, mine, theirs), jnp.where(on_left, theirs, mine)

    full_first = lax.all_gather(
        pack_first(side, w_out, w_qkv, w_q2, w_out2, w_kv2), "dp", axis=0, tiled=True
    )
    full_out = full_first[:, :D]
    own_halves = full_first[:, D + 3 * half : D + 5 * half]
    core_rows = swap_head(take(own_halves.reshape(2, half, D), core, 0))
    kv2_half = full_first[:, D + 5 * half :].reshape(rows // 6, 2, rows // 2, half)
    kv2_weights = [kv2_half[:, one].reshape(D // 2, half) for one in range(2)]
    in_half = take(w_in.reshape(rows, 2, 8, 2, units), side, 3)
    in_half = jnp.swapaxes(in_half, 1, 2).reshape(rows, FF)
    down_parts = w_down.reshape(2, units // 2, D)
    down_received = swap_dp(take(down_parts, 1 - core, 0), 1)
    down_half = jnp.where(core == side, take(down_parts, core, 0), down_received)
    full_feed = lax.all_gather(
        jnp.concatenate([in_half, down_half[:rows], down_half[rows:]], axis=1),
        "dp",
        axis=0,
        tiled=True,
    )
    full_in = full_feed[:, :FF]

    both_tokens = jnp.concatenate([own, swap_head(own)], axis=0).astype(jnp.float32)
    own_cot, other_cot = cotangent[0], swap_head(cotangent[0])
    both_cot = jnp.concatenate([own_cot, other_cot], axis=0)
    frame = jnp.arange(frames, dtype=jnp.int32)
    tables = lane_tables(
        jnp.concatenate([side * frames + frame, (1 - side) * frames + frame])
    )
    normed1 = normalize(both_tokens, norm_gains[0])[0].astype(jnp.bfloat16)
    inputs = own.astype(jnp.float32)
    norm1_saved = normalize(inputs, norm_gains[0])[1]
    qkv = project_qkv(normed1, full_first, D, 3 * half, *tables)
    no_length = jnp.zeros((1,), jnp.int32)
    pairs = half // (2 * LANES)
    self_columns = (0, pairs, 2 * pairs)
    attended, self_lse = attend(
        no_length, qkv, qkv, qkv, half, self_columns, False, "self_attention", 2 * LANES, 512
    )
    key_value = jnp.stack(
        [
            jnp.dot(context[0], weight, preferred_element_type=jnp.float32).astype(jnp.bfloat16)
            for weight in kv2_weights
        ]
    )
    attended, core_rows, key_value_other = in_order(attended, core_rows, swap_head(key_value))
    attended_other = swap_head(attended[frames:])
    sibling_rows = swap_dp(core_rows, 1)
    other_halves = jnp.where(
        core == 0,
        jnp.concatenate([core_rows, sibling_rows], axis=0),
        jnp.concatenate([sibling_rows, core_rows], axis=0),
    )
    full_q2, full_out2 = in_order(
        *[
            jnp.concatenate(
                ordered(own_halves[:, at : at + half], other_halves[:, at : at + half]), axis=1
            )
            for at in (0, half)
        ]
    )
    attended_frames = jnp.concatenate(ordered(attended[:frames], attended_other), axis=1)
    first = inputs + jnp.dot(attended_frames, full_out, preferred_element_type=jnp.float32)

    normed2, norm2_saved = normalize(first, norm_gains[1])
    normed2 = normed2.astype(jnp.bfloat16)
    query2 = jnp.dot(normed2, full_q2, preferred_element_type=jnp.float32)
    query2 = (query2.astype(jnp.bfloat16) * HEAD_DIM ** (-0.5)).astype(jnp.bfloat16)
    key2, value2 = jnp.concatenate(ordered(key_value, key_value_other), axis=2)
    crossed, cross_lse = attend(
        lengths, query2, key2, value2, D, (0, 0, 0), True, "cross_attention", 3 * LANES, frames
    )
    second = first + jnp.dot(crossed, full_out2, preferred_element_type=jnp.float32)

    def left_pair(values):
        mine, theirs = turn_rows(values)
        return mine, swap_dp(theirs, 1)

    lefts1 = left_pair(normed1)
    lefts_out = left_pair(attended_frames)
    lefts2 = left_pair(normed2)
    lefts_cross = left_pair(crossed)
    lefts_context = left_pair(context[0])
    cots = both_cot, swap_dp(both_cot, 1)

    normed3, norm3_saved = normalize(second, norm_gains[2])
    normed3 = normed3.astype(jnp.bfloat16)
    other3 = swap_head(normed3)
    lefts3 = left_pair(normed3)
    *fed, own_out = feed(normed3, own_cot, full_feed, 0, None)
    fed, lefts1, lefts_out, lefts2, lefts3, lefts_cross, lefts_context, cots = in_order(
        fed, lefts1, lefts_out, lefts2, lefts3, lefts_cross, lefts_context, cots
    )
    hidden, hidden_theirs, dgu, other_out = feed(other3, other_cot, full_feed, 1, fed)
    lefts3_late = left_pair(other3)
    lefts3 = lefts3[0], lefts3_late[0], lefts3[1], lefts3_late[1]
    hidden, dgu = in_order(hidden, dgu)
    hiddens = hidden, swap_dp(hidden_theirs, 1)
    dgus = dgu, swap_dp(dgu, 1)
    sent3 = times_turned(dgu, full_feed, 1, frames, 0, FF, jnp.bfloat16, "h3_back")
    hiddens, sent3 = in_order(hiddens, sent3)
    received3 = swap_head(sent3)
    down_term = products(hiddens, cots, 512, "down_grad")
    dgus, down_term = in_order(dgus, down_term)
    down_sum = RowSum(down_term)
    in_terms = products(lefts3, dgus, 512, "in_grad", 2)
    in_terms, dgu = in_order(in_terms, dgu)
    residual3, cross_low, gain_three = feed_back(
        dgu, full_feed, received3, second, norm_gains[2:], own_cot
    )
    cross_low, in_terms = in_order(cross_low, in_terms)
    in_sums = [RowSum(one) for one in in_terms]
    cross_low = after(cross_low, down_sum)
    received_out = swap_head(other_out)

    query2_grad, key2_grad, value2_grad, residual2, self_low, gain_two = cross_back(
        lengths,
        cross_low,
        full_out2,
        full_q2,
        query2,
        key2,
        value2,
        crossed,
        cross_lse,
        first,
        norm_gains[1:2],
        residual3,
    )
    grad_kept, grad_sent = split_back(side, self_low, full_first)
    grad_kept, received_out = in_order(grad_kept, received_out)
    grad_kept = after(grad_kept, down_sum)
    grad_received = swap_head(grad_sent)
    kv2_grad = jnp.concatenate([key2_grad, value2_grad], axis=1)

    def square(lefts, right, name):
        return products(lefts, (right, swap_dp(right, 1)), 512, name)

    def meet(lower, upper):
        sent, middle = jnp.where(on_left, upper, lower), lower.shape[0] // 2
        return (
            jnp.where(on_left, lower, upper),
            swap_head(sent[:middle]),
            swap_head(sent[middle:]),
        )

    def met(terms, z_first):
        return RowSum(add_low(terms[0], jnp.concatenate(terms[1:], axis=0)), z_first)

    query2_grad, cross_low, kv2_grad, grad_kept = in_order(
        query2_grad, cross_low, kv2_grad, grad_kept
    )
    out2_terms = square(lefts_cross, cross_low, "out2_grad")
    q2_terms = square(lefts2, query2_grad, "q2_grad")
    out2_terms, q2_terms, self_low, kv2_grad = in_order(out2_terms, q2_terms, self_low, kv2_grad)
    cross_terms = meet(out2_terms, q2_terms)
    kv2_terms = square(lefts_context, kv2_grad, "kv2_grad").reshape(8 * rows, D)
    out_terms = square(lefts_out, self_low, "out_grad")
    kv2_terms, out_terms, grad_kept = in_order(kv2_terms, out_terms, grad_kept)
    self_terms = meet(out_terms, kv2_terms)
    heads_grad = jnp.concatenate([grad_kept, grad_received], axis=0)
    heads_grad = after(heads_grad, down_sum, in_sums[0])

    def heads_back(part, earlier):
        return attend_back(
            no_length,
            qkv,
            qkv,
            qkv,
            [2 * one for one in self_columns],
            part,
            2,
            earlier,
            heads_grad,
            attended,
            self_lse,
            tables,
            False,
            "self_attention_back",
            LANES,
            512,
        )

    early = heads_back(0, None)
    early = after(early, *in_sums)
    early, cross_terms = in_order(early, cross_terms)
    cross_part = add_low(cross_terms[0], jnp.concatenate(cross_terms[1:], axis=0))
    early, cross_part = in_order(early, cross_part)
    cross_sum = RowSum(cross_part)
    qkv_grads = heads_back(1, early)
    siblings = [swap_dp(one, 1) for one in qkv_grads]
    sent1 = parts_turned(qkv_grads, full_first, 1, frames, D, jnp.bfloat16, "h1_back")
    sent1, siblings, self_early = in_order(sent1, siblings, self_terms[1])
    received1 = swap_head(sent1)
    qkv_term = products_of_parts(lefts1, qkv_grads, siblings, "qkv_grad")
    qkv_sum = RowSum(qkv_term)
    qkv_grads, qkv_term, self_late = in_order(qkv_grads, qkv_term, self_terms[2])
    self_sum = met((self_terms[0], self_early, self_late), True)
    qkv_grads = after(qkv_grads, *in_sums, cross_sum)
    qkv_grads, received1 = in_order(qkv_grads, received1)
    own1 = parts_turned(qkv_grads, full_first, 0, frames, D, jnp.float32, "h1_back")
    own1, received_out = in_order(own1, received_out)
    output = (second + own_out + received_out.astype(jnp.float32)).astype(jnp.bfloat16)
    normed_grad = own1 + received1.astype(jnp.float32)
    normed_back, gain_one = normalize_back(normed_grad, norm_gains[0], norm1_saved)
    input_grad = residual2 + normed_back

    gains = jnp.concatenate([gain_one[None], gain_two, gain_three], axis=0)
    gains = after(gains, qkv_sum, self_sum)
    gains = gains + swap_dp(gains, 1)
    gains = gains + swap_dp(gains, 2)
    gains_received = after(swap_dp(gains, 4), in_sums[1], cross_sum)
    gains = gains + gains_received
    gains_received = after(swap_dp(gains, 8), qkv_sum, self_sum)
    gains = gains + gains_received
    gains_received = after(swap_head(gains), cross_sum, qkv_sum, self_sum)
    gains = gains + gains_received

    def joined(mine):
        lower, upper = ordered(mine, swap_head(mine))
        return jnp.stack([lower, upper], axis=-2)

    down_rows, own1 = in_order(down_sum.finish(), own1)
    down_other = swap_dp(down_rows, 1)
    down_block = jnp.concatenate(
        [
            jnp.where(core == 0, down_rows, down_other),
            jnp.where(core == 0, down_other, down_rows),
        ],
        axis=0,
    )
    crossing = [
        (2 * one + (one % 2), 2 * one + 1 - (one % 2)) for one in range(lax.axis_size("dp"))
    ]
    down_crossed = lax.ppermute(down_block, ("dp", "head"), crossing)
    down_out = jnp.where(core == side, down_block, down_crossed).astype(jnp.float32)
    in_parts = []
    for one in in_sums:
        mine = one.finish()
        in_parts += [mine, swap_head(mine)]
    in_out = assemble_in_grad(side, in_parts)
    qkv_out = joined(qkv_sum.finish().reshape(rows, 3, half)).reshape(rows, 3 * D)
    cross_rows = joined(cross_sum.finish()).astype(jnp.float32)
    self_rows = joined(self_sum.finish()).astype(jnp.float32)
    kv2_out = self_rows[:, 1].reshape(rows // 2, 2 * D)
    return (
        output[None],
        input_grad[None],
        gains,
        qkv_out.astype(jnp.float32),
        self_rows[:, 0],
        cross_rows[:, 1],
        kv2_out,
        cross_rows[:, 0],
        in_out,
        down_out,
    )


def body(*arrays):
    if lax.axis_size("dp") == 16 and lax.axis_size("head") == 2 and arrays[0].shape[0] == 1:
        return paired_body(*arrays)
    return general_body(*arrays)


def solution(mesh):
    placed = (
        P("dp", "head", None),
        P("dp", None, None),
        P("dp"),
        P(),
        P("dp", None),
        P("dp", None),
        P("dp", None),
        P("dp", None),
        P("dp", None),
        P("dp", None),
        P("dp", None),
        P("dp", "head", None),
    )
    return jax.shard_map(
        body,
        mesh=mesh,
        in_specs=placed,
        out_specs=(
            P("dp", "head", None),
            P("dp", "head", None),
            P(),
            P("dp", None),
            P("dp", None),
            P("dp", None),
            P("dp", None),
            P("dp", None),
            P("dp", None),
            P("dp", None),
        ),
        check_vma=False,
    )
```

```python
import functools

import jax
import jax.numpy as jnp
from jax import lax
from jax.experimental import pallas as pl
from jax.experimental.pallas import tpu as pltpu
from jax.sharding import PartitionSpec as P

D = 1536
HEADS = 24
HEAD_DIM = 64
FF = 6144
CTX = 768


EPSILON = 1e-05
MASKED = -1000000000.0


def normalize(values, gain_row):
    centred = values - jnp.mean(values, axis=-1, keepdims=True)
    inverse = lax.rsqrt(jnp.mean(centred * centred, axis=-1, keepdims=True) + EPSILON)
    scaled = centred * inverse
    return (scaled * gain_row, (scaled, inverse))


def normalize_back(grad_out, gain_row, saved):
    scaled, inverse = saved
    gain_term = jnp.sum(grad_out * scaled, axis=0)
    inner = grad_out * gain_row
    result = inverse * (
        inner
        - jnp.mean(inner, axis=-1, keepdims=True)
        - scaled * jnp.mean(inner * scaled, axis=-1, keepdims=True)
    )
    return (result, gain_term)


def rotary_tables(first_frame, frame_rows):
    half_dim = HEAD_DIM // 2
    frequencies = 10000.0 ** (-2.0 * jnp.arange(half_dim, dtype=jnp.float32) / HEAD_DIM)
    positions = (first_frame + jnp.arange(frame_rows, dtype=jnp.int32)).astype(jnp.float32)
    angles = positions[:, None] * frequencies[None, :]
    return (jnp.cos(angles)[:, None, None, :], jnp.sin(angles)[:, None, None, :])


def rotate(rotated_in, cosine_table, sine_table):
    half_dim = rotated_in.shape[-1] // 2
    first_half = rotated_in[..., :half_dim]
    second_half = rotated_in[..., half_dim:]
    return jnp.concatenate(
        [
            first_half * cosine_table - second_half * sine_table,
            second_half * cosine_table + first_half * sine_table,
        ],
        axis=-1,
    )


def times_transposed(left, weight):
    return lax.dot_general(
        left, weight, (((1,), (1,)), ((), ())), preferred_element_type=jnp.float32
    )


def weight_term(left, right, spread_columns=None):

    def term_rows():
        product = lax.dot_general(
            left, right, (((0,), (0,)), ((), ())), preferred_element_type=jnp.float32
        )
        if spread_columns is None:
            return product
        return spread_columns(product)

    return lax.psum_scatter(
        term_rows().astype(jnp.bfloat16), "dp", scatter_dimension=0, tiled=True
    ).astype(jnp.float32)


def attend_forward(queries, key_heads, values, key_valid):
    length_q, local_heads, head_dim = queries.shape
    block_rows = min(512, length_q)
    scale = head_dim ** (-0.5)

    def one_block(query_block):
        scores = (
            jnp.einsum("qhd,khd->hqk", query_block, key_heads, preferred_element_type=jnp.float32)
            * scale
        )
        scores = jnp.where(key_valid[None, None, :], scores, MASKED)
        row_max = jnp.max(scores, axis=-1, keepdims=True)
        exponent = jnp.exp(scores - row_max)
        row_total = jnp.sum(exponent, axis=-1, keepdims=True)
        weights = (exponent / row_total).astype(jnp.bfloat16)
        output = jnp.einsum("hqk,khd->qhd", weights, values, preferred_element_type=jnp.float32)
        return (output.astype(jnp.bfloat16), (row_max + jnp.log(row_total))[..., 0])

    blocks = queries.reshape(length_q // block_rows, block_rows, local_heads, head_dim)
    outputs, logsum = lax.map(one_block, blocks)
    return (outputs.reshape(length_q, local_heads, head_dim), logsum)


def attend_backward(queries, key_heads, values, key_valid, logsum, out_grad):
    length_q, local_heads, head_dim = queries.shape
    block_rows = logsum.shape[2]
    scale = head_dim ** (-0.5)
    query_blocks = queries.reshape(length_q // block_rows, block_rows, local_heads, head_dim)
    grad_blocks = out_grad.reshape(length_q // block_rows, block_rows, local_heads, head_dim)

    def one_block(carried, inputs):
        key_grad, value_grad = carried
        query_block, grad_block, logsum_block = inputs
        scores = (
            jnp.einsum("qhd,khd->hqk", query_block, key_heads, preferred_element_type=jnp.float32)
            * scale
        )
        scores = jnp.where(key_valid[None, None, :], scores, MASKED)
        probabilities = jnp.exp(scores - logsum_block[..., None])
        value_grad = value_grad + jnp.einsum(
            "hqk,qhd->khd",
            probabilities.astype(jnp.bfloat16),
            grad_block,
            preferred_element_type=jnp.float32,
        )
        prob_grad = jnp.einsum(
            "qhd,khd->hqk", grad_block, values, preferred_element_type=jnp.float32
        )
        row_delta = jnp.sum(probabilities * prob_grad, axis=-1, keepdims=True)
        score_grad = (probabilities * (prob_grad - row_delta)).astype(jnp.bfloat16)
        query_grad = (
            jnp.einsum("hqk,khd->qhd", score_grad, key_heads, preferred_element_type=jnp.float32)
            * scale
        )
        key_grad = (
            key_grad
            + jnp.einsum(
                "hqk,qhd->khd", score_grad, query_block, preferred_element_type=jnp.float32
            )
            * scale
        )
        return ((key_grad, value_grad), query_grad)

    zeros_kv = jnp.zeros(key_heads.shape, jnp.float32)
    carried, query_grads = lax.scan(
        one_block, (zeros_kv, zeros_kv), (query_blocks, grad_blocks, logsum)
    )
    return (query_grads.reshape(length_q, local_heads, head_dim), carried[0], carried[1])


def self_attention(inputs, gain_row, w_qkv, w_out, cosine_table, sine_table, head_count):
    frame_rows = inputs.shape[0]
    frames = frame_rows * head_count
    local_heads = HEADS // head_count
    normed, norm_saved = normalize(inputs, gain_row)
    normed_low = normed.astype(jnp.bfloat16)
    projected = jnp.dot(normed_low, w_qkv, preferred_element_type=jnp.float32).reshape(
        frame_rows, 3, HEADS, HEAD_DIM
    )
    turned = jnp.concatenate(
        [rotate(projected[:, :2], cosine_table, sine_table), projected[:, 2:]], axis=1
    )
    turned_low = turned.astype(jnp.bfloat16).reshape(frame_rows, 3, D)
    head_major = lax.all_to_all(
        turned_low, "head", split_axis=2, concat_axis=0, tiled=True
    ).reshape(frames, 3, local_heads, HEAD_DIM)
    everywhere = jnp.ones((frames,), dtype=jnp.bool_)
    attended, logsum = attend_forward(
        head_major[:, 0], head_major[:, 1], head_major[:, 2], everywhere
    )
    frame_major = lax.all_to_all(
        attended.reshape(frames, local_heads * HEAD_DIM),
        "head",
        split_axis=0,
        concat_axis=1,
        tiled=True,
    )
    branch = jnp.dot(frame_major, w_out, preferred_element_type=jnp.float32)
    return (inputs + branch, (normed_low, norm_saved, head_major, logsum, frame_major))


def cross_attention(
    inputs, gain_row, w_q2, w_kv2, w_out2, context_low, key_valid, head_count, head_index
):
    frame_rows = inputs.shape[0]
    frames = frame_rows * head_count
    local_heads = HEADS // head_count
    local_width = local_heads * HEAD_DIM
    prompt_rows = context_low.shape[0]
    normed, norm_saved = normalize(inputs, gain_row)
    normed_low = normed.astype(jnp.bfloat16)
    query_low = jnp.dot(normed_low, w_q2, preferred_element_type=jnp.float32).astype(jnp.bfloat16)
    query_heads = lax.all_to_all(
        query_low, "head", split_axis=1, concat_axis=0, tiled=True
    ).reshape(frames, local_heads, HEAD_DIM)
    own_columns = lax.dynamic_index_in_dim(
        w_kv2.reshape(CTX, 2, head_count, local_width), head_index, 2, keepdims=False
    ).reshape(CTX, 2 * local_width)
    key_value = jnp.dot(context_low, own_columns, preferred_element_type=jnp.float32).astype(
        jnp.bfloat16
    )
    key_value = key_value.reshape(prompt_rows, 2, local_heads, HEAD_DIM)
    attended, logsum = attend_forward(query_heads, key_value[:, 0], key_value[:, 1], key_valid)
    frame_major = lax.all_to_all(
        attended.reshape(frames, local_width), "head", split_axis=0, concat_axis=1, tiled=True
    )
    branch = jnp.dot(frame_major, w_out2, preferred_element_type=jnp.float32)
    return (inputs + branch, (normed_low, norm_saved, query_heads, key_value, logsum, frame_major))


def feed_forward(inputs, gain_row, w_in, w_down):
    normed, norm_saved = normalize(inputs, gain_row)
    normed_low = normed.astype(jnp.bfloat16)
    gate_up = jnp.dot(normed_low, w_in, preferred_element_type=jnp.float32)
    gate_part = gate_up[:, :FF]
    up_part = gate_up[:, FF:]
    hidden = (jax.nn.silu(gate_part) * up_part).astype(jnp.bfloat16)
    branch = jnp.dot(hidden, w_down, preferred_element_type=jnp.float32)
    return (inputs + branch, (normed_low, norm_saved, gate_part, up_part, hidden))


def forward(
    inputs, gains, weights, context_low, key_valid, cosine_table, sine_table, head_count, head_index
):
    w_qkv, w_out, w_q2, w_kv2, w_out2, w_in, w_down = weights
    first, saved_self = self_attention(
        inputs, gains[0], w_qkv, w_out, cosine_table, sine_table, head_count
    )
    second, saved_cross = cross_attention(
        first, gains[1], w_q2, w_kv2, w_out2, context_low, key_valid, head_count, head_index
    )
    third, saved_feed = feed_forward(second, gains[2], w_in, w_down)
    return (third, (saved_self, saved_cross, saved_feed))


def backward(saved, cotangent_row, gains, weights, key_valid, cosine_table, sine_table, head_count):
    full_qkv, full_out, full_q2, full_kv2, full_out2, full_in, full_down = weights
    saved_self, saved_cross, saved_feed = saved
    frame_rows = cotangent_row.shape[0]
    frames = frame_rows * head_count
    local_heads = HEADS // head_count
    local_width = local_heads * HEAD_DIM
    normed3, norm3_saved, gate_part, up_part, hidden = saved_feed
    hidden_grad = times_transposed(cotangent_row, full_down)
    sigmoid_gate = jax.nn.sigmoid(gate_part)
    silu_gate = gate_part * sigmoid_gate
    gate_grad = hidden_grad * up_part * sigmoid_gate * (1.0 + gate_part * (1.0 - sigmoid_gate))
    up_grad = hidden_grad * silu_gate
    gate_up_grad = jnp.concatenate([gate_grad, up_grad], axis=1).astype(jnp.bfloat16)
    normed_back, gain_three = normalize_back(
        times_transposed(gate_up_grad, full_in), gains[2], norm3_saved
    )
    residual_grad = cotangent_row.astype(jnp.float32) + normed_back
    normed2, norm2_saved, query_heads, key_value, cross_logsum, cross_frames = saved_cross
    cross_low = residual_grad.astype(jnp.bfloat16)
    cross_out_grad = times_transposed(cross_low, full_out2).astype(jnp.bfloat16)
    cross_grad_heads = lax.all_to_all(
        cross_out_grad, "head", split_axis=1, concat_axis=0, tiled=True
    )
    cross_grad_heads = cross_grad_heads.reshape(frames, local_heads, HEAD_DIM)
    query_grad, key_grad, value_grad = attend_backward(
        query_heads, key_value[:, 0], key_value[:, 1], key_valid, cross_logsum, cross_grad_heads
    )
    query_frames = lax.all_to_all(
        query_grad.astype(jnp.bfloat16).reshape(frames, local_width),
        "head",
        split_axis=0,
        concat_axis=1,
        tiled=True,
    )
    prompt_rows = key_value.shape[0]
    kv_grad = (
        jnp.stack([key_grad, value_grad], axis=1)
        .astype(jnp.bfloat16)
        .reshape(prompt_rows, 2 * local_width)
    )
    normed_back, gain_two = normalize_back(
        times_transposed(query_frames, full_q2), gains[1], norm2_saved
    )
    residual_grad = residual_grad + normed_back
    normed1, norm1_saved, head_major, self_logsum, self_frames = saved_self
    self_low = residual_grad.astype(jnp.bfloat16)
    self_out_grad = times_transposed(self_low, full_out).astype(jnp.bfloat16)
    self_grad_heads = lax.all_to_all(self_out_grad, "head", split_axis=1, concat_axis=0, tiled=True)
    self_grad_heads = self_grad_heads.reshape(frames, local_heads, HEAD_DIM)
    everywhere = jnp.ones((frames,), dtype=jnp.bool_)
    query_grad, key_grad, value_grad = attend_backward(
        head_major[:, 0],
        head_major[:, 1],
        head_major[:, 2],
        everywhere,
        self_logsum,
        self_grad_heads,
    )
    stacked = jnp.stack([query_grad, key_grad, value_grad], axis=1).astype(jnp.bfloat16)
    returned = lax.all_to_all(
        stacked.reshape(frames, 3, local_width), "head", split_axis=0, concat_axis=2, tiled=True
    )
    returned = returned.reshape(frame_rows, 3, HEADS, HEAD_DIM).astype(jnp.float32)
    unturned = jnp.concatenate(
        [rotate(returned[:, :2], cosine_table, -sine_table), returned[:, 2:]], axis=1
    )
    qkv_low = unturned.astype(jnp.bfloat16).reshape(frame_rows, 3 * D)
    normed_back, gain_one = normalize_back(
        times_transposed(qkv_low, full_qkv), gains[0], norm1_saved
    )
    input_grad = residual_grad + normed_back
    pairs = (
        (normed1, qkv_low),
        (self_frames, self_low),
        (normed2, query_frames),
        (None, kv_grad),
        (cross_frames, cross_low),
        (normed3, gate_up_grad),
        (hidden, cotangent_row),
    )
    return (input_grad, jnp.stack([gain_one, gain_two, gain_three]), pairs)


def general_body(
    tokens, context, lengths, norm_gains, w_qkv, w_out, w_q2, w_kv2, w_out2, w_in, w_down, cotangent
):
    head_count = lax.axis_size("head")
    head_index = lax.axis_index("head")
    frame_rows = tokens.shape[1]
    local_heads = HEADS // head_count
    local_width = local_heads * HEAD_DIM
    prompt_rows = context.shape[1]
    cosine_table, sine_table = rotary_tables(head_index * frame_rows, frame_rows)
    weights = (
        lax.all_gather(w_qkv, "dp", axis=0, tiled=True),
        lax.all_gather(w_out, "dp", axis=0, tiled=True),
        lax.all_gather(w_q2, "dp", axis=0, tiled=True),
        lax.all_gather(w_kv2, "dp", axis=0, tiled=True),
        lax.all_gather(w_out2, "dp", axis=0, tiled=True),
        lax.all_gather(w_in, "dp", axis=0, tiled=True),
        lax.all_gather(w_down, "dp", axis=0, tiled=True),
    )

    def valid_keys(sequence):
        return jnp.arange(prompt_rows, dtype=jnp.int32) < lengths[sequence]

    collected = [[] for position in range(7)]
    sequence = 0
    output, saved = forward(
        tokens[sequence].astype(jnp.float32),
        norm_gains,
        weights,
        context[sequence],
        valid_keys(sequence),
        cosine_table,
        sine_table,
        head_count,
        head_index,
    )
    outputs = [output.astype(jnp.bfloat16)]
    input_grad, gain_terms, pairs = backward(
        saved,
        cotangent[sequence],
        norm_gains,
        weights,
        valid_keys(sequence),
        cosine_table,
        sine_table,
        head_count,
    )
    input_grads = [input_grad]
    for position in range(7):
        left_part, right_part = pairs[position]
        if left_part is None:
            left_part = context[sequence]
        collected[position].append((left_part, right_part))
    owner_mask = (jnp.arange(head_count, dtype=jnp.int32) == head_index).astype(jnp.float32)

    def spread_heads(product):
        row_count = product.shape[0]
        placed = product.reshape(row_count, 2, 1, local_width) * owner_mask[None, None, :, None]
        return placed.reshape(row_count, 2 * D)

    grad_list = []
    for position in range(7):
        lefts = jnp.concatenate([pair[0] for pair in collected[position]], axis=0)
        rights = jnp.concatenate([pair[1] for pair in collected[position]], axis=0)
        lefts, rights = (lefts, rights)
        if position == 3:
            grad_list.append(weight_term(lefts, rights, spread_heads))
        else:
            grad_list.append(weight_term(lefts, rights))
    summed = (
        lax.psum(grad_list[0].astype(jnp.bfloat16), "head").astype(jnp.float32),
        lax.psum(grad_list[1].astype(jnp.bfloat16), "head").astype(jnp.float32),
        lax.psum(grad_list[2].astype(jnp.bfloat16), "head").astype(jnp.float32),
        lax.psum(grad_list[3].astype(jnp.bfloat16), "head").astype(jnp.float32),
        lax.psum(grad_list[4].astype(jnp.bfloat16), "head").astype(jnp.float32),
        lax.psum(grad_list[5].astype(jnp.bfloat16), "head").astype(jnp.float32),
        lax.psum(grad_list[6].astype(jnp.bfloat16), "head").astype(jnp.float32),
    )
    gains_grad = lax.psum(gain_terms, ("dp", "head"))
    return (
        jnp.stack(outputs),
        jnp.stack(input_grads),
        gains_grad,
        summed[0],
        summed[1],
        summed[2],
        summed[3],
        summed[4],
        summed[5],
        summed[6],
    )


LOG2E = 1.4426950408889634
LN2 = 0.6931471805599453
ROPE_BASE = 10000.0
LANES = 128
VMEM_BYTES = 48 * 1024 * 1024
SHARE = 1


def declared(flops, bytes_accessed, transcendentals):
    return pl.CostEstimate(
        flops=flops // SHARE,
        bytes_accessed=bytes_accessed // SHARE,
        transcendentals=transcendentals // SHARE,
    )


def in_order(*values):
    return lax.optimization_barrier(values)


def flipped(index_bit, count):
    return [(one, one ^ index_bit) for one in range(count)]


def swap_dp(value, index_bit):
    return lax.ppermute(value, "dp", flipped(index_bit, lax.axis_size("dp")))


def swap_head(value):
    return lax.ppermute(value, "head", [(0, 1), (1, 0)])


def take(value, index, axis):
    return lax.dynamic_index_in_dim(value, index, axis, keepdims=False)


def add_low(kept, received):
    return (kept.astype(jnp.float32) + received.astype(jnp.float32)).astype(jnp.bfloat16)


class RowSum:
    def __init__(self, term, z_first=False):
        place, count = lax.axis_index("dp"), lax.axis_size("dp")
        at_y, z_low, z_high = (place // 2) % 2, (place // 4) % 2, place // 8
        self.kept = None
        if z_first:
            self.stages = [(2, z_low, 4), (1, z_high, 8), (0, at_y, 2)]
            self.part = term.reshape(2, 2, 2, term.shape[0] // 8, term.shape[1])
            self.send()
            return
        self.stages = [(1, z_low, 4), (0, z_high, 8)]
        self.shape = (2, 2, term.shape[0] // 8, term.shape[1])
        self.received = lax.psum_scatter(
            term,
            "dp",
            scatter_dimension=0,
            axis_index_groups=[[one, one + 2] for one in range(count) if one % 4 < 2],
            tiled=True,
        )

    def send(self):
        axis, own, bit = self.stages.pop(0)
        self.received = swap_dp(take(self.part, 1 - own, axis), bit)
        self.kept = take(self.part, own, axis)

    def step(self):
        if self.kept is None:
            self.part = self.received.reshape(self.shape)
        else:
            self.part = add_low(self.kept, self.received)
        self.received = None
        if self.stages:
            self.send()

    def finish(self):
        while self.received is not None:
            self.step()
        return self.part


def arrived(value, *sums):
    tied = lax.optimization_barrier((value, *[one.received for one in sums]))
    for one, received in zip(sums, tied[1:]):
        one.received = received
    return tied[0]


def after(value, *sums):
    sums = [one for one in sums if one.received is not None]
    tied = lax.optimization_barrier((value, *[one.received for one in sums]))
    for one, received in zip(sums, tied[1:]):
        one.received = received
        one.step()
    return tied[0]


def place_bits():
    return (lax.axis_index("dp") % 2).reshape(1).astype(jnp.int32)


def turn_kernel(bits_ref, values_ref, mine_ref, theirs_ref):
    turned = values_ref[...].T
    block = turned.shape[0] // 16
    core = bits_ref[0]
    for at in range(8):
        first = turned[2 * at * block : (2 * at + 1) * block]
        second = turned[(2 * at + 1) * block : (2 * at + 2) * block]
        to = slice((at % 2 * 4 + at // 2) * block, (at % 2 * 4 + at // 2 + 1) * block)
        mine_ref[to, :] = jnp.where(core == 0, first, second)
        theirs_ref[to, :] = jnp.where(core == 0, second, first)


def turn_rows(values):
    frames, rows = values.shape
    step = min(frames, 512)
    grid_spec = pltpu.PrefetchScalarGridSpec(
        num_scalar_prefetch=1,
        grid=(frames // step,),
        in_specs=[pl.BlockSpec((step, rows), lambda n, s: (n, 0))],
        out_specs=[pl.BlockSpec((rows // 2, step), lambda n, s: (0, n))] * 2,
    )
    return pl.pallas_call(
        turn_kernel,
        name="turn_rows",
        grid_spec=grid_spec,
        out_shape=[jax.ShapeDtypeStruct((rows // 2, frames), jnp.bfloat16)] * 2,
        compiler_params=pltpu.CompilerParams(vmem_limit_bytes=VMEM_BYTES),
        cost_estimate=declared(0, 4 * frames * rows, 0),
    )(place_bits(), values)


def product_kernel(terms, *refs):
    total = jnp.dot(refs[0][...], refs[terms][...], preferred_element_type=jnp.float32)
    for at in range(1, terms):
        total += jnp.dot(refs[at][...], refs[terms + at][...], preferred_element_type=jnp.float32)
    out_refs = refs[2 * terms :]
    step, span = pl.program_id(0), pl.num_programs(0) // len(out_refs)
    for at, out_ref in enumerate(out_refs):

        @pl.when(step // span == at)
        def _():
            out_ref[...] = total.astype(jnp.bfloat16)


def parts_kernel(left_ref, left2_ref, *refs):
    out_ref = refs[-1]
    for at in range(3):

        @pl.when(pl.program_id(0) == at)
        def _():
            total = jnp.dot(left_ref[...], refs[at][...], preferred_element_type=jnp.float32)
            total += jnp.dot(
                left2_ref[...], refs[3 + at][...], preferred_element_type=jnp.float32
            )
            out_ref[...] = total.astype(jnp.bfloat16)


def products_of_parts(lefts, parts, parts2, name):
    rows, frames = lefts[0].shape
    width = parts[0].shape[1]
    left_spec = pl.BlockSpec((rows, frames), lambda n: (0, 0))
    right_spec = pl.BlockSpec((frames, width), lambda n: (0, 0))
    return pl.pallas_call(
        parts_kernel,
        name=name,
        grid=(3,),
        in_specs=[left_spec] * 2 + [right_spec] * 6,
        out_specs=pl.BlockSpec((rows, width), lambda n: (0, n)),
        out_shape=jax.ShapeDtypeStruct((rows, 3 * width), jnp.bfloat16),
        compiler_params=pltpu.CompilerParams(vmem_limit_bytes=VMEM_BYTES),
        cost_estimate=declared(
            flops=12 * rows * frames * width,
            bytes_accessed=4 * rows * frames + 12 * frames * width + 6 * rows * width,
            transcendentals=0,
        ),
    )(*lefts, *parts, *parts2)


def parts_back_kernel(*refs):
    right_ref, out_ref, total = refs[3:]
    step = pl.program_id(0)
    for at in range(3):

        @pl.when(step == at)
        def _():
            back = nt_dot(refs[at][...], right_ref[...])
            total[...] = back if at == 0 else total[...] + back

    @pl.when(step == 2)
    def _():
        out_ref[...] = total[...].astype(out_ref.dtype)


def parts_turned(parts, right, at, rows, start, kind, name):
    depth, width = right.shape[0], parts[0].shape[1]
    return pl.pallas_call(
        parts_back_kernel,
        name=name,
        grid=(3,),
        in_specs=[pl.BlockSpec((rows, width), lambda n: (at, 0))] * 3
        + [pl.BlockSpec((depth, width), lambda n: (0, start // width + n))],
        out_specs=pl.BlockSpec((rows, depth), lambda n: (0, 0)),
        out_shape=jax.ShapeDtypeStruct((rows, depth), kind),
        scratch_shapes=[pltpu.VMEM((rows, depth), jnp.float32)],
        compiler_params=pltpu.CompilerParams(vmem_limit_bytes=VMEM_BYTES),
        cost_estimate=declared(
            flops=6 * rows * depth * width,
            bytes_accessed=6 * rows * width + 6 * depth * width + 4 * rows * depth,
            transcendentals=0,
        ),
    )(*parts, right)


def products(lefts, rights, tile, name, pieces=1):
    frames = lefts[0].shape[1]
    blocks = rights[0].shape[0] // frames
    terms = len(lefts)
    rows, width = lefts[0].shape[0], rights[0].shape[1]
    span = width // tile // pieces

    def piece_at(piece):
        return lambda n: (0, jnp.clip(n - piece * span, 0, span - 1))

    def rows_at(block):
        return lambda n: (block, n)

    left_spec = pl.BlockSpec((rows, frames), lambda n: (0, 0))
    right_specs = [pl.BlockSpec((frames, tile), rows_at(at % blocks)) for at in range(terms)]
    out = pl.pallas_call(
        functools.partial(product_kernel, terms),
        name=name,
        grid=(width // tile,),
        in_specs=[left_spec] * terms + right_specs,
        out_specs=[pl.BlockSpec((rows, tile), piece_at(piece)) for piece in range(pieces)],
        out_shape=[jax.ShapeDtypeStruct((rows, width // pieces), jnp.bfloat16)] * pieces,
        compiler_params=pltpu.CompilerParams(vmem_limit_bytes=VMEM_BYTES),
        cost_estimate=declared(
            flops=2 * terms * rows * frames * width,
            bytes_accessed=2 * terms * (rows + width) * frames + 2 * rows * width,
            transcendentals=0,
        ),
    )(*lefts, *[rights[at // blocks] for at in range(terms)])
    return out if pieces > 1 else out[0]


def product_rows(left, right):
    return lax.dot_general(
        left, right, (((0,), (0,)), ((), ())), preferred_element_type=jnp.float32
    )


def turn(values, cosine, sine):
    width, quarter = values.shape[1], HEAD_DIM // 2
    lane = lax.broadcasted_iota(jnp.int32, values.shape, 1) % HEAD_DIM
    moved = jnp.where(
        lane < quarter,
        pltpu.roll(values, width - quarter, 1),
        pltpu.roll(values, quarter, 1),
    )
    if width > LANES:
        cosine = jnp.concatenate([cosine] * (width // LANES), axis=1)
        sine = jnp.concatenate([sine] * (width // LANES), axis=1)
    return values * cosine + moved * sine


def lane_tables(positions):
    half_dim = HEAD_DIM // 2
    frequencies = ROPE_BASE ** (-2.0 * jnp.arange(half_dim, dtype=jnp.float32) / HEAD_DIM)
    angles = positions.astype(jnp.float32)[:, None] * frequencies[None, :]
    cosine, sine = jnp.cos(angles), jnp.sin(angles)
    return (
        jnp.concatenate([cosine] * 4, axis=1),
        jnp.concatenate([-sine, sine, -sine, sine], axis=1),
    )


def qkv_kernel(h_ref, w_ref, cosine_ref, sine_ref, out_ref):
    width = out_ref.shape[1]
    projected = jnp.dot(h_ref[...], w_ref[...], preferred_element_type=jnp.float32)
    step = pl.program_id(0)
    third = pl.num_programs(0) // 3

    @pl.when(step < 2 * third)
    def _():
        scale = jnp.where(step < third, HEAD_DIM ** (-0.5), 1.0)
        for at in range(0, width, LANES):
            turned = turn(projected[:, at : at + LANES], cosine_ref[...], sine_ref[...])
            out_ref[:, at : at + LANES] = (turned * scale).astype(jnp.bfloat16)

    @pl.when(step >= 2 * third)
    def _():
        out_ref[...] = projected.astype(jnp.bfloat16)


def project_qkv(normed, weight, start, width, cosine, sine):
    rows, depth = normed.shape
    tile = 384
    return pl.pallas_call(
        qkv_kernel,
        name="qkv_projection",
        grid=(width // tile,),
        in_specs=[
            pl.BlockSpec((rows, depth), lambda n: (0, 0)),
            pl.BlockSpec((depth, tile), lambda n: (0, start // tile + n)),
            pl.BlockSpec((rows, LANES), lambda n: (0, 0)),
            pl.BlockSpec((rows, LANES), lambda n: (0, 0)),
        ],
        out_specs=pl.BlockSpec((rows, tile), lambda n: (0, n)),
        out_shape=jax.ShapeDtypeStruct((rows, width), jnp.bfloat16),
        compiler_params=pltpu.CompilerParams(vmem_limit_bytes=VMEM_BYTES),
        cost_estimate=declared(
            flops=2 * rows * depth * width,
            bytes_accessed=2 * (rows * depth + depth * width + rows * width),
            transcendentals=0,
        ),
    )(normed, weight, cosine, sine)


def nt_dot(left, right):
    return lax.dot_general(
        left, right, (((1,), (1,)), ((), ())), preferred_element_type=jnp.float32
    )


def attend_kernel(masked, length_ref, q_ref, k_ref, v_ref, out_ref, lse_ref):
    for head in range(q_ref.shape[1] // HEAD_DIM):
        lanes = slice(head * HEAD_DIM, (head + 1) * HEAD_DIM)
        scores = nt_dot(q_ref[:, lanes], k_ref[:, lanes])
        if masked:
            key = lax.broadcasted_iota(jnp.int32, scores.shape, 1)
            scores = jnp.where(key < length_ref[0], scores, MASKED)
        row_max = jnp.max(scores, axis=1, keepdims=True)
        exponent = jnp.exp2(scores * LOG2E - row_max * LOG2E)
        total = jnp.sum(exponent, axis=1, keepdims=True)
        mixed = jnp.dot(
            exponent.astype(jnp.bfloat16), v_ref[:, lanes], preferred_element_type=jnp.float32
        )
        out_ref[:, lanes] = (mixed / total).astype(jnp.bfloat16)
        lse_ref[:, lanes] = jnp.broadcast_to(
            row_max * LOG2E + jnp.log2(total), (row_max.shape[0], HEAD_DIM)
        )


def attend(length, queries, keys, values, width, columns, masked, name, span, block):
    rows, key_rows = queries.shape[0], keys.shape[0]
    pairs = width // span
    q_at, k_at, v_at = columns
    grid_spec = pltpu.PrefetchScalarGridSpec(
        num_scalar_prefetch=1,
        grid=(pairs, rows // block),
        in_specs=[
            pl.BlockSpec((block, span), lambda p, i, s: (i, q_at + p)),
            pl.BlockSpec((key_rows, span), lambda p, i, s: (0, k_at + p)),
            pl.BlockSpec((key_rows, span), lambda p, i, s: (0, v_at + p)),
        ],
        out_specs=[
            pl.BlockSpec((block, span), lambda p, i, s: (i, p)),
            pl.BlockSpec((block, span), lambda p, i, s: (i, p)),
        ],
    )
    return pl.pallas_call(
        functools.partial(attend_kernel, masked),
        name=name,
        grid_spec=grid_spec,
        out_shape=[
            jax.ShapeDtypeStruct((rows, width), jnp.bfloat16),
            jax.ShapeDtypeStruct((rows, width), jnp.float32),
        ],
        compiler_params=pltpu.CompilerParams(vmem_limit_bytes=VMEM_BYTES),
        cost_estimate=declared(
            flops=16 * rows * key_rows * width,
            bytes_accessed=8 * rows * width,
            transcendentals=rows * key_rows * width // HEAD_DIM,
        ),
    )(length, queries, keys, values)


def attend_back_kernel(
    masked,
    turned,
    length_ref,
    q_ref,
    k_ref,
    v_ref,
    grad_ref,
    out_ref,
    lse_ref,
    *rest,
):
    if turned:
        cosq_ref, sinq_ref, cosk_ref, sink_ref = rest[:4]
        rest = rest[4:]
    dq_ref, dk_ref, dv_ref, dk_sum, dv_sum = rest[-5:]
    step, steps = pl.program_id(1), pl.num_programs(1)

    @pl.when(step == 0)
    def _():
        dk_sum[...] = jnp.zeros_like(dk_sum)
        dv_sum[...] = jnp.zeros_like(dv_sum)

    lse_rows = lse_ref[...].T
    delta_rows = (grad_ref[...].astype(jnp.float32) * out_ref[...].astype(jnp.float32)).T
    dq_parts = []
    for head in range(q_ref.shape[1] // HEAD_DIM):
        lanes = slice(head * HEAD_DIM, (head + 1) * HEAD_DIM)
        query, key, value = q_ref[:, lanes], k_ref[:, lanes], v_ref[:, lanes]
        grad = grad_ref[:, lanes]
        scores = nt_dot(key, query)
        if masked:
            index = lax.broadcasted_iota(jnp.int32, scores.shape, 0)
            scores = jnp.where(index < length_ref[0], scores, MASKED)
        lse = lse_rows[head * HEAD_DIM : head * HEAD_DIM + 1, :]
        delta = jnp.sum(delta_rows[lanes, :], axis=0, keepdims=True)
        weight = jnp.exp2(scores * LOG2E - lse)
        dv_sum[:, lanes] += jnp.dot(
            weight.astype(jnp.bfloat16), grad, preferred_element_type=jnp.float32
        )
        weight_grad = nt_dot(value, grad)
        score_grad = (weight * (weight_grad - delta)).astype(jnp.bfloat16)
        dk_sum[:, lanes] += jnp.dot(score_grad, query, preferred_element_type=jnp.float32)
        dq_parts.append(product_rows(score_grad, key) * HEAD_DIM ** (-0.5))
    dq = jnp.concatenate(dq_parts, axis=1).astype(jnp.bfloat16)
    if turned:
        dq = turn(dq.astype(jnp.float32), cosq_ref[...], -sinq_ref[...]).astype(jnp.bfloat16)
    dq_ref[...] = dq

    @pl.when(step == steps - 1)
    def _():
        dk = dk_sum[...].astype(jnp.bfloat16)
        if turned:
            dk = turn(dk.astype(jnp.float32), cosk_ref[...], -sink_ref[...]).astype(jnp.bfloat16)
        dk_ref[...] = dk
        dv_ref[...] = dv_sum[...].astype(jnp.bfloat16)


def attend_back(
    length,
    queries,
    keys,
    values,
    columns,
    part,
    part_count,
    earlier,
    grad,
    outputs,
    lse,
    tables,
    masked,
    name,
    span,
    block,
):
    rows, key_rows = queries.shape[0], keys.shape[0]
    width = grad.shape[1]
    pairs = width // span // part_count
    grad_at = part * pairs
    q_at, k_at, v_at = columns
    by_grad = pl.BlockSpec((block, span), lambda p, i, s: (i, grad_at + p))
    by_key = pl.BlockSpec((key_rows, span), lambda p, i, s: (0, grad_at + p))
    in_specs = [
        pl.BlockSpec((block, span), lambda p, i, s: (i, q_at + grad_at + p)),
        pl.BlockSpec((key_rows, span), lambda p, i, s: (0, k_at + grad_at + p)),
        pl.BlockSpec((key_rows, span), lambda p, i, s: (0, v_at + grad_at + p)),
        by_grad,
        by_grad,
        by_grad,
    ]
    operands = [queries, keys, values, grad, outputs, lse]
    if tables is not None:
        cosine, sine = tables
        in_specs += [pl.BlockSpec((block, LANES), lambda p, i, s: (i, 0))] * 2
        in_specs += [pl.BlockSpec((key_rows, LANES), lambda p, i, s: (0, 0))] * 2
        operands += [cosine, sine, cosine, sine]
    aliases = {}
    if earlier is not None:
        aliases = {len(operands) + 1 + at: at for at in range(3)}
        in_specs += [pl.BlockSpec(memory_space=pl.ANY)] * 3
        operands += list(earlier)
    grid_spec = pltpu.PrefetchScalarGridSpec(
        num_scalar_prefetch=1,
        grid=(pairs, rows // block),
        in_specs=in_specs,
        out_specs=[by_grad, by_key, by_key],
        scratch_shapes=[pltpu.VMEM((key_rows, span), jnp.float32)] * 2,
    )
    return pl.pallas_call(
        functools.partial(attend_back_kernel, masked, tables is not None),
        name=name,
        grid_spec=grid_spec,
        out_shape=[
            jax.ShapeDtypeStruct((rows, width), jnp.bfloat16),
            jax.ShapeDtypeStruct((key_rows, width), jnp.bfloat16),
            jax.ShapeDtypeStruct((key_rows, width), jnp.bfloat16),
        ],
        input_output_aliases=aliases,
        compiler_params=pltpu.CompilerParams(vmem_limit_bytes=VMEM_BYTES),
        cost_estimate=declared(
            flops=40 * rows * key_rows * width // part_count,
            bytes_accessed=20 * rows * width // part_count,
            transcendentals=rows * key_rows * width // HEAD_DIM // part_count,
        ),
    )(length, *operands)


def feed_kernel(bits_ref, h_ref, cot_ref, in_ref, down_ref, *rest):
    mine_ref, theirs_ref, dgu_ref, out_ref, down, total = rest[-6:]
    step, steps = pl.program_id(0), pl.num_programs(0)
    depth, tile = h_ref.shape[1], down.shape[0]
    piece = down_ref.shape[0] // 2
    for at in range(4):
        place, part = at // 2, at % 2
        down[at * piece : (at + 1) * piece, :] = down_ref[
            place * piece : (place + 1) * piece, part * depth : (part + 1) * depth
        ]
    @pl.when(step == 0)
    def _():
        total[...] = jnp.zeros_like(total)

    chunk = h_ref.shape[0] // 2
    for at in range(2):
        rows = slice(at * chunk, (at + 1) * chunk)
        gate_up = jnp.dot(h_ref[rows, :], in_ref[...], preferred_element_type=jnp.float32)
        grad = nt_dot(cot_ref[rows, :], down[...])
        gate, up = gate_up[:, :tile], gate_up[:, tile:]
        sigmoid = jax.nn.sigmoid(gate)
        silu = gate * sigmoid
        hidden = (silu * up).astype(jnp.bfloat16)
        turned = hidden.T
        first, second = turned[: tile // 2], turned[tile // 2 :]
        mine_ref[:, rows] = jnp.where(bits_ref[0] == 0, first, second)
        theirs_ref[:, rows] = jnp.where(bits_ref[0] == 0, second, first)
        dgu_ref[rows, tile:] = (grad * silu).astype(jnp.bfloat16)
        dgu_ref[rows, :tile] = (
            grad * up * sigmoid * (1.0 + gate * (1.0 - sigmoid))
        ).astype(jnp.bfloat16)
        total[rows, :] += jnp.dot(hidden, down[...], preferred_element_type=jnp.float32)

    @pl.when(step == steps - 1)
    def _():
        out_ref[...] = total[...].astype(out_ref.dtype)


def feed(normed, cotangent, weights, half, earlier):
    rows, depth = normed.shape
    units = FF // 2
    steps = depth // 192
    tile = units // steps
    operands = [normed, cotangent, weights, weights]
    in_specs = [
        pl.BlockSpec((rows, depth), lambda n, s: (0, 0)),
        pl.BlockSpec((rows, depth), lambda n, s: (0, 0)),
        pl.BlockSpec((depth, 2 * tile), lambda n, s: (0, n)),
        pl.BlockSpec((depth // steps, 2 * depth), lambda n, s: (n, 2)),
    ]
    aliases = {}
    if earlier is not None:
        in_specs += [pl.BlockSpec(memory_space=pl.ANY)] * 3
        aliases = {5: 0, 6: 1, 7: 2}
        operands += list(earlier)

    def turned_at(n, s):
        return (n % 2 * 4 + n // 2, half)

    grid_spec = pltpu.PrefetchScalarGridSpec(
        num_scalar_prefetch=1,
        grid=(steps,),
        in_specs=in_specs,
        out_specs=[
            pl.BlockSpec((tile // 2, rows), turned_at),
            pl.BlockSpec((tile // 2, rows), turned_at),
            pl.BlockSpec((rows, 2 * tile), lambda n, s: (half, n)),
            pl.BlockSpec((rows, depth), lambda n, s: (0, 0)),
        ],
        scratch_shapes=[
            pltpu.VMEM((tile, depth), jnp.bfloat16),
            pltpu.VMEM((rows, depth), jnp.float32),
        ],
    )
    return pl.pallas_call(
        feed_kernel,
        name="feed_forward",
        grid_spec=grid_spec,
        out_shape=[
            jax.ShapeDtypeStruct((units // 2, 2 * rows), jnp.bfloat16),
            jax.ShapeDtypeStruct((units // 2, 2 * rows), jnp.bfloat16),
            jax.ShapeDtypeStruct((2 * rows, 2 * units), jnp.bfloat16),
            jax.ShapeDtypeStruct((rows, depth), jnp.bfloat16 if half else jnp.float32),
        ],
        input_output_aliases=aliases,
        compiler_params=pltpu.CompilerParams(vmem_limit_bytes=VMEM_BYTES),
        cost_estimate=declared(
            flops=8 * rows * depth * units,
            bytes_accessed=6 * depth * units + 6 * rows * units + 8 * rows * depth,
            transcendentals=rows * units,
        ),
    )(place_bits(), *operands)


def back_kernel(left_ref, right_ref, out_ref, total):
    step, steps = pl.program_id(0), pl.num_programs(0)

    @pl.when(step == 0)
    def _():
        total[...] = jnp.zeros_like(total)

    total[...] += nt_dot(left_ref[...], right_ref[...])

    @pl.when(step == steps - 1)
    def _():
        out_ref[...] = total[...].astype(out_ref.dtype)


def times_turned(left, right, at, rows, start, width, kind, name):
    depth = right.shape[0]
    tile = 1536 if width % 1536 == 0 else 768
    return pl.pallas_call(
        back_kernel,
        name=name,
        grid=(width // tile,),
        in_specs=[
            pl.BlockSpec((rows, tile), lambda n: (at, n)),
            pl.BlockSpec((depth, tile), lambda n: (0, start // tile + n)),
        ],
        out_specs=pl.BlockSpec((rows, depth), lambda n: (0, 0)),
        out_shape=jax.ShapeDtypeStruct((rows, depth), kind),
        scratch_shapes=[pltpu.VMEM((rows, depth), jnp.float32)],
        compiler_params=pltpu.CompilerParams(vmem_limit_bytes=VMEM_BYTES),
        cost_estimate=declared(
            flops=2 * rows * depth * width,
            bytes_accessed=2 * rows * width + 2 * depth * width + 4 * rows * depth,
            transcendentals=0,
        ),
    )(left, right)


def norm_back_into(total, x_ref, gain_ref, residual_ref, sum_ref, low_ref, term_ref):
    chunk = 128
    term = jnp.zeros(term_ref.shape, jnp.float32)
    for at in range(0, total.shape[0], chunk):
        rows = slice(at, at + chunk)
        grad = total[rows, :]
        values = x_ref[rows, :]
        centred = values - jnp.mean(values, axis=1, keepdims=True)
        inverse = lax.rsqrt(jnp.mean(centred * centred, axis=1, keepdims=True) + EPSILON)
        scaled = centred * inverse
        term += jnp.sum(grad * scaled, axis=0, keepdims=True)
        inner = grad * gain_ref[...]
        back = inverse * (
            inner
            - jnp.mean(inner, axis=1, keepdims=True)
            - scaled * jnp.mean(inner * scaled, axis=1, keepdims=True)
        )
        summed = residual_ref[rows, :].astype(jnp.float32) + back
        sum_ref[rows, :] = summed
        low_ref[rows, :] = summed.astype(jnp.bfloat16)
    term_ref[...] = term


def feed_back_kernel(
    left_ref, right_ref, other_ref, x_ref, gain_ref, residual_ref, sum_ref, low_ref, term_ref, total
):
    step, steps = pl.program_id(0), pl.num_programs(0)

    @pl.when(step == 0)
    def _():
        total[...] = other_ref[...].astype(jnp.float32)

    total[...] += nt_dot(left_ref[...], right_ref[...])

    @pl.when(step == steps - 1)
    def _():
        norm_back_into(total, x_ref, gain_ref, residual_ref, sum_ref, low_ref, term_ref)


def feed_back(left, right, other, values, gain, residual):
    rows, depth = values.shape
    tile = 1536
    whole = pl.BlockSpec((rows, depth), lambda n: (0, 0))
    line = pl.BlockSpec((1, depth), lambda n: (0, 0))
    return pl.pallas_call(
        feed_back_kernel,
        name="h3_back_norm",
        grid=(FF // tile,),
        in_specs=[
            pl.BlockSpec((rows, tile), lambda n: (0, n)),
            pl.BlockSpec((depth, tile), lambda n: (0, n)),
            whole,
            whole,
            line,
            whole,
        ],
        out_specs=[whole, whole, line],
        out_shape=[
            jax.ShapeDtypeStruct((rows, depth), jnp.float32),
            jax.ShapeDtypeStruct((rows, depth), jnp.bfloat16),
            jax.ShapeDtypeStruct((1, depth), jnp.float32),
        ],
        scratch_shapes=[pltpu.VMEM((rows, depth), jnp.float32)],
        compiler_params=pltpu.CompilerParams(vmem_limit_bytes=VMEM_BYTES),
        cost_estimate=declared(2 * rows * depth * FF, 2 * depth * FF, 0),
    )(left, right, other, values, gain, residual)


def cross_back_kernel(
    length_ref,
    low_ref,
    out_weight_ref,
    q_weight_ref,
    q_ref,
    k_ref,
    v_ref,
    out_ref,
    lse_ref,
    x_ref,
    gain_ref,
    residual_ref,
    dq_ref,
    dk_ref,
    dv_ref,
    sum_ref,
    new_low_ref,
    term_ref,
    total,
):
    step, steps = pl.program_id(0), pl.num_programs(0)
    grad_all = nt_dot(low_ref[...], out_weight_ref[...])
    lse_rows = lse_ref[...].T
    delta_rows = (grad_all * out_ref[...].astype(jnp.float32)).T
    grad_all = grad_all.astype(jnp.bfloat16)
    for head in range(q_ref.shape[1] // HEAD_DIM):
        lanes = slice(head * HEAD_DIM, (head + 1) * HEAD_DIM)
        query, key, value = q_ref[:, lanes], k_ref[:, lanes], v_ref[:, lanes]
        grad = grad_all[:, lanes]
        scores = nt_dot(key, query)
        index = lax.broadcasted_iota(jnp.int32, scores.shape, 0)
        scores = jnp.where(index < length_ref[0], scores, MASKED)
        lse = lse_rows[head * HEAD_DIM : head * HEAD_DIM + 1, :]
        delta = jnp.sum(delta_rows[lanes, :], axis=0, keepdims=True)
        weight = jnp.exp2(scores * LOG2E - lse)
        dv = jnp.dot(weight.astype(jnp.bfloat16), grad, preferred_element_type=jnp.float32)
        dv_ref[:, lanes] = dv.astype(jnp.bfloat16)
        score_grad = (weight * (nt_dot(value, grad) - delta)).astype(jnp.bfloat16)
        dk = jnp.dot(score_grad, query, preferred_element_type=jnp.float32)
        dk_ref[:, lanes] = dk.astype(jnp.bfloat16)
        dq = product_rows(score_grad, key) * HEAD_DIM ** (-0.5)
        dq_ref[:, lanes] = dq.astype(jnp.bfloat16)
    back = nt_dot(dq_ref[...], q_weight_ref[...])

    @pl.when(step == 0)
    def _():
        total[...] = back

    @pl.when(step > 0)
    def _():
        total[...] += back

    @pl.when(step == steps - 1)
    def _():
        norm_back_into(total, x_ref, gain_ref, residual_ref, sum_ref, new_low_ref, term_ref)


def cross_back(length, low, out_weight, q_weight, query, key, value, outputs, lse, values, gain, residual):
    rows, depth = values.shape
    key_rows = key.shape[0]
    tile = 384
    steps = depth // tile
    whole = pl.BlockSpec((rows, depth), lambda n, s: (0, 0))
    line = pl.BlockSpec((1, depth), lambda n, s: (0, 0))
    by_query = pl.BlockSpec((rows, tile), lambda n, s: (0, n))
    by_key = pl.BlockSpec((key_rows, tile), lambda n, s: (0, n))
    grid_spec = pltpu.PrefetchScalarGridSpec(
        num_scalar_prefetch=1,
        grid=(steps,),
        in_specs=[
            whole,
            pl.BlockSpec((tile, depth), lambda n, s: (n, 0)),
            pl.BlockSpec((depth, tile), lambda n, s: (0, n)),
            by_query,
            by_key,
            by_key,
            by_query,
            by_query,
            whole,
            line,
            whole,
        ],
        out_specs=[by_query, by_key, by_key, whole, whole, line],
        scratch_shapes=[pltpu.VMEM((rows, depth), jnp.float32)],
    )
    return pl.pallas_call(
        cross_back_kernel,
        name="cross_back",
        grid_spec=grid_spec,
        out_shape=[
            jax.ShapeDtypeStruct((rows, depth), jnp.bfloat16),
            jax.ShapeDtypeStruct((key_rows, depth), jnp.bfloat16),
            jax.ShapeDtypeStruct((key_rows, depth), jnp.bfloat16),
            jax.ShapeDtypeStruct((rows, depth), jnp.float32),
            jax.ShapeDtypeStruct((rows, depth), jnp.bfloat16),
            jax.ShapeDtypeStruct((1, depth), jnp.float32),
        ],
        compiler_params=pltpu.CompilerParams(vmem_limit_bytes=VMEM_BYTES),
        cost_estimate=declared(4 * rows * depth * depth, 8 * depth * depth, 0),
    )(length, low, out_weight, q_weight, query, key, value, outputs, lse, values, gain, residual)


def split_back_kernel(side_ref, left_ref, right_ref, kept_ref, sent_ref):
    half = kept_ref.shape[1]
    lower = nt_dot(left_ref[...], right_ref[:half, :]).astype(jnp.bfloat16)
    upper = nt_dot(left_ref[...], right_ref[half:, :]).astype(jnp.bfloat16)
    kept_ref[...] = jnp.where(side_ref[0] == 0, lower, upper)
    sent_ref[...] = jnp.where(side_ref[0] == 0, upper, lower)


def split_back(side, left, weights):
    rows, depth = left.shape
    return pl.pallas_call(
        split_back_kernel,
        name="attention_grad",
        grid=(1,),
        in_specs=[
            pl.BlockSpec(memory_space=pltpu.SMEM),
            pl.BlockSpec((rows, depth), lambda n: (0, 0)),
            pl.BlockSpec((depth, depth), lambda n: (0, 0)),
        ],
        out_specs=[pl.BlockSpec((rows, depth // 2), lambda n: (0, 0))] * 2,
        out_shape=[jax.ShapeDtypeStruct((rows, depth // 2), jnp.bfloat16)] * 2,
        compiler_params=pltpu.CompilerParams(vmem_limit_bytes=VMEM_BYTES),
        cost_estimate=declared(2 * rows * depth * depth, 2 * depth * depth, 0),
    )(side.reshape(1).astype(jnp.int32), left, weights)


def in_grad_kernel(side_ref, *refs):
    out_ref = refs[-1]
    unit = refs[0].shape[1] // 8
    for part in range(2):
        mine_ref, theirs_ref = refs[2 * part], refs[2 * part + 1]
        for at in range(8):
            mine = mine_ref[:, at * unit : (at + 1) * unit].astype(jnp.float32)
            theirs = theirs_ref[:, at * unit : (at + 1) * unit].astype(jnp.float32)
            tile, gate_or_up = part * 4 + at // 2, at % 2
            to = (gate_or_up * 8 + tile) * 2 * unit
            out_ref[:, to : to + unit] = jnp.where(side_ref[0] == 0, mine, theirs)
            out_ref[:, to + unit : to + 2 * unit] = jnp.where(side_ref[0] == 0, theirs, mine)


def assemble_in_grad(side, parts):
    rows, width = parts[0].shape
    whole = pl.BlockSpec(memory_space=pltpu.VMEM)
    return pl.pallas_call(
        in_grad_kernel,
        name="in_grad_rows",
        in_specs=[pl.BlockSpec(memory_space=pltpu.SMEM)] + [whole] * 4,
        out_specs=whole,
        out_shape=jax.ShapeDtypeStruct((rows, 4 * width), jnp.float32),
        compiler_params=pltpu.CompilerParams(vmem_limit_bytes=VMEM_BYTES),
        cost_estimate=declared(0, 16 * rows * width, 0),
    )(side.reshape(1).astype(jnp.int32), *parts)


def pack_kernel(side_ref, out_w_ref, qkv_ref, q2_ref, out2_ref, kv2_ref, packed_ref):
    left = side_ref[0] == 0
    half = q2_ref.shape[1] // 2
    rows = kv2_ref.shape[0]
    whole = out_w_ref.shape[1]
    packed_ref[:, :whole] = out_w_ref[...]

    def chosen(ref, at):
        return jnp.where(left, ref[:, at : at + half], ref[:, at + half : at + 2 * half])

    for one in range(3):
        at = whole + one * half
        packed_ref[:, at : at + half] = chosen(qkv_ref, 2 * one * half)
    for one, ref in enumerate((q2_ref, out2_ref)):
        at = whole + (3 + one) * half
        packed_ref[:, at : at + half] = chosen(ref, 0)
    at = whole + 5 * half
    packed_ref[:rows, at : at + half] = chosen(kv2_ref, 0)
    packed_ref[rows:, at : at + half] = chosen(kv2_ref, 2 * half)


def pack_first(side, w_out, w_qkv, w_q2, w_out2, w_kv2):
    rows, depth = w_out.shape
    whole = pl.BlockSpec(memory_space=pltpu.VMEM)
    return pl.pallas_call(
        pack_kernel,
        name="pack_first",
        in_specs=[pl.BlockSpec(memory_space=pltpu.SMEM)] + [whole] * 5,
        out_specs=whole,
        out_shape=jax.ShapeDtypeStruct((rows, 4 * depth), jnp.bfloat16),
        compiler_params=pltpu.CompilerParams(vmem_limit_bytes=VMEM_BYTES),
        cost_estimate=declared(0, 24 * rows * depth, 0),
    )(side.reshape(1).astype(jnp.int32), w_out, w_qkv, w_q2, w_out2, w_kv2)


def paired_body(
    tokens, context, lengths, norm_gains, w_qkv, w_out, w_q2, w_kv2, w_out2, w_in, w_down, cotangent
):
    place, side = lax.axis_index("dp"), lax.axis_index("head")
    core = place % 2
    on_left = side == 0
    own = tokens[0]
    frames = own.shape[0]
    rows = w_qkv.shape[0]
    half = D // 2
    units = w_down.shape[0]

    def ordered(mine, theirs):
        return jnp.where(on_left, mine, theirs), jnp.where(on_left, theirs, mine)

    full_first = lax.all_gather(
        pack_first(side, w_out, w_qkv, w_q2, w_out2, w_kv2), "dp", axis=0, tiled=True
    )
    full_out = full_first[:, :D]
    own_halves = full_first[:, D + 3 * half : D + 5 * half]
    core_rows = swap_head(take(own_halves.reshape(2, half, D), core, 0))
    kv2_half = full_first[:, D + 5 * half :].reshape(rows // 6, 2, rows // 2, half)
    kv2_weights = [kv2_half[:, one].reshape(D // 2, half) for one in range(2)]
    in_half = take(w_in.reshape(rows, 2, 8, 2, units), side, 3)
    in_half = jnp.swapaxes(in_half, 1, 2).reshape(rows, FF)
    down_parts = w_down.reshape(2, units // 2, D)
    down_received = swap_dp(take(down_parts, 1 - core, 0), 1)
    down_half = jnp.where(core == side, take(down_parts, core, 0), down_received)
    full_feed = lax.all_gather(
        jnp.concatenate([in_half, down_half[:rows], down_half[rows:]], axis=1),
        "dp",
        axis=0,
        tiled=True,
    )
    full_in = full_feed[:, :FF]

    both_tokens = jnp.concatenate([own, swap_head(own)], axis=0).astype(jnp.float32)
    own_cot, other_cot = cotangent[0], swap_head(cotangent[0])
    both_cot = jnp.concatenate([own_cot, other_cot], axis=0)
    frame = jnp.arange(frames, dtype=jnp.int32)
    tables = lane_tables(
        jnp.concatenate([side * frames + frame, (1 - side) * frames + frame])
    )
    normed1 = normalize(both_tokens, norm_gains[0])[0].astype(jnp.bfloat16)
    inputs = own.astype(jnp.float32)
    norm1_saved = normalize(inputs, norm_gains[0])[1]
    qkv = project_qkv(normed1, full_first, D, 3 * half, *tables)
    no_length = jnp.zeros((1,), jnp.int32)
    pairs = half // (2 * LANES)
    self_columns = (0, pairs, 2 * pairs)
    attended, self_lse = attend(
        no_length, qkv, qkv, qkv, half, self_columns, False, "self_attention", 2 * LANES, 512
    )
    key_value = jnp.stack(
        [
            jnp.dot(context[0], weight, preferred_element_type=jnp.float32).astype(jnp.bfloat16)
            for weight in kv2_weights
        ]
    )
    attended, core_rows, key_value_other = in_order(attended, core_rows, swap_head(key_value))
    attended_other = swap_head(attended[frames:])
    sibling_rows = swap_dp(core_rows, 1)
    other_halves = jnp.where(
        core == 0,
        jnp.concatenate([core_rows, sibling_rows], axis=0),
        jnp.concatenate([sibling_rows, core_rows], axis=0),
    )
    full_q2, full_out2 = in_order(
        *[
            jnp.concatenate(
                ordered(own_halves[:, at : at + half], other_halves[:, at : at + half]), axis=1
            )
            for at in (0, half)
        ]
    )
    attended_frames = jnp.concatenate(ordered(attended[:frames], attended_other), axis=1)
    first = inputs + jnp.dot(attended_frames, full_out, preferred_element_type=jnp.float32)

    normed2, norm2_saved = normalize(first, norm_gains[1])
    normed2 = normed2.astype(jnp.bfloat16)
    query2 = jnp.dot(normed2, full_q2, preferred_element_type=jnp.float32)
    query2 = (query2.astype(jnp.bfloat16) * HEAD_DIM ** (-0.5)).astype(jnp.bfloat16)
    key2, value2 = jnp.concatenate(ordered(key_value, key_value_other), axis=2)
    crossed, cross_lse = attend(
        lengths, query2, key2, value2, D, (0, 0, 0), True, "cross_attention", 3 * LANES, frames
    )
    second = first + jnp.dot(crossed, full_out2, preferred_element_type=jnp.float32)

    def left_pair(values):
        mine, theirs = turn_rows(values)
        return mine, swap_dp(theirs, 1)

    lefts1 = left_pair(normed1)
    lefts_out = left_pair(attended_frames)
    lefts2 = left_pair(normed2)
    lefts_cross = left_pair(crossed)
    lefts_context = left_pair(context[0])
    cots = both_cot, swap_dp(both_cot, 1)

    normed3, norm3_saved = normalize(second, norm_gains[2])
    normed3 = normed3.astype(jnp.bfloat16)
    other3 = swap_head(normed3)
    lefts3 = left_pair(normed3)
    *fed, own_out = feed(normed3, own_cot, full_feed, 0, None)
    fed, lefts1, lefts_out, lefts2, lefts3, lefts_cross, lefts_context, cots = in_order(
        fed, lefts1, lefts_out, lefts2, lefts3, lefts_cross, lefts_context, cots
    )
    hidden, hidden_theirs, dgu, other_out = feed(other3, other_cot, full_feed, 1, fed)
    lefts3_late = left_pair(other3)
    lefts3 = lefts3[0], lefts3_late[0], lefts3[1], lefts3_late[1]
    hidden, dgu = in_order(hidden, dgu)
    hiddens = hidden, swap_dp(hidden_theirs, 1)
    dgus = dgu, swap_dp(dgu, 1)
    sent3 = times_turned(dgu, full_feed, 1, frames, 0, FF, jnp.bfloat16, "h3_back")
    hiddens, sent3, lefts3 = in_order(hiddens, sent3, lefts3)
    received3 = swap_head(sent3)
    down_term = products(hiddens, cots, 256, "down_grad")
    dgus, down_term = in_order(dgus, down_term)
    down_sum = RowSum(down_term)
    in_terms = products(lefts3, dgus, 512, "in_grad", 2)
    in_terms, dgu = in_order(in_terms, dgu)
    residual3, cross_low, gain_three = feed_back(
        dgu, full_feed, received3, second, norm_gains[2:], own_cot
    )
    cross_low, in_terms = in_order(cross_low, in_terms)
    in_sums = [RowSum(one) for one in in_terms]
    cross_low = after(cross_low, down_sum)
    received_out = swap_head(other_out)

    query2_grad, key2_grad, value2_grad, residual2, self_low, gain_two = cross_back(
        lengths,
        cross_low,
        full_out2,
        full_q2,
        query2,
        key2,
        value2,
        crossed,
        cross_lse,
        first,
        norm_gains[1:2],
        residual3,
    )
    grad_kept, grad_sent = split_back(side, self_low, full_first)
    grad_kept, received_out = in_order(grad_kept, received_out)
    grad_kept = after(grad_kept, down_sum)
    grad_received = swap_head(grad_sent)
    kv2_grad = jnp.concatenate([key2_grad, value2_grad], axis=1)

    def square(lefts, right, name):
        return products(lefts, (right, swap_dp(right, 1)), 512, name)

    def meet(lower, upper):
        sent, middle = jnp.where(on_left, upper, lower), lower.shape[0] // 2
        return (
            jnp.where(on_left, lower, upper),
            swap_head(sent[:middle]),
            swap_head(sent[middle:]),
        )

    def met(terms, z_first):
        return RowSum(add_low(terms[0], jnp.concatenate(terms[1:], axis=0)), z_first)

    query2_grad, cross_low, kv2_grad, grad_kept = in_order(
        query2_grad, cross_low, kv2_grad, grad_kept
    )
    out2_terms = square(lefts_cross, cross_low, "out2_grad")
    q2_terms = square(lefts2, query2_grad, "q2_grad")
    out2_terms, q2_terms, self_low, kv2_grad = in_order(out2_terms, q2_terms, self_low, kv2_grad)
    cross_terms = meet(out2_terms, q2_terms)
    kv2_terms = square(lefts_context, kv2_grad, "kv2_grad").reshape(8 * rows, D)
    out_terms = square(lefts_out, self_low, "out_grad")
    kv2_terms, out_terms, grad_kept = in_order(kv2_terms, out_terms, grad_kept)
    self_terms = meet(out_terms, kv2_terms)
    heads_grad = jnp.concatenate([grad_kept, grad_received], axis=0)
    heads_grad = after(heads_grad, down_sum, in_sums[0])

    def heads_back(part, earlier):
        return attend_back(
            no_length,
            qkv,
            qkv,
            qkv,
            [2 * one for one in self_columns],
            part,
            2,
            earlier,
            heads_grad,
            attended,
            self_lse,
            tables,
            False,
            "self_attention_back",
            LANES,
            512,
        )

    early = heads_back(0, None)
    early = after(early, *in_sums)
    early, cross_terms = in_order(early, cross_terms)
    cross_part = add_low(cross_terms[0], jnp.concatenate(cross_terms[1:], axis=0))
    early, cross_part = in_order(early, cross_part)
    cross_sum = RowSum(cross_part)
    qkv_grads = heads_back(1, early)
    siblings = [swap_dp(one, 1) for one in qkv_grads]
    sent1 = parts_turned(qkv_grads, full_first, 1, frames, D, jnp.bfloat16, "h1_back")
    sent1, siblings, self_early = in_order(sent1, siblings, self_terms[1])
    received1 = swap_head(sent1)
    qkv_term = products_of_parts(lefts1, qkv_grads, siblings, "qkv_grad")
    qkv_sum = RowSum(qkv_term)
    qkv_grads, qkv_term, self_late = in_order(qkv_grads, qkv_term, self_terms[2])
    self_sum = met((self_terms[0], self_early, self_late), True)
    qkv_grads = after(qkv_grads, *in_sums, cross_sum)
    qkv_grads, received1 = in_order(qkv_grads, received1)
    own1 = parts_turned(qkv_grads, full_first, 0, frames, D, jnp.float32, "h1_back")
    own1, received_out = in_order(own1, received_out)
    output = (second + own_out + received_out.astype(jnp.float32)).astype(jnp.bfloat16)
    normed_grad = own1 + received1.astype(jnp.float32)
    normed_back, gain_one = normalize_back(normed_grad, norm_gains[0], norm1_saved)
    input_grad = residual2 + normed_back

    gains = jnp.concatenate([gain_one[None], gain_two, gain_three], axis=0)
    gains = after(gains, qkv_sum, self_sum)
    gains = gains + swap_dp(gains, 1)
    gains = gains + swap_dp(gains, 2)
    gains_received = after(swap_dp(gains, 4), in_sums[1], cross_sum)
    gains = gains + gains_received
    gains_received = after(swap_dp(gains, 8), qkv_sum, self_sum)
    gains = gains + gains_received
    gains_received = after(swap_head(gains), cross_sum, qkv_sum, self_sum)
    gains = gains + gains_received

    def joined(mine):
        lower, upper = ordered(mine, swap_head(mine))
        return jnp.stack([lower, upper], axis=-2)

    down_rows, own1 = in_order(down_sum.finish(), own1)
    down_other = swap_dp(down_rows, 1)
    down_block = jnp.concatenate(
        [
            jnp.where(core == 0, down_rows, down_other),
            jnp.where(core == 0, down_other, down_rows),
        ],
        axis=0,
    )
    crossing = [
        (2 * one + (one % 2), 2 * one + 1 - (one % 2)) for one in range(lax.axis_size("dp"))
    ]
    down_crossed = lax.ppermute(down_block, ("dp", "head"), crossing)
    down_out = jnp.where(core == side, down_block, down_crossed).astype(jnp.float32)
    in_parts = []
    for one in in_sums:
        mine = one.finish()
        in_parts += [mine, swap_head(mine)]
    in_out = assemble_in_grad(side, in_parts)
    qkv_out = joined(qkv_sum.finish().reshape(rows, 3, half)).reshape(rows, 3 * D)
    cross_rows = joined(cross_sum.finish()).astype(jnp.float32)
    self_rows = joined(self_sum.finish()).astype(jnp.float32)
    kv2_out = self_rows[:, 1].reshape(rows // 2, 2 * D)
    return (
        output[None],
        input_grad[None],
        gains,
        qkv_out.astype(jnp.float32),
        self_rows[:, 0],
        cross_rows[:, 1],
        kv2_out,
        cross_rows[:, 0],
        in_out,
        down_out,
    )


def body(*arrays):
    if lax.axis_size("dp") == 16 and lax.axis_size("head") == 2 and arrays[0].shape[0] == 1:
        return paired_body(*arrays)
    return general_body(*arrays)


def solution(mesh):
    placed = (
        P("dp", "head", None),
        P("dp", None, None),
        P("dp"),
        P(),
        P("dp", None),
        P("dp", None),
        P("dp", None),
        P("dp", None),
        P("dp", None),
        P("dp", None),
        P("dp", None),
        P("dp", "head", None),
    )
    return jax.shard_map(
        body,
        mesh=mesh,
        in_specs=placed,
        out_specs=(
            P("dp", "head", None),
            P("dp", "head", None),
            P(),
            P("dp", None),
            P("dp", None),
            P("dp", None),
            P("dp", None),
            P("dp", None),
            P("dp", None),
            P("dp", None),
        ),
        check_vma=False,
    )
```
